32 devices in a mesh: chan: 8 (over z, y), facet: 4 (over x, core).
Axes of the slice: x: 2, y: 2, z: 4, core: 2. Of those that a mesh axis runs over, the one named last changes fastest.
Arguments:
- solution: float32 [8, 2048, 2048], P('chan', 'facet'), may hold values from -6 to 6
- residual: float32 [8, 2048, 2048], P('chan', 'facet'), may hold values from -120 to 120
- direction: float32 [8, 2048, 2048], P('chan', 'facet'), may hold values from -120 to 120
- spectra: float32 [8, 4096, 4096], P('chan', None, 'facet'), may hold values from 0.05 to 1
- basis: float32 [8, 8], replicated, may hold values from -2 to 2
- slot_channel: int32 [8], replicated, may hold values from 0 to 7, each once
Outputs:
- new_solution: float32 [8, 2048, 2048], P('chan', 'facet')
- new_residual: float32 [8, 2048, 2048], P('chan', 'facet')
- new_direction: float32 [8, 2048, 2048], P('chan', 'facet')
The draws below stay inside these ranges and needn't reach their ends.
Inputs may be any that keep to these rules, and one draw needn't show every extreme that they name: `slot_channel`: every channel appears in exactly one slot.
All inputs are finite; a program needn't handle non-finite values.
Results may differ from the reference program's by a relative error of at most 0.000064.
Values sent between devices are 32-bit elements; how exact they have to be, the bound alone decides.
A program may use at most 256 MiB of HBM per device.

```python
import math
import jax
import jax.numpy as jnp
from jax import lax

L = 4096
RANK = 8
N = 2048
CHANNELS = 8


def scaled_cube(key):
    noise_key, row_key, col_key = jax.random.split(key, 3)
    cube_shape = (CHANNELS, N, N)
    noise_values = jax.random.truncated_normal(noise_key, -4.0, 4.0, cube_shape, jnp.float32)
    row_place = jnp.arange(N, dtype=jnp.float32) / (N - 1)
    row_scale = jnp.exp(math.log(3.0) * row_place + math.log(10.0 / 3.0) * jax.random.uniform(row_key, (N,), jnp.float32))
    col_scale = jnp.exp(math.log(10.0) * jax.random.uniform(col_key, (N,), jnp.float32))
    chan_place = jnp.arange(CHANNELS, dtype=jnp.float32) / (CHANNELS - 1)
    chan_scale = jnp.exp(math.log(3.0) * chan_place)
    return noise_values * chan_scale[:, None, None] * row_scale[None, :, None] * col_scale[None, None, :] * 0.1


def draw_residual(key, part):
    return scaled_cube(jax.random.fold_in(key, 11))


def draw_direction(key, part):
    return scaled_cube(jax.random.fold_in(key, 23))


def steps_of(own_key, shape, cuts, smallest, high):
    factor_of = 1.0
    for position, shards_of in cuts:
        heights = jax.random.uniform(jax.random.fold_in(jax.random.fold_in(own_key, 6), position), (shards_of,), jnp.float32, smallest / len(cuts), high / len(cuts))
        factor_of = factor_of * jnp.repeat(jnp.exp(heights), shape[position] // shards_of).reshape((-1,) + (1,) * (len(shape) - 1 - position))
    return factor_of


def centred(key, shape, width, reach, pieces=(), held_as=jnp.bfloat16):
    gain = steps_of(key, shape, pieces, -0.22, 0.18) if pieces else 1.0
    entries = jax.random.normal(key, shape, jnp.float32) * width * gain
    return jnp.minimum(jnp.maximum(entries, -reach), reach).astype(held_as)


def setup_inputs(seed: int = 0) -> dict:
    arg_keys = jax.random.split(jax.random.key(seed), 7)
    solution = centred(arg_keys[0], (CHANNELS, N, N), 1.0, 6.0, ((0, 8), (1, 4)), jnp.float32)
    residual = draw_residual(jax.random.fold_in(arg_keys[6], 71), 0)
    direction = draw_direction(jax.random.fold_in(arg_keys[6], 71), 0)
    spectra = jnp.clip(jnp.exp(math.log(1.0) - 2.9957323 * jax.random.uniform(arg_keys[3], (CHANNELS, L, L), jnp.float32) ** steps_of(arg_keys[3], (CHANNELS, L, L), ((0, 8), (2, 4)), -0.2, 0.2)), 0.05, 1.0)
    basis = centred(arg_keys[4], (CHANNELS, RANK), CHANNELS ** -0.5, 2.0, (), jnp.float32)
    slot_channel = jax.random.permutation(arg_keys[5], CHANNELS).astype(jnp.int32)
    return dict(solution=solution, residual=residual, direction=direction, spectra=spectra, basis=basis, slot_channel=slot_channel)


PRIOR_FLOOR = 0.25


def convolve(planes, spectrum):
    padded = jnp.pad(planes, ((0, L - N), (0, L - N)))
    freqs = jnp.fft.fft2(padded)
    inverse = jnp.real(jnp.fft.ifft2(freqs * spectrum))
    return inverse[:N, :N].astype(planes.dtype)


def reference(solution, residual, direction, spectra, basis, slot_channel):
    blurred = lax.map(lambda pair_in: convolve(pair_in[0], pair_in[1]), (direction, spectra))
    loadings = basis[slot_channel.astype(jnp.int32)]
    coeffs = jnp.einsum("cq,cij->qij", loadings, direction, precision=lax.Precision.HIGHEST)
    applied = blurred + PRIOR_FLOOR * direction + jnp.einsum("cq,qij->cij", loadings, coeffs, precision=lax.Precision.HIGHEST)
    norm_now = jnp.sum(residual * residual)
    curvature = jnp.sum(direction * applied)
    step_size = norm_now / curvature
    new_solution = solution + step_size * direction
    new_residual = residual - step_size * applied
    norm_next = jnp.sum(new_residual * new_residual)
    new_direction = new_residual + (norm_next / norm_now) * direction
    return (new_solution, new_residual, new_direction)
```

```python
import functools
import math

import jax
import jax.numpy as jnp
import ml_dtypes
import numpy as np
from jax import lax
from jax.experimental import pallas as pl
from jax.experimental.pallas import tpu as pltpu
from jax.sharding import PartitionSpec as P

RADIX = 32
FINE = 128
ROOT = 64
LANES = 128
TILE = 256
HIGHEST = lax.Precision.HIGHEST
PRIOR_FLOOR = 0.25
HALF = math.sqrt(0.5)
MESH = pl.DeviceIdType.MESH


def np_split(table):
    high = table.astype(ml_dtypes.bfloat16)
    low = (table - high.astype(np.float64)).astype(ml_dtypes.bfloat16)
    return high, low


@functools.cache
def row_tables():
    length = RADIX * FINE
    coarse = np.arange(RADIX)[:, None, None]
    fine = np.arange(FINE)[None, :, None]
    place = np.arange(FINE)[None, None, :]
    angle = -2.0 * np.pi * ((place * (RADIX * fine + coarse)) % length) / length
    real, imag = np.cos(angle), np.sin(angle)
    forward = np.concatenate(
        [np.concatenate([real, -imag], axis=2), np.concatenate([imag, real], axis=2)], axis=1
    )
    inverse = np.transpose(forward, (0, 2, 1)) / float(length * length)
    return np_split(forward) + np_split(inverse)


@functools.cache
def column_factors(width, length):
    column = np.arange(length)[None, :]

    def wave(rows):
        angle = -2.0 * np.pi * ((rows[:, None] * column) % length) / length
        return np.cos(angle).astype(np.float32), np.sin(angle).astype(np.float32)

    return wave(np.arange(width // ROOT) * ROOT) + wave(np.arange(ROOT))


def split(values):
    high = values.astype(jnp.bfloat16)
    low = (values - high.astype(jnp.float32)).astype(jnp.bfloat16)
    return high, low


def turn(real, imag, num, den, sign):
    num %= den
    if (num * 8) % den == 0:
        eighth = (sign * (num * 8 // den)) % 8
        if eighth == 0:
            return real, imag
        if eighth == 1:
            return (real - imag) * HALF, (real + imag) * HALF
        if eighth == 2:
            return -imag, real
        if eighth == 3:
            return (real + imag) * -HALF, (real - imag) * HALF
        if eighth == 4:
            return -real, -imag
        if eighth == 5:
            return (imag - real) * HALF, (real + imag) * -HALF
        if eighth == 6:
            return imag, -real
        return (real + imag) * HALF, (imag - real) * HALF
    c = math.cos(2.0 * math.pi * num / den)
    s = sign * math.sin(2.0 * math.pi * num / den)
    return real * c - imag * s, real * s + imag * c


def fft(points, sign):
    count = len(points)
    if count == 1:
        return points
    half = count // 2
    even, odd = [], []
    for i in range(half):
        (ar, ai), (br, bi) = points[i], points[i + half]
        even.append((ar + br, ai + bi))
        if 4 * i == count:
            odd.append((ai - bi, br - ar) if sign < 0 else (bi - ai, ar - br))
        else:
            odd.append(turn(ar - br, ai - bi, i, count, sign))
    result = [None] * count
    result[0::2] = fft(even, sign)
    result[1::2] = fft(odd, sign)
    return result


def dot3(table_high, table_low, values):
    high, low = split(values)
    dot = functools.partial(jnp.dot, preferred_element_type=jnp.float32)
    return dot(table_high, high) + dot(table_low, high) + dot(table_high, low)


def row_kernel(slot_ref, planes_ref, *refs):
    lanes = planes_ref.shape[2] // LANES
    spectra = refs[:lanes]
    forward_high, forward_low, inverse_high, inverse_low, _, out_ref, work = refs[lanes:]
    used = RADIX // 2
    slots = [slot_ref[a] * FINE for a in range(used)]
    steps = FINE // 8 * lanes

    def position(step):
        col = pl.ds(pl.multiple_of(step % lanes * LANES, LANES), LANES)
        return step // lanes * 8, col

    def rows(base, at):
        return pl.ds(pl.multiple_of(base + at, 8), 8)

    def forward(step, _):
        at, col = position(step)
        points = [(planes_ref[0, rows(s, at), col], planes_ref[1, rows(s, at), col]) for s in slots]
        for k, (real, imag) in enumerate(fft(points, -1)):
            work[2 * k, rows(0, at), col] = real
            work[2 * k, rows(FINE, at), col] = imag
        points = [turn(*point, a, RADIX, -1) for a, point in enumerate(points)]
        for k, (real, imag) in enumerate(fft(points, -1)):
            work[2 * k + 1, rows(0, at), col] = real
            work[2 * k + 1, rows(FINE, at), col] = imag
        return 0

    lax.fori_loop(0, steps, forward, 0)

    def middle(k, _):
        freqs = dot3(forward_high[k], forward_low[k], work[k])
        weight = jnp.concatenate(
            [ref[pl.ds(k, FINE, stride=RADIX), :] for ref in spectra], axis=1
        )
        freqs = freqs * jnp.concatenate([weight, weight], axis=0)
        work[k] = dot3(inverse_high[k], inverse_low[k], freqs)
        return 0

    lax.fori_loop(0, RADIX, middle, 0, unroll=16)

    def inverse(step, _):
        at, col = position(step)

        def side(odd):
            points = [
                (work[2 * k + odd, rows(0, at), col], work[2 * k + odd, rows(FINE, at), col])
                for k in range(used)
            ]
            return fft(points, 1)

        even, odd = side(0), side(1)
        for a, s in enumerate(slots):
            real, imag = turn(*odd[a], a, RADIX, 1)
            out_ref[0, rows(s, at), col] = even[a][0] + real
            out_ref[1, rows(s, at), col] = even[a][1] + imag
        return 0

    lax.fori_loop(0, steps, inverse, 0)


def row_pass(planes, spectrum, slots, after):
    _, height, columns = planes.shape
    tables = [jnp.asarray(table) for table in row_tables()]
    lanes = TILE // LANES
    whole = pl.BlockSpec(
        (RADIX, 2 * FINE, 2 * FINE), lambda i, s: (0, 0, 0), pipeline_mode=pl.Buffered(1)
    )
    tile = pl.BlockSpec((2, height, TILE), lambda i, s: (0, 0, i))
    strips = [
        pl.BlockSpec((2 * height, LANES), lambda i, s, c=c: (0, i * lanes + c))
        for c in range(lanes)
    ]
    return pl.pallas_call(
        row_kernel,
        grid_spec=pltpu.PrefetchScalarGridSpec(
            num_scalar_prefetch=1,
            grid=(columns // TILE,),
            in_specs=[tile] + strips + [whole] * 4 + [pl.BlockSpec(memory_space=pl.ANY)],
            out_specs=tile,
            scratch_shapes=[pltpu.VMEM((RADIX, 2 * FINE, TILE), jnp.float32)],
        ),
        out_shape=jax.ShapeDtypeStruct(planes.shape, jnp.float32),
        compiler_params=pltpu.CompilerParams(vmem_limit_bytes=60 << 20),
        cost_estimate=pl.CostEstimate(
            flops=6 * 2 * 256 * RADIX * 256 * columns, bytes_accessed=64 << 20, transcendentals=0
        ),
        name="row_pass",
    )(slots, planes, *([spectrum] * lanes), *tables, after)


def table_kernel(place_ref, coarse_real, coarse_imag, fine_real, fine_imag, high_ref, low_ref):
    columns = fine_real.shape[1]
    row = pl.ds(pl.program_id(0) % 8, 1)
    cr, ci = coarse_real[row, :], coarse_imag[row, :]
    fr, fi = fine_real[...], fine_imag[...]
    high_ref[:, :columns], low_ref[:, :columns] = split(cr * fr - ci * fi)
    high_ref[:, columns:], low_ref[:, columns:] = split(cr * fi + ci * fr)


def width_table(width, columns, length, place):
    factors = [jnp.asarray(factor) for factor in column_factors(width, length)]
    coarse = pl.BlockSpec((8, columns), lambda i, p: (i // 8, p[0]))
    fine = pl.BlockSpec((ROOT, columns), lambda i, p: (0, p[0]))
    out = pl.BlockSpec((ROOT, 2 * columns), lambda i, p: (i, 0))
    return pl.pallas_call(
        table_kernel,
        grid_spec=pltpu.PrefetchScalarGridSpec(
            num_scalar_prefetch=1,
            grid=(width // ROOT,),
            in_specs=[coarse, coarse, fine, fine],
            out_specs=[out, out],
        ),
        out_shape=[jax.ShapeDtypeStruct((width, 2 * columns), jnp.bfloat16)] * 2,
        cost_estimate=pl.CostEstimate(
            flops=20 * width * columns, bytes_accessed=8 * width * columns, transcendentals=0
        ),
        name="width_table",
    )(place.reshape(1), *factors)


def width_kernel(count, *refs):
    blocks = refs[:count]
    table_high, table_low = refs[count : count + 2]
    out_ref, high_ref, low_ref = refs[-3:]

    @pl.when(pl.program_id(0) == 0)
    def _():
        base = 0
        for ref in blocks:
            rows = ref.shape[0]
            high_ref[base : base + rows], low_ref[base : base + rows] = split(ref[...])
            base += rows

    dot = functools.partial(jnp.dot, preferred_element_type=jnp.float32)
    high, low = high_ref[...], low_ref[...]
    weight = table_high[...]
    out_ref[0] = dot(high, weight) + dot(low, weight) + dot(high, table_low[...])


def width_forward(blocks, tables, planes, first, columns, height):
    width = blocks[0].shape[1]
    total = sum(block.shape[0] for block in blocks)
    tiles = columns // TILE
    before = [] if planes is None else [planes]
    table = pl.BlockSpec((width, TILE), lambda n: (0, n))
    return pl.pallas_call(
        functools.partial(width_kernel, len(blocks)),
        grid=(2 * tiles,),
        in_specs=[pl.BlockSpec(block.shape, lambda n: (0, 0)) for block in blocks]
        + [table, table]
        + [pl.BlockSpec(memory_space=pl.ANY)] * len(before),
        out_specs=pl.BlockSpec(
            (1, total, TILE), lambda n: (n // tiles, first // total, n % tiles)
        ),
        out_shape=jax.ShapeDtypeStruct((2, height, columns), jnp.float32),
        scratch_shapes=[pltpu.VMEM((total, width), jnp.bfloat16)] * 2,
        input_output_aliases={len(blocks) + 2: 0} if before else {},
        compiler_params=pltpu.CompilerParams(vmem_limit_bytes=48 << 20),
        cost_estimate=pl.CostEstimate(
            flops=12 * total * width * columns,
            bytes_accessed=8 * width * columns + 4 * total * (width + 2 * columns),
            transcendentals=0,
        ),
        name="width_forward",
    )(*blocks, *tables, *before)


def back_kernel(count, planes_ref, table_high, table_low, _, *refs):
    outs = refs[:count]
    high_ref, low_ref = refs[count:]
    columns = planes_ref.shape[2]

    @pl.when(pl.program_id(0) == 0)
    def _():
        for part in range(2):
            col = slice(part * columns, (part + 1) * columns)
            high_ref[:, col], low_ref[:, col] = split(planes_ref[part])

    wide = (((1,), (1,)), ((), ()))
    dot = functools.partial(
        lax.dot_general, dimension_numbers=wide, preferred_element_type=jnp.float32
    )
    high, low = high_ref[...], low_ref[...]
    weight = table_high[...]
    image = dot(high, weight) + dot(low, weight) + dot(high, table_low[...])
    base = 0
    for ref in outs:
        rows = ref.shape[0]
        ref[...] = image[base : base + rows]
        base += rows


def width_back(planes, tables, first, sizes, after):
    _, _, columns = planes.shape
    width = tables[0].shape[0]
    total = sum(sizes)
    table = pl.BlockSpec((TILE, 2 * columns), lambda n: (n, 0))
    return pl.pallas_call(
        functools.partial(back_kernel, len(sizes)),
        grid=(width // TILE,),
        in_specs=[
            pl.BlockSpec((2, total, columns), lambda n: (0, first // total, 0)),
            table,
            table,
            pl.BlockSpec(memory_space=pl.ANY),
        ],
        out_specs=[pl.BlockSpec((rows, TILE), lambda n: (0, n)) for rows in sizes],
        out_shape=[jax.ShapeDtypeStruct((rows, width), jnp.float32) for rows in sizes],
        scratch_shapes=[pltpu.VMEM((total, 2 * columns), jnp.bfloat16)] * 2,
        compiler_params=pltpu.CompilerParams(vmem_limit_bytes=48 << 20),
        cost_estimate=pl.CostEstimate(
            flops=12 * total * width * columns,
            bytes_accessed=8 * width * columns + 4 * total * (width + 2 * columns),
            transcendentals=0,
        ),
        name="width_back",
    )(planes, *tables, after)


def prior_kernel(gram_ref, cube_ref, out_ref):
    count = cube_ref.shape[0]
    for c in range(count):
        total = gram_ref[c, 0] * cube_ref[0]
        for k in range(1, count):
            total = total + gram_ref[c, k] * cube_ref[k]
        out_ref[c] = total


def prior_term(cube, gram):
    count, rows, width = cube.shape
    block = pl.BlockSpec((count, 8, width), lambda i: (0, i, 0))
    return pl.pallas_call(
        prior_kernel,
        grid=(rows // 8,),
        in_specs=[pl.BlockSpec(memory_space=pltpu.SMEM), block],
        out_specs=block,
        out_shape=jax.ShapeDtypeStruct(cube.shape, jnp.float32),
        cost_estimate=pl.CostEstimate(
            flops=2 * count * cube.size, bytes_accessed=8 * cube.size, transcendentals=0
        ),
        name="prior_term",
    )(gram, cube)


def moment_kernel(terms, *refs):
    parts = refs[:terms]
    residual_ref, direction_ref = refs[terms : terms + 2]
    applied_ref, moment_ref = refs[-2:]

    @pl.when(pl.program_id(0) == 0)
    def _():
        moment_ref[...] = jnp.zeros_like(moment_ref)

    applied = parts[0][...]
    for ref in parts[1:]:
        applied = applied + ref[...]
    applied_ref[...] = applied
    residual, direction = residual_ref[...], direction_ref[...]
    width = applied.shape[1]

    def fold(product):
        total = product[:8]
        for at in range(8, product.shape[0], 8):
            total = total + product[at : at + 8]
        folded = total[:, :LANES]
        for at in range(LANES, width, LANES):
            folded = folded + total[:, at : at + LANES]
        return folded

    moment_ref[0] += fold(residual * residual)
    moment_ref[1] += fold(direction * applied)
    moment_ref[2] += fold(residual * applied)
    moment_ref[3] += fold(applied * applied)


def moments_of(wide, chunk, residual, direction, applied, first):
    rows, width = chunk[0].shape
    step = 64 if rows % 64 == 0 else rows
    at = first // step
    here = pl.BlockSpec((step, width), lambda i: (at + i, 0))
    own = pl.BlockSpec((step, width), lambda i: (i, 0))
    terms = len(wide) + len(chunk)
    before = [] if applied is None else [applied]
    return pl.pallas_call(
        functools.partial(moment_kernel, terms),
        grid=(rows // step,),
        in_specs=[here] * len(wide)
        + [own] * len(chunk)
        + [here, here]
        + [pl.BlockSpec(memory_space=pl.ANY)] * len(before),
        out_specs=[here, pl.BlockSpec((4, 8, LANES), lambda i: (0, 0, 0))],
        out_shape=[
            jax.ShapeDtypeStruct(residual.shape, jnp.float32),
            jax.ShapeDtypeStruct((4, 8, LANES), jnp.float32),
        ],
        input_output_aliases={terms + 2: 0} if before else {},
        cost_estimate=pl.CostEstimate(
            flops=10 * rows * width,
            bytes_accessed=4 * (terms + 3) * rows * width,
            transcendentals=0,
        ),
        name="moments",
    )(*wide, *chunk, residual, direction, *before)


def reduce_kernel(axes, sizes, parts, *refs):
    inputs = refs[:parts]
    out_ref, mine, landed, send_sem, recv_sem = refs[parts:]
    barrier = pltpu.get_barrier_semaphore()

    def peers(axis):
        size = sizes[axis]
        me = lax.axis_index(axes[axis])
        return [lax.rem(me + hop, size) for hop in range(1, size)]

    for axis in range(2):
        for peer in peers(axis):
            pl.semaphore_signal(barrier, inc=1, device_id={axes[axis]: peer}, device_id_type=MESH)
    total = inputs[0][...]
    for ref in inputs[1:]:
        total = total + ref[...]
    pl.semaphore_wait(barrier, sizes[0] + sizes[1] - 2)
    slot = 0
    for axis in range(2):
        mine[axis] = total
        copies = []
        for hop, peer in enumerate(peers(axis)):
            copies.append(
                pltpu.make_async_remote_copy(
                    src_ref=mine.at[axis],
                    dst_ref=landed.at[slot + hop],
                    send_sem=send_sem.at[slot + hop],
                    recv_sem=recv_sem.at[slot + hop],
                    device_id={axes[axis]: peer},
                    device_id_type=MESH,
                )
            )
        for copy in copies:
            copy.start()
        for hop, copy in enumerate(copies):
            copy.wait()
        me = lax.axis_index(axes[axis])
        size = sizes[axis]
        total = jnp.zeros_like(total)
        for source in range(size):
            hop = lax.rem(me - source + size, size)
            got = landed[slot + jnp.maximum(hop, 1) - 1]
            total = total + jnp.where(hop == 0, mine[axis], got)
        slot += size - 1
    sums = jnp.sum(jnp.sum(total, axis=2, keepdims=True), axis=1, keepdims=True)
    out_ref[...] = jnp.broadcast_to(sums, total.shape)


def reduce_moments(moments, axes, sizes):
    shape = moments[0].shape
    slots = sizes[0] + sizes[1] - 2
    return pl.pallas_call(
        functools.partial(reduce_kernel, axes, sizes, len(moments)),
        out_shape=jax.ShapeDtypeStruct(shape, jnp.float32),
        in_specs=[pl.BlockSpec(memory_space=pltpu.VMEM)] * len(moments),
        out_specs=pl.BlockSpec(memory_space=pltpu.VMEM),
        scratch_shapes=[
            pltpu.VMEM((2,) + shape, jnp.float32),
            pltpu.VMEM((slots,) + shape, jnp.float32),
            pltpu.SemaphoreType.DMA((slots,)),
            pltpu.SemaphoreType.DMA((slots,)),
        ],
        compiler_params=pltpu.CompilerParams(collective_id=0, has_side_effects=True),
        name="reduce_moments",
    )(*moments)


def update_kernel(
    sum_ref, solution_ref, residual_ref, direction_ref, applied_ref, x_ref, r_ref, d_ref
):
    def scalar(at):
        return sum_ref[at, 0:1, 0:1]

    norm_now, curvature, cross, square = [scalar(at) for at in range(4)]
    step_size = norm_now / curvature
    norm_next = norm_now - 2.0 * step_size * cross + step_size * step_size * square
    ratio = norm_next / norm_now
    direction = direction_ref[...]
    x_ref[...] = solution_ref[...] + step_size * direction
    residual = residual_ref[...] - step_size * applied_ref[...]
    r_ref[...] = residual
    d_ref[...] = residual + ratio * direction


def update(sums, solution, residual, direction, applied):
    height, width = applied.shape
    step = 64
    block = pl.BlockSpec((step, width), lambda i: (i, 0))
    return pl.pallas_call(
        update_kernel,
        grid=(height // step,),
        in_specs=[pl.BlockSpec(sums.shape, lambda i: (0, 0, 0))] + [block] * 4,
        out_specs=[block] * 3,
        out_shape=[jax.ShapeDtypeStruct((height, width), jnp.float32)] * 3,
        cost_estimate=pl.CostEstimate(
            flops=6 * height * width, bytes_accessed=28 * height * width, transcendentals=0
        ),
        name="update",
    )(sums, solution, residual, direction, applied)


def swap_pairs(array, count, bit):
    pairs = [(place, place ^ bit) for place in range(count)]
    return lax.ppermute(array, "facet", pairs)


def body(solution, residual, direction, spectra, basis, slot_channel):
    channel_count = basis.shape[0]
    length = RADIX * FINE
    facets = lax.axis_size("facet")
    place = lax.axis_index("facet")
    height, width = direction.shape[1:]
    columns = spectra.shape[2]
    own = direction[0]
    top = facets // 2
    per_facet = height // FINE

    stacked = own.reshape(channel_count, height // channel_count, width)
    regrouped = lax.all_to_all(stacked, "chan", split_axis=0, concat_axis=0, tiled=True)
    one_hot = (
        slot_channel[:, None] == jnp.arange(channel_count, dtype=jnp.int32)[None, :]
    ).astype(jnp.float32)
    loadings = jnp.dot(one_hot, basis, precision=HIGHEST)
    gram = jnp.einsum("cq,dq->cd", loadings, loadings, precision=HIGHEST)
    gram = gram + PRIOR_FLOOR * jnp.eye(channel_count, dtype=jnp.float32)

    chunks = [own[at * FINE : (at + 1) * FINE] for at in range(per_facet)]
    far = []
    for chunk in chunks:
        blocks = {top: swap_pairs(chunk, facets, top)}
        bit = top // 2
        while bit:
            blocks.update({key ^ bit: swap_pairs(blocks[key], facets, bit) for key in list(blocks)})
            bit //= 2
        far.append(blocks)
    near = {0: own}
    bit = top // 2
    while bit:
        near.update({key ^ bit: swap_pairs(near[key], facets, bit) for key in list(near)})
        bit //= 2

    groups = []
    if per_facet > 1:
        groups += [([near[key]], [(key, s) for s in range(per_facet)]) for key in range(top)]
    else:
        groups.append(([near[key] for key in range(top)], [(key, 0) for key in range(top)]))
    for s, blocks in enumerate(far):
        keys = range(top, facets)
        groups.append(([blocks[key] for key in keys], [(key, s) for key in keys]))
    order = [entry for _, entries in groups for entry in entries]
    slot_of = np.zeros((facets, per_facet), np.int32)
    for at, (key, s) in enumerate(order):
        slot_of[key, s] = at
    slots = jnp.asarray(slot_of)[jnp.arange(facets, dtype=jnp.int32) ^ place].reshape(-1)

    tables = width_table(width, columns, length, place)
    planes = None
    first = 0
    starts = []
    for blocks, entries in groups:
        planes = width_forward(blocks, tables, planes, first, columns, facets * height)
        starts.append(first)
        first += len(entries) * FINE

    local_prior = prior_term(regrouped, gram)
    prior = lax.all_to_all(local_prior, "chan", split_axis=0, concat_axis=0, tiled=True)
    prior = prior.reshape(height, width)

    rows = row_pass(planes, spectra[0], slots, local_prior)

    after = rows
    arrived = []
    near_sums = {}
    for (blocks, entries), start in list(zip(groups, starts))[::-1]:
        if entries[0][0] < top:
            continue
        sizes = [FINE] * len(entries)
        parts = width_back(rows, tables, start, sizes, after)
        after = parts[0]
        sums = {key: part for (key, _), part in zip(entries, parts)}
        bit = 1
        while bit < top:
            sums = {
                key: sums[key] + swap_pairs(sums[key | bit], facets, bit)
                for key in sorted(sums, reverse=True)
                if not key & bit
            }
            bit *= 2
        arrived.append((entries[0][1], swap_pairs(sums[top], facets, top)))
    for (blocks, entries), start in list(zip(groups, starts))[::-1]:
        if entries[0][0] >= top:
            continue
        if per_facet > 1:
            key = entries[0][0]
            near_sums[key] = width_back(rows, tables, start, [height], after)[0]
            after = near_sums[key]
        else:
            parts = width_back(rows, tables, start, [FINE] * len(entries), after)
            near_sums = {key: part for (key, _), part in zip(entries, parts)}
    bit = 1
    while 2 * bit < top:
        near_sums = {
            key: near_sums[key] + swap_pairs(near_sums[key | bit], facets, bit)
            for key in sorted(near_sums, reverse=True)
            if not key & bit
        }
        bit *= 2
    wide = [near_sums[0], swap_pairs(near_sums[bit], facets, bit), prior]

    applied = None
    moments = []
    for s, part in arrived:
        applied, moment = moments_of(wide, [part], residual[0], own, applied, s * FINE)
        moments.append(moment)
    sizes = (lax.axis_size("chan"), facets)
    sums = reduce_moments(moments, ("chan", "facet"), sizes)
    results = update(sums, solution[0], residual[0], own, applied)
    return tuple(result[None] for result in results)


def solution(mesh):
    return jax.shard_map(
        body,
        mesh=mesh,
        in_specs=(
            P("chan", "facet", None),
            P("chan", "facet", None),
            P("chan", "facet", None),
            P("chan", None, "facet"),
            P(),
            P(),
        ),
        out_specs=(P("chan", "facet", None), P("chan", "facet", None), P("chan", "facet", None)),
        check_vma=False,
    )
```

```python
import functools
import math

import jax
import jax.numpy as jnp
import ml_dtypes
import numpy as np
from jax import lax
from jax.experimental import pallas as pl
from jax.experimental.pallas import tpu as pltpu
from jax.sharding import PartitionSpec as P

RADIX = 32
FINE = 128
ROOT = 64
LANES = 128
TILE = 256
HIGHEST = lax.Precision.HIGHEST
PRIOR_FLOOR = 0.25
HALF = math.sqrt(0.5)
MESH = pl.DeviceIdType.MESH
SMALL = pl.CostEstimate(flops=1, bytes_accessed=1, transcendentals=0)


def np_split(table):
    high = table.astype(ml_dtypes.bfloat16)
    low = (table - high.astype(np.float64)).astype(ml_dtypes.bfloat16)
    return high, low


@functools.cache
def row_tables():
    length = RADIX * FINE
    coarse = np.arange(RADIX)[:, None, None]
    fine = np.arange(FINE)[None, :, None]
    place = np.arange(FINE)[None, None, :]
    angle = -2.0 * np.pi * ((place * (RADIX * fine + coarse)) % length) / length
    real, imag = np.cos(angle), np.sin(angle)
    forward = np.concatenate(
        [np.concatenate([real, -imag], axis=2), np.concatenate([imag, real], axis=2)], axis=1
    )
    inverse = np.transpose(forward, (0, 2, 1)) / float(length * length)
    return np_split(forward) + np_split(inverse)


@functools.cache
def column_factors(width, length):
    column = np.arange(length)[None, :]

    def wave(rows):
        angle = -2.0 * np.pi * ((rows[:, None] * column) % length) / length
        return np.cos(angle).astype(np.float32), np.sin(angle).astype(np.float32)

    return wave(np.arange(width // ROOT) * ROOT) + wave(np.arange(ROOT))


def split(values):
    high = values.astype(jnp.bfloat16)
    low = (values - high.astype(jnp.float32)).astype(jnp.bfloat16)
    return high, low


def turn(real, imag, num, den, sign):
    num %= den
    if (num * 8) % den == 0:
        eighth = (sign * (num * 8 // den)) % 8
        if eighth == 0:
            return real, imag
        if eighth == 1:
            return (real - imag) * HALF, (real + imag) * HALF
        if eighth == 2:
            return -imag, real
        if eighth == 3:
            return (real + imag) * -HALF, (real - imag) * HALF
        if eighth == 4:
            return -real, -imag
        if eighth == 5:
            return (imag - real) * HALF, (real + imag) * -HALF
        if eighth == 6:
            return imag, -real
        return (real + imag) * HALF, (imag - real) * HALF
    c = math.cos(2.0 * math.pi * num / den)
    s = sign * math.sin(2.0 * math.pi * num / den)
    return real * c - imag * s, real * s + imag * c


def fft(points, sign):
    count = len(points)
    if count == 1:
        return points
    half = count // 2
    even, odd = [], []
    for i in range(half):
        (ar, ai), (br, bi) = points[i], points[i + half]
        even.append((ar + br, ai + bi))
        if 4 * i == count:
            odd.append((ai - bi, br - ar) if sign < 0 else (bi - ai, ar - br))
        else:
            odd.append(turn(ar - br, ai - bi, i, count, sign))
    result = [None] * count
    result[0::2] = fft(even, sign)
    result[1::2] = fft(odd, sign)
    return result


def dot3(table_high, table_low, values):
    high, low = split(values)
    dot = functools.partial(jnp.dot, preferred_element_type=jnp.float32)
    return dot(table_high, high) + dot(table_low, high) + dot(table_high, low)


def row_kernel(slot_ref, planes_ref, *refs):
    lanes = planes_ref.shape[2] // LANES
    spectra = refs[:lanes]
    forward_high, forward_low, inverse_high, inverse_low, out_ref, work = refs[lanes:]
    used = RADIX // 2
    slots = [slot_ref[a] * FINE for a in range(used)]
    steps = FINE // 8 * lanes

    def position(step):
        col = pl.ds(pl.multiple_of(step % lanes * LANES, LANES), LANES)
        return step // lanes * 8, col

    def rows(base, at):
        return pl.ds(pl.multiple_of(base + at, 8), 8)

    def forward(step, _):
        at, col = position(step)
        points = [(planes_ref[0, rows(s, at), col], planes_ref[1, rows(s, at), col]) for s in slots]
        for k, (real, imag) in enumerate(fft(points, -1)):
            work[2 * k, rows(0, at), col] = real
            work[2 * k, rows(FINE, at), col] = imag
        points = [turn(*point, a, RADIX, -1) for a, point in enumerate(points)]
        for k, (real, imag) in enumerate(fft(points, -1)):
            work[2 * k + 1, rows(0, at), col] = real
            work[2 * k + 1, rows(FINE, at), col] = imag
        return 0

    lax.fori_loop(0, steps, forward, 0)

    def middle(k, _):
        freqs = dot3(forward_high[k], forward_low[k], work[k])
        weight = jnp.concatenate(
            [ref[pl.ds(k, FINE, stride=RADIX), :] for ref in spectra], axis=1
        )
        freqs = freqs * jnp.concatenate([weight, weight], axis=0)
        work[k] = dot3(inverse_high[k], inverse_low[k], freqs)
        return 0

    lax.fori_loop(0, RADIX, middle, 0, unroll=16)

    def inverse(step, _):
        at, col = position(step)

        def side(odd):
            points = [
                (work[2 * k + odd, rows(0, at), col], work[2 * k + odd, rows(FINE, at), col])
                for k in range(used)
            ]
            return fft(points, 1)

        even, odd = side(0), side(1)
        for a, s in enumerate(slots):
            real, imag = turn(*odd[a], a, RADIX, 1)
            out_ref[0, rows(s, at), col] = even[a][0] + real
            out_ref[1, rows(s, at), col] = even[a][1] + imag
        return 0

    lax.fori_loop(0, steps, inverse, 0)


def row_pass(planes, spectrum, slots):
    _, height, columns = planes.shape
    tables = [jnp.asarray(table) for table in row_tables()]
    lanes = TILE // LANES
    whole = pl.BlockSpec(
        (RADIX, 2 * FINE, 2 * FINE), lambda i, s: (0, 0, 0), pipeline_mode=pl.Buffered(1)
    )
    tile = pl.BlockSpec((2, height, TILE), lambda i, s: (0, 0, i))
    strips = [
        pl.BlockSpec((2 * height, LANES), lambda i, s, c=c: (0, i * lanes + c))
        for c in range(lanes)
    ]
    return pl.pallas_call(
        row_kernel,
        grid_spec=pltpu.PrefetchScalarGridSpec(
            num_scalar_prefetch=1,
            grid=(columns // TILE,),
            in_specs=[tile] + strips + [whole] * 4,
            out_specs=tile,
            scratch_shapes=[pltpu.VMEM((RADIX, 2 * FINE, TILE), jnp.float32)],
        ),
        out_shape=jax.ShapeDtypeStruct(planes.shape, jnp.float32),
        compiler_params=pltpu.CompilerParams(vmem_limit_bytes=60 << 20),
        cost_estimate=SMALL,
        name="row_pass",
    )(slots, planes, *([spectrum] * lanes), *tables)


def table_kernel(place_ref, coarse_real, coarse_imag, fine_real, fine_imag, high_ref, low_ref):
    columns = fine_real.shape[1]
    row = pl.ds(pl.program_id(0) % 8, 1)
    coarse_r, coarse_i = coarse_real[row, :], coarse_imag[row, :]
    for at in range(0, columns, LANES):
        real, imag = slice(at, at + LANES), slice(columns + at, columns + at + LANES)
        cr, ci = coarse_r[:, real], coarse_i[:, real]
        fr, fi = fine_real[:, real], fine_imag[:, real]
        high_ref[:, real], low_ref[:, real] = split(cr * fr - ci * fi)
        high_ref[:, imag], low_ref[:, imag] = split(cr * fi + ci * fr)


def width_table(width, columns, length, place):
    factors = [jnp.asarray(factor) for factor in column_factors(width, length)]
    coarse = pl.BlockSpec((8, columns), lambda i, p: (i // 8, p[0]))
    fine = pl.BlockSpec((ROOT, columns), lambda i, p: (0, p[0]))
    out = pl.BlockSpec((ROOT, 2 * columns), lambda i, p: (i, 0))
    return pl.pallas_call(
        table_kernel,
        grid_spec=pltpu.PrefetchScalarGridSpec(
            num_scalar_prefetch=1,
            grid=(width // ROOT,),
            in_specs=[coarse, coarse, fine, fine],
            out_specs=[out, out],
        ),
        out_shape=[jax.ShapeDtypeStruct((width, 2 * columns), jnp.bfloat16)] * 2,
        cost_estimate=SMALL,
        name="width_table",
    )(place.reshape(1), *factors)


def width_kernel(count, *refs):
    blocks = refs[:count]
    table_high, table_low = refs[count : count + 2]
    out_ref, high_ref, low_ref = refs[-3:]

    @pl.when(pl.program_id(0) == 0)
    def _():
        base = 0
        for ref in blocks:
            rows = ref.shape[0]
            high_ref[base : base + rows], low_ref[base : base + rows] = split(ref[...])
            base += rows

    dot = functools.partial(jnp.dot, preferred_element_type=jnp.float32)
    high, low = high_ref[...], low_ref[...]
    weight = table_high[...]
    out_ref[0] = dot(high, weight) + dot(low, weight) + dot(high, table_low[...])


def width_forward(blocks, tables, planes, first, columns, height):
    width = blocks[0].shape[1]
    total = sum(block.shape[0] for block in blocks)
    tiles = columns // TILE
    before = [] if planes is None else [planes]
    table = pl.BlockSpec((width, TILE), lambda n: (0, n))
    return pl.pallas_call(
        functools.partial(width_kernel, len(blocks)),
        grid=(2 * tiles,),
        in_specs=[pl.BlockSpec(block.shape, lambda n: (0, 0)) for block in blocks]
        + [table, table]
        + [pl.BlockSpec(memory_space=pl.ANY)] * len(before),
        out_specs=pl.BlockSpec(
            (1, total, TILE), lambda n: (n // tiles, first // total, n % tiles)
        ),
        out_shape=jax.ShapeDtypeStruct((2, height, columns), jnp.float32),
        scratch_shapes=[pltpu.VMEM((total, width), jnp.bfloat16)] * 2,
        input_output_aliases={len(blocks) + 2: 0} if before else {},
        compiler_params=pltpu.CompilerParams(vmem_limit_bytes=48 << 20),
        cost_estimate=SMALL,
        name="width_forward",
    )(*blocks, *tables, *before)


def back_kernel(count, planes_ref, table_high, table_low, *refs):
    outs = refs[-count - 2 : -2]
    high_ref, low_ref = refs[-2:]
    columns = planes_ref.shape[2]

    @pl.when(pl.program_id(0) == 0)
    def _():
        for part in range(2):
            col = slice(part * columns, (part + 1) * columns)
            high_ref[:, col], low_ref[:, col] = split(planes_ref[part])

    wide = (((1,), (1,)), ((), ()))
    dot = functools.partial(
        lax.dot_general, dimension_numbers=wide, preferred_element_type=jnp.float32
    )
    high, low = high_ref[...], low_ref[...]
    weight = table_high[...]
    image = dot(high, weight) + dot(low, weight) + dot(high, table_low[...])
    base = 0
    for ref in outs:
        rows = ref.shape[0]
        ref[...] = image[base : base + rows]
        base += rows


def width_back(planes, tables, first, sizes, after):
    _, _, columns = planes.shape
    width = tables[0].shape[0]
    total = sum(sizes)
    table = pl.BlockSpec((TILE, 2 * columns), lambda n: (n, 0))
    return pl.pallas_call(
        functools.partial(back_kernel, len(sizes)),
        grid=(width // TILE,),
        in_specs=[
            pl.BlockSpec((2, total, columns), lambda n: (0, first // total, 0)),
            table,
            table,
        ]
        + [pl.BlockSpec(memory_space=pl.ANY)] * len(after),
        out_specs=[pl.BlockSpec((rows, TILE), lambda n: (0, n)) for rows in sizes],
        out_shape=[jax.ShapeDtypeStruct((rows, width), jnp.float32) for rows in sizes],
        scratch_shapes=[pltpu.VMEM((total, 2 * columns), jnp.bfloat16)] * 2,
        compiler_params=pltpu.CompilerParams(vmem_limit_bytes=48 << 20),
        cost_estimate=SMALL,
        name="width_back",
    )(planes, *tables, *after)


def prior_kernel(gram_ref, cube_ref, _, out_ref):
    count, rows, width = cube_ref.shape
    gram = [[gram_ref[c, k] for k in range(count)] for c in range(count)]
    for at in range(0, rows, 8):
        for col in range(0, width, LANES):
            here = slice(at, at + 8), slice(col, col + LANES)
            values = [cube_ref[(k,) + here] for k in range(count)]
            for c in range(count):
                total = gram[c][0] * values[0]
                for k in range(1, count):
                    total = total + gram[c][k] * values[k]
                out_ref[(c,) + here] = total


def prior_term(cube, gram, after):
    count, rows, width = cube.shape
    block = pl.BlockSpec((count, 8, width), lambda i: (0, i, 0))
    return pl.pallas_call(
        prior_kernel,
        grid=(rows // 8,),
        in_specs=[
            pl.BlockSpec(memory_space=pltpu.SMEM),
            block,
            pl.BlockSpec(memory_space=pl.ANY),
        ],
        out_specs=block,
        out_shape=jax.ShapeDtypeStruct(cube.shape, jnp.float32),
        cost_estimate=SMALL,
        name="prior_term",
    )(gram, cube, after)


def moment_kernel(terms, *refs):
    parts = refs[:terms]
    residual_ref, direction_ref = refs[terms : terms + 2]
    applied_ref, moment_ref = refs[-2:]

    @pl.when(pl.program_id(0) == 0)
    def _():
        moment_ref[...] = jnp.zeros_like(moment_ref)

    applied = parts[0][...]
    for ref in parts[1:]:
        applied = applied + ref[...]
    applied_ref[...] = applied
    residual, direction = residual_ref[...], direction_ref[...]
    width = applied.shape[1]

    def fold(product):
        total = product[:8]
        for at in range(8, product.shape[0], 8):
            total = total + product[at : at + 8]
        folded = total[:, :LANES]
        for at in range(LANES, width, LANES):
            folded = folded + total[:, at : at + LANES]
        return folded

    moment_ref[0] += fold(residual * residual)
    moment_ref[1] += fold(direction * applied)
    moment_ref[2] += fold(residual * applied)
    moment_ref[3] += fold(applied * applied)


def moments_of(wide, prior, chunk, residual, direction, applied, first):
    rows, width = chunk.shape
    step = min(64, rows)
    at = first // step
    here = pl.BlockSpec((step, width), lambda i: (at + i, 0))
    chunk_spec = pl.BlockSpec((step, width), lambda i: (i, 0))
    terms = len(wide) + 2
    before = [] if applied is None else [applied]
    return pl.pallas_call(
        functools.partial(moment_kernel, terms),
        grid=(rows // step,),
        in_specs=[here] * len(wide)
        + [here, chunk_spec, here, here]
        + [pl.BlockSpec(memory_space=pl.ANY)] * len(before),
        out_specs=[here, pl.BlockSpec((4, 8, LANES), lambda i: (0, 0, 0))],
        out_shape=[
            jax.ShapeDtypeStruct(residual.shape, jnp.float32),
            jax.ShapeDtypeStruct((4, 8, LANES), jnp.float32),
        ],
        input_output_aliases={terms + 2: 0} if before else {},
        cost_estimate=SMALL,
        name="moments",
    )(*wide, prior, chunk, residual, direction, *before)


def group_sum(axes, sizes, total, out_ref, mine, landed, send_sem, recv_sem):
    slot = 0
    for axis in range(2):
        size = sizes[axis]
        me = lax.axis_index(axes[axis])
        mine[axis] = total
        copies = [
            pltpu.make_async_remote_copy(
                src_ref=mine.at[axis],
                dst_ref=landed.at[slot + hop - 1],
                send_sem=send_sem.at[slot + hop - 1],
                recv_sem=recv_sem.at[slot + hop - 1],
                device_id={axes[axis]: lax.rem(me + hop, size)},
                device_id_type=MESH,
            )
            for hop in range(1, size)
        ]
        for copy in copies:
            copy.start()
        for copy in copies:
            copy.wait()
        total = jnp.zeros_like(total)
        for source in range(size):
            hop = lax.rem(me - source + size, size)
            arrived = landed[slot + jnp.maximum(hop, 1) - 1]
            total = total + jnp.where(hop == 0, mine[axis], arrived)
        slot += size - 1
    sums = jnp.sum(jnp.sum(total, axis=2, keepdims=True), axis=1, keepdims=True)
    out_ref[...] = jnp.broadcast_to(sums, total.shape)


def reduce_kernel(axes, sizes, parts, *refs):
    inputs = refs[:parts]
    out_ref, mine, landed, send_sem, recv_sem = refs[parts:]
    barrier = pltpu.get_barrier_semaphore()
    for axis in range(2):
        me = lax.axis_index(axes[axis])
        for hop in range(1, sizes[axis]):
            peer = lax.rem(me + hop, sizes[axis])
            pl.semaphore_signal(barrier, inc=1, device_id={axes[axis]: peer}, device_id_type=MESH)
    total = inputs[0][...]
    for ref in inputs[1:]:
        total = total + ref[...]
    pl.semaphore_wait(barrier, sizes[0] + sizes[1] - 2)
    group_sum(axes, sizes, total, out_ref, mine, landed, send_sem, recv_sem)


def reduce_moments(moments, axes, sizes):
    shape = moments[0].shape
    slots = sizes[0] + sizes[1] - 2
    return pl.pallas_call(
        functools.partial(reduce_kernel, axes, sizes, len(moments)),
        out_shape=jax.ShapeDtypeStruct(shape, jnp.float32),
        in_specs=[pl.BlockSpec(memory_space=pltpu.VMEM)] * len(moments),
        out_specs=pl.BlockSpec(memory_space=pltpu.VMEM),
        scratch_shapes=[
            pltpu.VMEM((2,) + shape, jnp.float32),
            pltpu.VMEM((slots,) + shape, jnp.float32),
            pltpu.SemaphoreType.DMA((slots,)),
            pltpu.SemaphoreType.DMA((slots,)),
        ],
        compiler_params=pltpu.CompilerParams(collective_id=0, has_side_effects=True),
        cost_estimate=SMALL,
        name="reduce_moments",
    )(*moments)


def scatter_kernel(axes, sizes, rows_hbm, high_hbm, low_hbm, prior_hbm, residual_hbm,
                   direction_hbm, applied_hbm, sums_ref, table_high, table_low, held, high_ref,
                   low_ref, part, landed, beside, own, near, cross, stream, moment, mine, got,
                   table_sem, held_sem, stream_sem, out_sem, send_sem, recv_sem, group_send,
                   group_recv):
    width = table_high.shape[0]
    columns = held.shape[3]
    unit = held.shape[2]
    height = own.shape[0]
    chunks = height // FINE
    tiles = width // TILE
    place = lax.axis_index("facet")
    sibling = place + 1 - 2 * lax.rem(place, 2)
    partner = lax.rem(place + 2, 4)

    def peers(axis):
        me = lax.axis_index(axes[axis])
        return [lax.rem(me + hop, sizes[axis]) for hop in range(1, sizes[axis])]

    def table_copies(t):
        at = pl.ds(pl.multiple_of(t * TILE, TILE), TILE)
        return [
            pltpu.make_async_copy(source.at[at], target.at[at], table_sem.at[n, t])
            for n, (source, target) in enumerate(((high_hbm, table_high), (low_hbm, table_low)))
        ]

    firsts = [2 * height + unit * c for c in range(chunks)]
    firsts += [height + unit * h for h in range(height // unit)]
    firsts += [unit * h for h in range(height // unit)]
    loads = [
        pltpu.make_async_copy(
            rows_hbm.at[:, pl.ds(first, unit)], held.at[u % 2], held_sem.at[u % 2]
        )
        for u, first in enumerate(firsts)
    ]

    barrier = pltpu.get_barrier_semaphore()
    loads[0].start()
    for t in range(tiles):
        for copy in table_copies(t):
            copy.start()
    for axis in range(2):
        for peer in peers(axis):
            pl.semaphore_signal(barrier, inc=1, device_id={axes[axis]: peer}, device_id_type=MESH)

    def image(u, target):
        loads[u].wait()
        if u + 1 < len(loads):
            loads[u + 1].start()
        for part_at in range(2):
            col = slice(part_at * columns, (part_at + 1) * columns)
            high_ref[:, col], low_ref[:, col] = split(held[u % 2, part_at])
        wide = (((1,), (1,)), ((), ()))
        dot = functools.partial(
            lax.dot_general, dimension_numbers=wide, preferred_element_type=jnp.float32
        )

        def tile(t, _):
            if u == 0:
                for copy in table_copies(t):
                    copy.wait()
            at = pl.ds(pl.multiple_of(t * TILE, TILE), TILE)
            weight = table_high[at, :]
            high = high_ref[...]
            target[:, at] = (
                dot(high, weight) + dot(low_ref[...], weight) + dot(high, table_low[at, :])
            )
            return 0

        lax.fori_loop(0, tiles, tile, 0)

    def remote(source, target, slot, device):
        return pltpu.make_async_remote_copy(
            src_ref=source,
            dst_ref=target,
            send_sem=send_sem.at[slot],
            recv_sem=recv_sem.at[slot],
            device_id={"facet": device},
            device_id_type=MESH,
        )

    def chunk_rows(c):
        return pl.ds(c * FINE, FINE)

    paired = [
        remote(part.at[c, pl.ds(FINE, FINE)], landed.at[c], c, sibling) for c in range(chunks)
    ]
    crossing = [
        remote(part.at[c, pl.ds(0, FINE)], cross.at[chunk_rows(c)], chunks + c, partner)
        for c in range(chunks)
    ]
    halves = height // unit
    nearby = [
        remote(
            beside.at[h], near.at[pl.ds(h * unit, unit)], 2 * chunks + h, sibling
        )
        for h in range(halves)
    ]

    def cross_over(c):
        paired[c].wait_recv()

        def add(i, _):
            at = pl.ds(pl.multiple_of(i * 8, 8), 8)
            part[c, at, :] += landed[c, at, :]
            return 0

        lax.fori_loop(0, FINE // 8, add, 0)
        crossing[c].start()

    for c in range(chunks):
        image(c, part.at[c])
        if c == 0:
            pl.semaphore_wait(barrier, sizes[0] + sizes[1] - 2)
        paired[c].start()
        if c:
            cross_over(c - 1)
    for h in range(halves):
        image(chunks + h, beside.at[h])
        if h == 0:
            cross_over(chunks - 1)
        nearby[h].start()
    streams = [
        [
            pltpu.make_async_copy(source.at[chunk_rows(c)], stream.at[n], stream_sem.at[n])
            for n, source in enumerate((prior_hbm, residual_hbm, direction_hbm))
        ]
        for c in range(chunks)
    ]
    for copy in streams[0]:
        copy.start()
    for h in range(halves):
        image(chunks + halves + h, own.at[pl.ds(h * unit, unit)])

    moment[...] = jnp.zeros_like(moment)
    for copy in nearby:
        copy.wait_recv()
    outs = []

    def fold(total):
        folded = total[:, :LANES]
        for at in range(LANES, width, LANES):
            folded = folded + total[:, at : at + LANES]
        return folded

    for c in range(chunks):
        for copy in streams[c]:
            copy.wait()
        crossing[c].wait_recv()

        def gather(i, _):
            at = pl.ds(pl.multiple_of(i * 8, 8), 8)
            here = pl.ds(pl.multiple_of(c * FINE + i * 8, 8), 8)
            applied = own[here, :] + near[here, :] + cross[here, :] + stream[0, at, :]
            own[here, :] = applied
            residual, direction = stream[1, at, :], stream[2, at, :]
            moment[0] += fold(residual * residual)
            moment[1] += fold(direction * applied)
            moment[2] += fold(residual * applied)
            moment[3] += fold(applied * applied)
            return 0

        lax.fori_loop(0, FINE // 8, gather, 0)
        if c + 1 < chunks:
            for copy in streams[c + 1]:
                copy.start()
        out = pltpu.make_async_copy(
            own.at[chunk_rows(c)], applied_hbm.at[chunk_rows(c)], out_sem.at[c]
        )
        out.start()
        outs.append(out)

    group_sum(axes, sizes, moment[...], sums_ref, mine, got, group_send, group_recv)
    for copy in paired + crossing + nearby:
        copy.wait_send()
    for out in outs:
        out.wait()


def scatter(rows, tables, prior, residual, direction, sizes):
    height, width = direction.shape
    columns = rows.shape[2]
    unit = 2 * FINE
    chunks = height // FINE
    hops = sizes[0] + sizes[1] - 2
    flights = 2 * chunks + height // unit
    anywhere = pl.BlockSpec(memory_space=pl.ANY)
    shape = (4, 8, LANES)
    whole = pltpu.VMEM((height, width), jnp.float32)
    dma = pltpu.SemaphoreType.DMA
    return pl.pallas_call(
        functools.partial(scatter_kernel, ("chan", "facet"), sizes),
        in_specs=[anywhere] * 6,
        out_specs=[anywhere, pl.BlockSpec(memory_space=pltpu.VMEM)],
        out_shape=[
            jax.ShapeDtypeStruct((height, width), jnp.float32),
            jax.ShapeDtypeStruct(shape, jnp.float32),
        ],
        scratch_shapes=[
            pltpu.VMEM((width, 2 * columns), jnp.bfloat16),
            pltpu.VMEM((width, 2 * columns), jnp.bfloat16),
            pltpu.VMEM((2, 2, unit, columns), jnp.float32),
            pltpu.VMEM((unit, 2 * columns), jnp.bfloat16),
            pltpu.VMEM((unit, 2 * columns), jnp.bfloat16),
            pltpu.VMEM((chunks, unit, width), jnp.float32),
            pltpu.VMEM((chunks, FINE, width), jnp.float32),
            pltpu.VMEM((height // unit, unit, width), jnp.float32),
            whole,
            whole,
            whole,
            pltpu.VMEM((3, FINE, width), jnp.float32),
            pltpu.VMEM(shape, jnp.float32),
            pltpu.VMEM((2,) + shape, jnp.float32),
            pltpu.VMEM((hops,) + shape, jnp.float32),
            dma((2, width // TILE)),
            dma((2,)),
            dma((3,)),
            dma((chunks,)),
            dma((flights,)),
            dma((flights,)),
            dma((hops,)),
            dma((hops,)),
        ],
        compiler_params=pltpu.CompilerParams(
            collective_id=1, has_side_effects=True, vmem_limit_bytes=60 << 20
        ),
        cost_estimate=SMALL,
        name="scatter",
    )(rows, *tables, prior, residual, direction)


def update_kernel(
    sum_ref, solution_ref, residual_ref, direction_ref, applied_ref, x_ref, r_ref, d_ref
):
    def scalar(at):
        return sum_ref[at, 0:1, 0:1]

    norm_now, curvature, cross, square = [scalar(at) for at in range(4)]
    step_size = norm_now / curvature
    norm_next = norm_now - 2.0 * step_size * cross + step_size * step_size * square
    ratio = norm_next / norm_now
    direction = direction_ref[...]
    x_ref[...] = solution_ref[...] + step_size * direction
    residual = residual_ref[...] - step_size * applied_ref[...]
    r_ref[...] = residual
    d_ref[...] = residual + ratio * direction


def update(sums, solution, residual, direction, applied):
    height, width = applied.shape
    step = 64
    block = pl.BlockSpec((step, width), lambda i: (i, 0))
    return pl.pallas_call(
        update_kernel,
        grid=(height // step,),
        in_specs=[pl.BlockSpec(sums.shape, lambda i: (0, 0, 0))] + [block] * 4,
        out_specs=[block] * 3,
        out_shape=[jax.ShapeDtypeStruct((height, width), jnp.float32)] * 3,
        cost_estimate=SMALL,
        name="update",
    )(sums, solution, residual, direction, applied)


def swap_pairs(array, count, bit):
    pairs = [(place, place ^ bit) for place in range(count)]
    return lax.ppermute(array, "facet", pairs)


def body(solution, residual, direction, spectra, basis, slot_channel):
    channel_count = basis.shape[0]
    length = RADIX * FINE
    facets = lax.axis_size("facet")
    place = lax.axis_index("facet")
    height, width = direction.shape[1:]
    columns = spectra.shape[2]
    own = direction[0]
    top = facets // 2
    per_facet = height // FINE
    barrier = lax.optimization_barrier

    chunks = [own[at * FINE : (at + 1) * FINE] for at in range(per_facet)]
    crossed = [swap_pairs(chunk, facets, top) for chunk in chunks]

    def spread(block, key):
        blocks = {key: block}
        bit = top // 2
        while bit:
            blocks.update({k ^ bit: swap_pairs(blocks[k], facets, bit) for k in list(blocks)})
            bit //= 2
        return blocks

    near = spread(own, 0)

    cube = own.reshape(channel_count, height // channel_count, width)
    regrouped = lax.all_to_all(cube, "chan", split_axis=0, concat_axis=0, tiled=True)
    one_hot = (
        slot_channel[:, None] == jnp.arange(channel_count, dtype=jnp.int32)[None, :]
    ).astype(jnp.float32)
    loadings = jnp.dot(one_hot, basis, precision=HIGHEST)
    gram = jnp.einsum("cq,dq->cd", loadings, loadings, precision=HIGHEST)
    gram = gram + PRIOR_FLOOR * jnp.eye(channel_count, dtype=jnp.float32)

    groups = []
    if per_facet > 1:
        groups += [[(key, s) for s in range(per_facet)] for key in range(top)]
    else:
        groups.append([(key, 0) for key in range(top)])
    groups += [[(key, s) for key in range(top, facets)] for s in range(per_facet)]
    starts = np.cumsum([0] + [len(entries) * FINE for entries in groups])
    slot_of = np.zeros((facets, per_facet), np.int32)
    for at, (key, s) in enumerate(entry for entries in groups for entry in entries):
        slot_of[key, s] = at
    slots = jnp.asarray(slot_of)[jnp.arange(facets, dtype=jnp.int32) ^ place].reshape(-1)

    tables = width_table(width, columns, length, place)
    planes = None
    far = {}
    for step, entries in enumerate(groups):
        if entries[0][0] >= top:
            blocks = [far[s][key] for key, s in entries]
        elif per_facet > 1:
            blocks = [near[entries[0][0]]]
        else:
            blocks = [near[key] for key, _ in entries]
        planes = width_forward(
            blocks, tables, planes, int(starts[step]), columns, facets * height
        )
        if step < per_facet:
            block, planes = barrier((crossed[step], planes))
            far[step] = spread(block, top)
        if step == len(groups) - 2:
            local = prior_term(regrouped, gram, planes)
            local, planes = barrier((local, planes))
            prior = lax.all_to_all(local, "chan", split_axis=0, concat_axis=0, tiled=True)
            prior = prior.reshape(height, width)

    rows = row_pass(planes, spectra[0], slots)

    sizes = (lax.axis_size("chan"), facets)
    if facets == 4 and per_facet % 2 == 0:
        applied, sums = scatter(rows, tables, prior, residual[0], own, sizes)
        results = update(sums, solution[0], residual[0], own, applied)
        return tuple(result[None] for result in results)

    arrived = {}
    near_sums = {}
    held = [rows]
    previous = None
    sequence = [at for at in range(len(groups)) if groups[at][0][0] >= top]
    sequence += [at for at in range(len(groups)) if groups[at][0][0] < top][::-1]

    def send(entries, parts):
        sums = {key: part for (key, _), part in zip(entries, parts)}
        bit = 1
        while bit < top:
            sums = {
                key: sums[key] + swap_pairs(sums[key | bit], facets, bit)
                for key in sorted(sums, reverse=True)
                if not key & bit
            }
            bit *= 2
        arrived[entries[0][1]] = swap_pairs(sums[top], facets, top)
        return sums[top]

    for turn_at, at in enumerate(sequence):
        entries = groups[at]
        far_rows = entries[0][0] >= top
        counts = [FINE] * len(entries) if far_rows or per_facet == 1 else [height]
        parts = width_back(rows, tables, int(starts[at]), counts, held)
        held = [parts[0]]
        if previous is not None:
            held.append(send(*previous))
            previous = None
        if turn_at >= 3 and turn_at - 3 < per_facet:
            held.append(arrived[groups[sequence[turn_at - 3]][0][1]])
        if far_rows:
            previous = (entries, parts)
        else:
            near_sums.update({key: part for (key, _), part in zip(entries, parts)})
    bit = 1
    while 2 * bit < top:
        near_sums = {
            key: near_sums[key] + swap_pairs(near_sums[key | bit], facets, bit)
            for key in sorted(near_sums, reverse=True)
            if not key & bit
        }
        bit *= 2
    wide = [near_sums[0], swap_pairs(near_sums[bit], facets, bit)]

    applied = None
    moments = []
    for s in range(per_facet):
        first = s * FINE
        applied, moment = moments_of(
            wide, prior, arrived[s], residual[0], own, applied, first
        )
        moments.append(moment)
    sums = reduce_moments(moments, ("chan", "facet"), sizes)
    results = update(sums, solution[0], residual[0], own, applied)
    return tuple(result[None] for result in results)


def solution(mesh):
    return jax.shard_map(
        body,
        mesh=mesh,
        in_specs=(
            P("chan", "facet", None),
            P("chan", "facet", None),
            P("chan", "facet", None),
            P("chan", None, "facet"),
            P(),
            P(),
        ),
        out_specs=(P("chan", "facet", None), P("chan", "facet", None), P("chan", "facet", None)),
        check_vma=False,
    )
```

```python
import functools
import math

import jax
import jax.numpy as jnp
import ml_dtypes
import numpy as np
from jax import lax
from jax.experimental import pallas as pl
from jax.experimental.pallas import tpu as pltpu
from jax.sharding import PartitionSpec as P

RADIX = 32
FINE = 128
ROOT = 64
LANES = 128
TILE = 256
HIGHEST = lax.Precision.HIGHEST
PRIOR_FLOOR = 0.25
HALF = math.sqrt(0.5)
MESH = pl.DeviceIdType.MESH
SMALL = pl.CostEstimate(flops=1, bytes_accessed=1, transcendentals=0)


def np_split(table):
    high = table.astype(ml_dtypes.bfloat16)
    low = (table - high.astype(np.float64)).astype(ml_dtypes.bfloat16)
    return high, low


@functools.cache
def row_tables():
    length = RADIX * FINE
    coarse = np.arange(RADIX)[:, None, None]
    fine = np.arange(FINE)[None, :, None]
    place = np.arange(FINE)[None, None, :]
    angle = -2.0 * np.pi * ((place * (RADIX * fine + coarse)) % length) / length
    real, imag = np.cos(angle), np.sin(angle)
    forward = np.concatenate(
        [np.concatenate([real, -imag], axis=2), np.concatenate([imag, real], axis=2)], axis=1
    )
    inverse = np.transpose(forward, (0, 2, 1)) / float(length * length)
    return np_split(forward) + np_split(inverse)


@functools.cache
def column_factors(width, length):
    column = np.arange(length)[None, :]

    def wave(rows):
        angle = -2.0 * np.pi * ((rows[:, None] * column) % length) / length
        return np.cos(angle).astype(np.float32), np.sin(angle).astype(np.float32)

    return wave(np.arange(width // ROOT) * ROOT) + wave(np.arange(ROOT))


def split(values):
    high = values.astype(jnp.bfloat16)
    low = (values - high.astype(jnp.float32)).astype(jnp.bfloat16)
    return high, low


def turn(real, imag, num, den, sign):
    num %= den
    if (num * 8) % den == 0:
        eighth = (sign * (num * 8 // den)) % 8
        if eighth == 0:
            return real, imag
        if eighth == 1:
            return (real - imag) * HALF, (real + imag) * HALF
        if eighth == 2:
            return -imag, real
        if eighth == 3:
            return (real + imag) * -HALF, (real - imag) * HALF
        if eighth == 4:
            return -real, -imag
        if eighth == 5:
            return (imag - real) * HALF, (real + imag) * -HALF
        if eighth == 6:
            return imag, -real
        return (real + imag) * HALF, (imag - real) * HALF
    c = math.cos(2.0 * math.pi * num / den)
    s = sign * math.sin(2.0 * math.pi * num / den)
    return real * c - imag * s, real * s + imag * c


def fft(points, sign):
    count = len(points)
    if count == 1:
        return points
    half = count // 2
    even, odd = [], []
    for i in range(half):
        (ar, ai), (br, bi) = points[i], points[i + half]
        even.append((ar + br, ai + bi))
        if 4 * i == count:
            odd.append((ai - bi, br - ar) if sign < 0 else (bi - ai, ar - br))
        else:
            odd.append(turn(ar - br, ai - bi, i, count, sign))
    result = [None] * count
    result[0::2] = fft(even, sign)
    result[1::2] = fft(odd, sign)
    return result


def dot3(table_high, table_low, values):
    high, low = split(values)
    dot = functools.partial(jnp.dot, preferred_element_type=jnp.float32)
    return dot(table_high, high) + dot(table_low, high) + dot(table_high, low)


def row_kernel(slot_ref, planes_ref, *refs):
    lanes = planes_ref.shape[2] // LANES
    spectra = refs[:lanes]
    forward_high, forward_low, inverse_high, inverse_low, out_ref, work = refs[lanes:]
    used = RADIX // 2
    slots = [slot_ref[a] * FINE for a in range(used)]
    steps = FINE // 8 * lanes

    def position(step):
        col = pl.ds(pl.multiple_of(step % lanes * LANES, LANES), LANES)
        return step // lanes * 8, col

    def rows(base, at):
        return pl.ds(pl.multiple_of(base + at, 8), 8)

    def forward(step, _):
        at, col = position(step)
        points = [(planes_ref[0, rows(s, at), col], planes_ref[1, rows(s, at), col]) for s in slots]
        for k, (real, imag) in enumerate(fft(points, -1)):
            work[2 * k, rows(0, at), col] = real
            work[2 * k, rows(FINE, at), col] = imag
        points = [turn(*point, a, RADIX, -1) for a, point in enumerate(points)]
        for k, (real, imag) in enumerate(fft(points, -1)):
            work[2 * k + 1, rows(0, at), col] = real
            work[2 * k + 1, rows(FINE, at), col] = imag
        return 0

    lax.fori_loop(0, steps, forward, 0)

    def middle(k, _):
        freqs = dot3(forward_high[k], forward_low[k], work[k])
        weight = jnp.concatenate(
            [ref[pl.ds(k, FINE, stride=RADIX), :] for ref in spectra], axis=1
        )
        freqs = freqs * jnp.concatenate([weight, weight], axis=0)
        work[k] = dot3(inverse_high[k], inverse_low[k], freqs)
        return 0

    lax.fori_loop(0, RADIX, middle, 0, unroll=16)

    def inverse(step, _):
        at, col = position(step)

        def side(odd):
            points = [
                (work[2 * k + odd, rows(0, at), col], work[2 * k + odd, rows(FINE, at), col])
                for k in range(used)
            ]
            return fft(points, 1)

        even, odd = side(0), side(1)
        for a, s in enumerate(slots):
            real, imag = turn(*odd[a], a, RADIX, 1)
            out_ref[0, rows(s, at), col] = even[a][0] + real
            out_ref[1, rows(s, at), col] = even[a][1] + imag
        return 0

    lax.fori_loop(0, steps, inverse, 0)


def row_pass(planes, spectrum, slots):
    _, height, columns = planes.shape
    tables = [jnp.asarray(table) for table in row_tables()]
    lanes = TILE // LANES
    whole = pl.BlockSpec(
        (RADIX, 2 * FINE, 2 * FINE), lambda i, s: (0, 0, 0), pipeline_mode=pl.Buffered(1)
    )
    tile = pl.BlockSpec((2, height, TILE), lambda i, s: (0, 0, i))
    strips = [
        pl.BlockSpec((2 * height, LANES), lambda i, s, c=c: (0, i * lanes + c))
        for c in range(lanes)
    ]
    return pl.pallas_call(
        row_kernel,
        grid_spec=pltpu.PrefetchScalarGridSpec(
            num_scalar_prefetch=1,
            grid=(columns // TILE,),
            in_specs=[tile] + strips + [whole] * 4,
            out_specs=tile,
            scratch_shapes=[pltpu.VMEM((RADIX, 2 * FINE, TILE), jnp.float32)],
        ),
        out_shape=jax.ShapeDtypeStruct(planes.shape, jnp.float32),
        compiler_params=pltpu.CompilerParams(vmem_limit_bytes=60 << 20),
        cost_estimate=SMALL,
        name="row_pass",
    )(slots, planes, *([spectrum] * lanes), *tables)


def table_kernel(place_ref, coarse_real, coarse_imag, fine_real, fine_imag, high_ref, low_ref):
    columns = fine_real.shape[1]
    row = pl.ds(pl.program_id(0) % 8, 1)
    coarse_r, coarse_i = coarse_real[row, :], coarse_imag[row, :]
    for at in range(0, columns, LANES):
        real, imag = slice(at, at + LANES), slice(columns + at, columns + at + LANES)
        cr, ci = coarse_r[:, real], coarse_i[:, real]
        fr, fi = fine_real[:, real], fine_imag[:, real]
        high_ref[:, real], low_ref[:, real] = split(cr * fr - ci * fi)
        high_ref[:, imag], low_ref[:, imag] = split(cr * fi + ci * fr)


def width_table(width, columns, length, place):
    factors = [jnp.asarray(factor) for factor in column_factors(width, length)]
    coarse = pl.BlockSpec((8, columns), lambda i, p: (i // 8, p[0]))
    fine = pl.BlockSpec((ROOT, columns), lambda i, p: (0, p[0]))
    out = pl.BlockSpec((ROOT, 2 * columns), lambda i, p: (i, 0))
    return pl.pallas_call(
        table_kernel,
        grid_spec=pltpu.PrefetchScalarGridSpec(
            num_scalar_prefetch=1,
            grid=(width // ROOT,),
            in_specs=[coarse, coarse, fine, fine],
            out_specs=[out, out],
        ),
        out_shape=[jax.ShapeDtypeStruct((width, 2 * columns), jnp.bfloat16)] * 2,
        cost_estimate=SMALL,
        name="width_table",
    )(place.reshape(1), *factors)


def width_kernel(count, *refs):
    blocks = refs[:count]
    table_high, table_low = refs[count : count + 2]
    out_ref, high_ref, low_ref = refs[-3:]

    @pl.when(pl.program_id(0) == 0)
    def _():
        base = 0
        for ref in blocks:
            rows = ref.shape[0]
            high_ref[base : base + rows], low_ref[base : base + rows] = split(ref[...])
            base += rows

    dot = functools.partial(jnp.dot, preferred_element_type=jnp.float32)
    high, low = high_ref[...], low_ref[...]
    weight = table_high[...]
    out_ref[0] = dot(high, weight) + dot(low, weight) + dot(high, table_low[...])


def width_forward(blocks, tables, planes, first, columns, height):
    width = blocks[0].shape[1]
    total = sum(block.shape[0] for block in blocks)
    tiles = columns // TILE
    before = [] if planes is None else [planes]
    table = pl.BlockSpec((width, TILE), lambda n: (0, n))
    return pl.pallas_call(
        functools.partial(width_kernel, len(blocks)),
        grid=(2 * tiles,),
        in_specs=[pl.BlockSpec(block.shape, lambda n: (0, 0)) for block in blocks]
        + [table, table]
        + [pl.BlockSpec(memory_space=pl.ANY)] * len(before),
        out_specs=pl.BlockSpec(
            (1, total, TILE), lambda n: (n // tiles, first // total, n % tiles)
        ),
        out_shape=jax.ShapeDtypeStruct((2, height, columns), jnp.float32),
        scratch_shapes=[pltpu.VMEM((total, width), jnp.bfloat16)] * 2,
        input_output_aliases={len(blocks) + 2: 0} if before else {},
        compiler_params=pltpu.CompilerParams(vmem_limit_bytes=48 << 20),
        cost_estimate=SMALL,
        name="width_forward",
    )(*blocks, *tables, *before)


def back_kernel(count, planes_ref, table_high, table_low, *refs):
    outs = refs[-count - 2 : -2]
    high_ref, low_ref = refs[-2:]
    columns = planes_ref.shape[2]

    @pl.when(pl.program_id(0) == 0)
    def _():
        for part in range(2):
            col = slice(part * columns, (part + 1) * columns)
            high_ref[:, col], low_ref[:, col] = split(planes_ref[part])

    wide = (((1,), (1,)), ((), ()))
    dot = functools.partial(
        lax.dot_general, dimension_numbers=wide, preferred_element_type=jnp.float32
    )
    high, low = high_ref[...], low_ref[...]
    weight = table_high[...]
    image = dot(high, weight) + dot(low, weight) + dot(high, table_low[...])
    base = 0
    for ref in outs:
        rows = ref.shape[0]
        ref[...] = image[base : base + rows]
        base += rows


def width_back(planes, tables, first, sizes, after):
    _, _, columns = planes.shape
    width = tables[0].shape[0]
    total = sum(sizes)
    table = pl.BlockSpec((TILE, 2 * columns), lambda n: (n, 0))
    return pl.pallas_call(
        functools.partial(back_kernel, len(sizes)),
        grid=(width // TILE,),
        in_specs=[
            pl.BlockSpec((2, total, columns), lambda n: (0, first // total, 0)),
            table,
            table,
        ]
        + [pl.BlockSpec(memory_space=pl.ANY)] * len(after),
        out_specs=[pl.BlockSpec((rows, TILE), lambda n: (0, n)) for rows in sizes],
        out_shape=[jax.ShapeDtypeStruct((rows, width), jnp.float32) for rows in sizes],
        scratch_shapes=[pltpu.VMEM((total, 2 * columns), jnp.bfloat16)] * 2,
        compiler_params=pltpu.CompilerParams(vmem_limit_bytes=48 << 20),
        cost_estimate=SMALL,
        name="width_back",
    )(planes, *tables, *after)


def prior_kernel(gram_ref, cube_ref, _, out_ref):
    count, rows, width = cube_ref.shape
    gram = [[gram_ref[c, k] for k in range(count)] for c in range(count)]
    for at in range(0, rows, 8):
        for col in range(0, width, LANES):
            here = slice(at, at + 8), slice(col, col + LANES)
            values = [cube_ref[(k,) + here] for k in range(count)]
            for c in range(count):
                total = gram[c][0] * values[0]
                for k in range(1, count):
                    total = total + gram[c][k] * values[k]
                out_ref[(c,) + here] = total


def prior_term(cube, gram, after):
    count, rows, width = cube.shape
    block = pl.BlockSpec((count, 8, width), lambda i: (0, i, 0))
    return pl.pallas_call(
        prior_kernel,
        grid=(rows // 8,),
        in_specs=[
            pl.BlockSpec(memory_space=pltpu.SMEM),
            block,
            pl.BlockSpec(memory_space=pl.ANY),
        ],
        out_specs=block,
        out_shape=jax.ShapeDtypeStruct(cube.shape, jnp.float32),
        cost_estimate=SMALL,
        name="prior_term",
    )(gram, cube, after)


def moment_kernel(terms, *refs):
    parts = refs[:terms]
    residual_ref, direction_ref = refs[terms : terms + 2]
    applied_ref, moment_ref = refs[-2:]

    @pl.when(pl.program_id(0) == 0)
    def _():
        moment_ref[...] = jnp.zeros_like(moment_ref)

    applied = parts[0][...]
    for ref in parts[1:]:
        applied = applied + ref[...]
    applied_ref[...] = applied
    residual, direction = residual_ref[...], direction_ref[...]
    width = applied.shape[1]

    def fold(product):
        total = product[:8]
        for at in range(8, product.shape[0], 8):
            total = total + product[at : at + 8]
        folded = total[:, :LANES]
        for at in range(LANES, width, LANES):
            folded = folded + total[:, at : at + LANES]
        return folded

    moment_ref[0] += fold(residual * residual)
    moment_ref[1] += fold(direction * applied)
    moment_ref[2] += fold(residual * applied)
    moment_ref[3] += fold(applied * applied)


def moments_of(wide, prior, chunk, residual, direction, applied, first):
    rows, width = chunk.shape
    step = min(64, rows)
    at = first // step
    here = pl.BlockSpec((step, width), lambda i: (at + i, 0))
    chunk_spec = pl.BlockSpec((step, width), lambda i: (i, 0))
    terms = len(wide) + 2
    before = [] if applied is None else [applied]
    return pl.pallas_call(
        functools.partial(moment_kernel, terms),
        grid=(rows // step,),
        in_specs=[here] * len(wide)
        + [here, chunk_spec, here, here]
        + [pl.BlockSpec(memory_space=pl.ANY)] * len(before),
        out_specs=[here, pl.BlockSpec((4, 8, LANES), lambda i: (0, 0, 0))],
        out_shape=[
            jax.ShapeDtypeStruct(residual.shape, jnp.float32),
            jax.ShapeDtypeStruct((4, 8, LANES), jnp.float32),
        ],
        input_output_aliases={terms + 2: 0} if before else {},
        cost_estimate=SMALL,
        name="moments",
    )(*wide, prior, chunk, residual, direction, *before)


def group_sum(axes, sizes, total, out_ref, mine, landed, send_sem, recv_sem):
    slot = 0
    for axis in range(2):
        size = sizes[axis]
        me = lax.axis_index(axes[axis])
        mine[axis] = total
        copies = [
            pltpu.make_async_remote_copy(
                src_ref=mine.at[axis],
                dst_ref=landed.at[slot + hop - 1],
                send_sem=send_sem.at[slot + hop - 1],
                recv_sem=recv_sem.at[slot + hop - 1],
                device_id={axes[axis]: lax.rem(me + hop, size)},
                device_id_type=MESH,
            )
            for hop in range(1, size)
        ]
        for copy in copies:
            copy.start()
        for copy in copies:
            copy.wait()
        total = jnp.zeros_like(total)
        for source in range(size):
            hop = lax.rem(me - source + size, size)
            arrived = landed[slot + jnp.maximum(hop, 1) - 1]
            total = total + jnp.where(hop == 0, mine[axis], arrived)
        slot += size - 1
    sums = jnp.sum(jnp.sum(total, axis=2, keepdims=True), axis=1, keepdims=True)
    out_ref[...] = jnp.broadcast_to(sums, total.shape)


def reduce_kernel(axes, sizes, parts, *refs):
    inputs = refs[:parts]
    out_ref, mine, landed, send_sem, recv_sem = refs[parts:]
    barrier = pltpu.get_barrier_semaphore()
    for axis in range(2):
        me = lax.axis_index(axes[axis])
        for hop in range(1, sizes[axis]):
            peer = lax.rem(me + hop, sizes[axis])
            pl.semaphore_signal(barrier, inc=1, device_id={axes[axis]: peer}, device_id_type=MESH)
    total = inputs[0][...]
    for ref in inputs[1:]:
        total = total + ref[...]
    pl.semaphore_wait(barrier, sizes[0] + sizes[1] - 2)
    group_sum(axes, sizes, total, out_ref, mine, landed, send_sem, recv_sem)


def reduce_moments(moments, axes, sizes):
    shape = moments[0].shape
    slots = sizes[0] + sizes[1] - 2
    return pl.pallas_call(
        functools.partial(reduce_kernel, axes, sizes, len(moments)),
        out_shape=jax.ShapeDtypeStruct(shape, jnp.float32),
        in_specs=[pl.BlockSpec(memory_space=pltpu.VMEM)] * len(moments),
        out_specs=pl.BlockSpec(memory_space=pltpu.VMEM),
        scratch_shapes=[
            pltpu.VMEM((2,) + shape, jnp.float32),
            pltpu.VMEM((slots,) + shape, jnp.float32),
            pltpu.SemaphoreType.DMA((slots,)),
            pltpu.SemaphoreType.DMA((slots,)),
        ],
        compiler_params=pltpu.CompilerParams(collective_id=0, has_side_effects=True),
        cost_estimate=SMALL,
        name="reduce_moments",
    )(*moments)


def gather_kernel(axes, sizes, basis_ref, slot_ref, own_hbm, coarse_real_hbm, coarse_imag_hbm,
                  fine_real_hbm, fine_imag_hbm, planes_hbm, prior_hbm, high_hbm, low_hbm,
                  table_high, table_low, coarse, fine, mine, beside, cross, passed, high_ref,
                  low_ref, result, cube, gram, own_sem, factor_sem, table_sem, result_sem,
                  prior_sem, send_sem, recv_sem, group_send, group_recv):
    height, width = own_hbm.shape
    columns = fine.shape[2]
    unit = high_ref.shape[0]
    chunks = height // FINE
    halves = height // unit
    slots = sizes[0]
    block = height // slots
    place = lax.axis_index("facet")
    me = lax.axis_index("chan")
    sibling = place + 1 - 2 * lax.rem(place, 2)
    partner = lax.rem(place + 2, 4)

    def chunk_rows(c):
        return pl.ds(c * FINE, FINE)

    def half_rows(h):
        return pl.ds(h * unit, unit)

    def block_rows(at):
        return pl.ds(pl.multiple_of(at * block, block), block)

    def remote(source, target, slot, device):
        return pltpu.make_async_remote_copy(
            src_ref=source,
            dst_ref=target,
            send_sem=send_sem.at[slot],
            recv_sem=recv_sem.at[slot],
            device_id={"facet": device},
            device_id_type=MESH,
        )

    crossing = [
        remote(own_hbm.at[chunk_rows(c)], cross.at[c], c, partner) for c in range(chunks)
    ]
    nearby = [
        remote(own_hbm.at[half_rows(h)], beside.at[half_rows(h)], chunks + h, sibling)
        for h in range(halves)
    ]
    passing = [
        remote(cross.at[c], passed.at[c], chunks + halves + c, sibling) for c in range(chunks)
    ]
    regroup = []
    for hop in range(1, slots):
        peer = lax.rem(me + hop, slots)
        regroup.append(
            pltpu.make_async_remote_copy(
                src_ref=own_hbm.at[block_rows(peer)],
                dst_ref=cube.at[me],
                send_sem=group_send.at[hop - 1],
                recv_sem=group_recv.at[hop - 1],
                device_id={"chan": peer},
                device_id_type=MESH,
            )
        )
    kept = pltpu.make_async_copy(own_hbm.at[block_rows(me)], cube.at[me], prior_sem.at[0])
    own_loads = [
        pltpu.make_async_copy(own_hbm.at[half_rows(h)], mine.at[half_rows(h)], own_sem.at[h])
        for h in range(halves)
    ]
    col = pl.ds(pl.multiple_of(place * columns, columns), columns)
    factors = [
        pltpu.make_async_copy(source.at[:, col], target, factor_sem.at[n])
        for n, (source, target) in enumerate(
            (
                (coarse_real_hbm, coarse.at[0]),
                (coarse_imag_hbm, coarse.at[1]),
                (fine_real_hbm, fine.at[0]),
                (fine_imag_hbm, fine.at[1]),
            )
        )
    ]

    barrier = pltpu.get_barrier_semaphore()
    for axis in range(2):
        at = lax.axis_index(axes[axis])
        for hop in range(1, sizes[axis]):
            peer = lax.rem(at + hop, sizes[axis])
            pl.semaphore_signal(barrier, inc=1, device_id={axes[axis]: peer}, device_id_type=MESH)
    for copy in factors + own_loads + [kept]:
        copy.start()
    pl.semaphore_wait(barrier, sizes[0] + sizes[1] - 2)
    for copy in crossing + nearby + regroup:
        copy.start()

    for copy in factors:
        copy.wait()

    def table_rows(j, _):
        rows = pl.ds(pl.multiple_of(j * ROOT, ROOT), ROOT)
        coarse_r, coarse_i = coarse[0, pl.ds(j, 1), :], coarse[1, pl.ds(j, 1), :]
        for at in range(0, columns, LANES):
            real, imag = slice(at, at + LANES), slice(columns + at, columns + at + LANES)
            cr, ci = coarse_r[:, real], coarse_i[:, real]
            fr, fi = fine[0, :, real], fine[1, :, real]
            table_high[rows, real], table_low[rows, real] = split(cr * fr - ci * fi)
            table_high[rows, imag], table_low[rows, imag] = split(cr * fi + ci * fr)
        return 0

    lax.fori_loop(0, width // ROOT, table_rows, 0)
    table_outs = [
        pltpu.make_async_copy(table_high, high_hbm, table_sem.at[0]),
        pltpu.make_async_copy(table_low, low_hbm, table_sem.at[1]),
    ]
    for copy in table_outs:
        copy.start()

    loadings = [
        [basis_ref[slot_ref[c], q] for q in range(basis_ref.shape[1])] for c in range(slots)
    ]
    for c in range(slots):
        for k in range(c + 1):
            total = loadings[c][0] * loadings[k][0]
            for q in range(1, basis_ref.shape[1]):
                total = total + loadings[c][q] * loadings[k][q]
            if c == k:
                total = total + PRIOR_FLOOR
            gram[c, k] = total
            gram[k, c] = total

    outs = []

    def transform(pieces):
        u = len(outs)
        base = 0
        for ref, first, rows in pieces:
            here = slice(base, base + rows)
            high_ref[here], low_ref[here] = split(ref[first : first + rows])
            base += rows
        if u >= 2:
            outs[u - 2].wait()
        dot = functools.partial(jnp.dot, preferred_element_type=jnp.float32)
        for part in range(2):

            def tile(t, _, part=part):
                at = pl.ds(pl.multiple_of(t * TILE, TILE), TILE)
                source = pl.ds(pl.multiple_of(part * columns + t * TILE, TILE), TILE)
                weight = table_high[:, source]
                high = high_ref[...]
                result[u % 2, part, :, at] = (
                    dot(high, weight) + dot(low_ref[...], weight) + dot(high, table_low[:, source])
                )
                return 0

            lax.fori_loop(0, columns // TILE, tile, 0)
        out = pltpu.make_async_copy(
            result.at[u % 2], planes_hbm.at[:, pl.ds(u * unit, unit)], result_sem.at[u % 2]
        )
        out.start()
        outs.append(out)

    def pass_on(c):
        crossing[c].wait_recv()
        passing[c].start()

    def far(c):
        passing[c].wait_recv()
        transform([(cross.at[c], 0, FINE), (passed.at[c], 0, FINE)])

    for h in range(halves):
        own_loads[h].wait()
        transform([(mine, h * unit, unit)])
    pass_on(0)
    for h in range(halves):
        nearby[h].wait_recv()
        transform([(beside, h * unit, unit)])
    for c in range(1, chunks - 1):
        pass_on(c)
        far(c - 1)
    if chunks > 1:
        far(chunks - 2)
        pass_on(chunks - 1)

    kept.wait()
    for copy in regroup:
        copy.wait_recv()
    gram_values = [[gram[c, k] for k in range(slots)] for c in range(slots)]

    def mix(step, _):
        rows = pl.ds(pl.multiple_of(step // (width // LANES) * 8, 8), 8)
        lanes = pl.ds(pl.multiple_of(step % (width // LANES) * LANES, LANES), LANES)
        values = [cube[k, rows, lanes] for k in range(slots)]
        for c in range(slots):
            total = gram_values[c][0] * values[0]
            for k in range(1, slots):
                total = total + gram_values[c][k] * values[k]
            cube[c, rows, lanes] = total
        return 0

    lax.fori_loop(0, block // 8 * (width // LANES), mix, 0, unroll=2)
    prior_out = pltpu.make_async_copy(cube, prior_hbm, prior_sem.at[1])
    prior_out.start()
    far(chunks - 1)

    for copy in crossing + nearby + passing + regroup:
        copy.wait_send()
    for copy in table_outs + outs[-2:] + [prior_out]:
        copy.wait()


def gather(basis, slot_channel, own, columns, length, sizes):
    height, width = own.shape
    factors = [jnp.asarray(factor) for factor in column_factors(width, length)]
    unit = 2 * FINE
    chunks = height // FINE
    halves = height // unit
    flights = 2 * chunks + halves
    block = height // sizes[0]
    anywhere = pl.BlockSpec(memory_space=pl.ANY)
    scalars = pl.BlockSpec(memory_space=pltpu.SMEM)
    table = jax.ShapeDtypeStruct((width, 2 * columns), jnp.bfloat16)
    dma = pltpu.SemaphoreType.DMA
    return pl.pallas_call(
        functools.partial(gather_kernel, ("chan", "facet"), sizes),
        in_specs=[scalars, scalars] + [anywhere] * 5,
        out_specs=[anywhere] * 4,
        out_shape=[
            jax.ShapeDtypeStruct((2, sizes[1] * height, columns), jnp.float32),
            jax.ShapeDtypeStruct((sizes[0], block, width), jnp.float32),
            table,
            table,
        ],
        scratch_shapes=[
            pltpu.VMEM(table.shape, jnp.bfloat16),
            pltpu.VMEM(table.shape, jnp.bfloat16),
            pltpu.VMEM((2, width // ROOT, columns), jnp.float32),
            pltpu.VMEM((2, ROOT, columns), jnp.float32),
            pltpu.VMEM((height, width), jnp.float32),
            pltpu.VMEM((height, width), jnp.float32),
            pltpu.VMEM((chunks, FINE, width), jnp.float32),
            pltpu.VMEM((chunks, FINE, width), jnp.float32),
            pltpu.VMEM((unit, width), jnp.bfloat16),
            pltpu.VMEM((unit, width), jnp.bfloat16),
            pltpu.VMEM((2, 2, unit, columns), jnp.float32),
            pltpu.VMEM((sizes[0], block, width), jnp.float32),
            pltpu.SMEM((sizes[0], sizes[0]), jnp.float32),
            dma((halves,)),
            dma((4,)),
            dma((2,)),
            dma((2,)),
            dma((2,)),
            dma((flights,)),
            dma((flights,)),
            dma((sizes[0] - 1,)),
            dma((sizes[0] - 1,)),
        ],
        compiler_params=pltpu.CompilerParams(
            collective_id=2, has_side_effects=True, vmem_limit_bytes=60 << 20
        ),
        cost_estimate=SMALL,
        name="gather",
    )(basis, slot_channel, own, *factors)


def scatter_kernel(axes, sizes, rows_hbm, high_hbm, low_hbm, prior_hbm, residual_hbm,
                   direction_hbm, applied_hbm, sums_ref, table_high, table_low, held, high_ref,
                   low_ref, part, landed, beside, own, near, cross, prior, stream, moment,
                   mine, got, table_sem, held_sem, stream_sem, out_sem, kept_sem, send_sem,
                   recv_sem, group_send, group_recv, regroup_send, regroup_recv):
    width = table_high.shape[0]
    columns = held.shape[3]
    unit = held.shape[2]
    height = own.shape[0]
    chunks = height // FINE
    tiles = width // TILE
    place = lax.axis_index("facet")
    sibling = place + 1 - 2 * lax.rem(place, 2)
    partner = lax.rem(place + 2, 4)

    def peers(axis):
        me = lax.axis_index(axes[axis])
        return [lax.rem(me + hop, sizes[axis]) for hop in range(1, sizes[axis])]

    def table_copies(t):
        at = pl.ds(pl.multiple_of(t * TILE, TILE), TILE)
        return [
            pltpu.make_async_copy(source.at[at], target.at[at], table_sem.at[n, t])
            for n, (source, target) in enumerate(((high_hbm, table_high), (low_hbm, table_low)))
        ]

    firsts = [2 * height + unit * c for c in range(chunks)]
    firsts += [height + unit * h for h in range(height // unit)]
    firsts += [unit * h for h in range(height // unit)]
    loads = [
        pltpu.make_async_copy(
            rows_hbm.at[:, pl.ds(first, unit)], held.at[u % 2], held_sem.at[u % 2]
        )
        for u, first in enumerate(firsts)
    ]

    barrier = pltpu.get_barrier_semaphore()
    loads[0].start()
    for t in range(tiles):
        for copy in table_copies(t):
            copy.start()
    for axis in range(2):
        for peer in peers(axis):
            pl.semaphore_signal(barrier, inc=1, device_id={axes[axis]: peer}, device_id_type=MESH)

    def image(u, target):
        loads[u].wait()
        if u + 1 < len(loads):
            loads[u + 1].start()
        for part_at in range(2):
            col = slice(part_at * columns, (part_at + 1) * columns)
            high_ref[:, col], low_ref[:, col] = split(held[u % 2, part_at])
        wide = (((1,), (1,)), ((), ()))
        dot = functools.partial(
            lax.dot_general, dimension_numbers=wide, preferred_element_type=jnp.float32
        )

        def tile(t, _):
            if u == 0:
                for copy in table_copies(t):
                    copy.wait()
            at = pl.ds(pl.multiple_of(t * TILE, TILE), TILE)
            weight = table_high[at, :]
            high = high_ref[...]
            target[:, at] = (
                dot(high, weight) + dot(low_ref[...], weight) + dot(high, table_low[at, :])
            )
            return 0

        lax.fori_loop(0, tiles, tile, 0)

    def remote(source, target, slot, device):
        return pltpu.make_async_remote_copy(
            src_ref=source,
            dst_ref=target,
            send_sem=send_sem.at[slot],
            recv_sem=recv_sem.at[slot],
            device_id={"facet": device},
            device_id_type=MESH,
        )

    def chunk_rows(c):
        return pl.ds(c * FINE, FINE)

    paired = [
        remote(part.at[c, pl.ds(FINE, FINE)], landed.at[c], c, sibling) for c in range(chunks)
    ]
    crossing = [
        remote(part.at[c, pl.ds(0, FINE)], cross.at[chunk_rows(c)], chunks + c, partner)
        for c in range(chunks)
    ]
    halves = height // unit
    nearby = [
        remote(
            beside.at[h], near.at[pl.ds(h * unit, unit)], 2 * chunks + h, sibling
        )
        for h in range(halves)
    ]

    def cross_over(c):
        paired[c].wait_recv()

        def add(i, _):
            at = pl.ds(pl.multiple_of(i * 8, 8), 8)
            part[c, at, :] += landed[c, at, :]
            return 0

        lax.fori_loop(0, FINE // 8, add, 0)
        crossing[c].start()

    me = lax.axis_index(axes[0])
    block = height // sizes[0]
    mine_rows = pl.ds(pl.multiple_of(me * block, block), block)
    kept = pltpu.make_async_copy(prior_hbm.at[me], prior.at[mine_rows], kept_sem)
    kept.start()
    regroup = []
    for hop, peer in enumerate(peers(0)):
        regroup.append(
            pltpu.make_async_remote_copy(
                src_ref=prior_hbm.at[peer],
                dst_ref=prior.at[mine_rows],
                send_sem=regroup_send.at[hop],
                recv_sem=regroup_recv.at[hop],
                device_id={axes[0]: peer},
                device_id_type=MESH,
            )
        )
    pl.semaphore_wait(barrier, sizes[0] + sizes[1] - 2)
    for copy in regroup:
        copy.start()

    for c in range(chunks):
        image(c, part.at[c])
        paired[c].start()
        if c:
            cross_over(c - 1)
    for h in range(halves):
        image(chunks + h, beside.at[h])
        if h == 0:
            cross_over(chunks - 1)
        nearby[h].start()
    streams = [
        [
            pltpu.make_async_copy(source.at[chunk_rows(c)], stream.at[n], stream_sem.at[n])
            for n, source in enumerate((residual_hbm, direction_hbm))
        ]
        for c in range(chunks)
    ]
    for copy in streams[0]:
        copy.start()
    for h in range(halves):
        image(chunks + halves + h, own.at[pl.ds(h * unit, unit)])

    moment[...] = jnp.zeros_like(moment)
    for copy in nearby + regroup:
        copy.wait_recv()
    kept.wait()
    outs = []

    def fold(total):
        folded = total[:, :LANES]
        for at in range(LANES, width, LANES):
            folded = folded + total[:, at : at + LANES]
        return folded

    for c in range(chunks):
        for copy in streams[c]:
            copy.wait()
        crossing[c].wait_recv()

        def gather(i, _):
            at = pl.ds(pl.multiple_of(i * 8, 8), 8)
            here = pl.ds(pl.multiple_of(c * FINE + i * 8, 8), 8)
            applied = own[here, :] + near[here, :] + cross[here, :] + prior[here, :]
            own[here, :] = applied
            residual, direction = stream[0, at, :], stream[1, at, :]
            moment[0] += fold(residual * residual)
            moment[1] += fold(direction * applied)
            moment[2] += fold(residual * applied)
            moment[3] += fold(applied * applied)
            return 0

        lax.fori_loop(0, FINE // 8, gather, 0)
        if c + 1 < chunks:
            for copy in streams[c + 1]:
                copy.start()
        out = pltpu.make_async_copy(
            own.at[chunk_rows(c)], applied_hbm.at[chunk_rows(c)], out_sem.at[c]
        )
        out.start()
        outs.append(out)

    group_sum(axes, sizes, moment[...], sums_ref, mine, got, group_send, group_recv)
    for copy in paired + crossing + nearby + regroup:
        copy.wait_send()
    for out in outs:
        out.wait()


def scatter(rows, tables, prior, residual, direction, sizes):
    height, width = direction.shape
    columns = rows.shape[2]
    unit = 2 * FINE
    chunks = height // FINE
    hops = sizes[0] + sizes[1] - 2
    flights = 2 * chunks + height // unit
    anywhere = pl.BlockSpec(memory_space=pl.ANY)
    shape = (4, 8, LANES)
    whole = pltpu.VMEM((height, width), jnp.float32)
    dma = pltpu.SemaphoreType.DMA
    return pl.pallas_call(
        functools.partial(scatter_kernel, ("chan", "facet"), sizes),
        in_specs=[anywhere] * 6,
        out_specs=[anywhere, pl.BlockSpec(memory_space=pltpu.VMEM)],
        out_shape=[
            jax.ShapeDtypeStruct((height, width), jnp.float32),
            jax.ShapeDtypeStruct(shape, jnp.float32),
        ],
        scratch_shapes=[
            pltpu.VMEM((width, 2 * columns), jnp.bfloat16),
            pltpu.VMEM((width, 2 * columns), jnp.bfloat16),
            pltpu.VMEM((2, 2, unit, columns), jnp.float32),
            pltpu.VMEM((unit, 2 * columns), jnp.bfloat16),
            pltpu.VMEM((unit, 2 * columns), jnp.bfloat16),
            pltpu.VMEM((chunks, unit, width), jnp.float32),
            pltpu.VMEM((chunks, FINE, width), jnp.float32),
            pltpu.VMEM((height // unit, unit, width), jnp.float32),
            whole,
            whole,
            whole,
            whole,
            pltpu.VMEM((2, FINE, width), jnp.float32),
            pltpu.VMEM(shape, jnp.float32),
            pltpu.VMEM((2,) + shape, jnp.float32),
            pltpu.VMEM((hops,) + shape, jnp.float32),
            dma((2, width // TILE)),
            dma((2,)),
            dma((2,)),
            dma((chunks,)),
            dma,
            dma((flights,)),
            dma((flights,)),
            dma((hops,)),
            dma((hops,)),
            dma((sizes[0] - 1,)),
            dma((sizes[0] - 1,)),
        ],
        compiler_params=pltpu.CompilerParams(
            collective_id=1, has_side_effects=True, vmem_limit_bytes=60 << 20
        ),
        cost_estimate=SMALL,
        name="scatter",
    )(rows, *tables, prior, residual, direction)


def update_kernel(
    sum_ref, solution_ref, residual_ref, direction_ref, applied_ref, x_ref, r_ref, d_ref
):
    def scalar(at):
        return sum_ref[at, 0:1, 0:1]

    norm_now, curvature, cross, square = [scalar(at) for at in range(4)]
    step_size = norm_now / curvature
    norm_next = norm_now - 2.0 * step_size * cross + step_size * step_size * square
    ratio = norm_next / norm_now
    direction = direction_ref[...]
    x_ref[...] = solution_ref[...] + step_size * direction
    residual = residual_ref[...] - step_size * applied_ref[...]
    r_ref[...] = residual
    d_ref[...] = residual + ratio * direction


def update(sums, solution, residual, direction, applied):
    height, width = applied.shape
    step = 64
    block = pl.BlockSpec((step, width), lambda i: (i, 0))
    return pl.pallas_call(
        update_kernel,
        grid=(height // step,),
        in_specs=[pl.BlockSpec(sums.shape, lambda i: (0, 0, 0))] + [block] * 4,
        out_specs=[block] * 3,
        out_shape=[jax.ShapeDtypeStruct((height, width), jnp.float32)] * 3,
        cost_estimate=SMALL,
        name="update",
    )(sums, solution, residual, direction, applied)


def swap_pairs(array, count, bit):
    pairs = [(place, place ^ bit) for place in range(count)]
    return lax.ppermute(array, "facet", pairs)


def body(solution, residual, direction, spectra, basis, slot_channel):
    channel_count = basis.shape[0]
    length = RADIX * FINE
    facets = lax.axis_size("facet")
    place = lax.axis_index("facet")
    height, width = direction.shape[1:]
    columns = spectra.shape[2]
    own = direction[0]
    top = facets // 2
    per_facet = height // FINE
    barrier = lax.optimization_barrier

    groups = []
    if per_facet > 1:
        groups += [[(key, s) for s in range(per_facet)] for key in range(top)]
    else:
        groups.append([(key, 0) for key in range(top)])
    groups += [[(key, s) for key in range(top, facets)] for s in range(per_facet)]
    starts = np.cumsum([0] + [len(entries) * FINE for entries in groups])
    slot_of = np.zeros((facets, per_facet), np.int32)
    for at, (key, s) in enumerate(entry for entries in groups for entry in entries):
        slot_of[key, s] = at
    slots = jnp.asarray(slot_of)[jnp.arange(facets, dtype=jnp.int32) ^ place].reshape(-1)

    sizes = (lax.axis_size("chan"), facets)
    if facets == 4 and per_facet % 2 == 0 and height % (8 * sizes[0]) == 0:
        planes, local, *tables = gather(basis, slot_channel, own, columns, length, sizes)
        rows = row_pass(planes, spectra[0], slots)
        applied, sums = scatter(rows, tables, local, residual[0], own, sizes)
        results = update(sums, solution[0], residual[0], own, applied)
        return tuple(result[None] for result in results)

    chunks = [own[at * FINE : (at + 1) * FINE] for at in range(per_facet)]
    crossed = [swap_pairs(chunk, facets, top) for chunk in chunks]

    def spread(block, key):
        blocks = {key: block}
        bit = top // 2
        while bit:
            blocks.update({k ^ bit: swap_pairs(blocks[k], facets, bit) for k in list(blocks)})
            bit //= 2
        return blocks

    near = spread(own, 0)

    cube = own.reshape(channel_count, height // channel_count, width)
    regrouped = lax.all_to_all(cube, "chan", split_axis=0, concat_axis=0, tiled=True)
    one_hot = (
        slot_channel[:, None] == jnp.arange(channel_count, dtype=jnp.int32)[None, :]
    ).astype(jnp.float32)
    loadings = jnp.dot(one_hot, basis, precision=HIGHEST)
    gram = jnp.einsum("cq,dq->cd", loadings, loadings, precision=HIGHEST)
    gram = gram + PRIOR_FLOOR * jnp.eye(channel_count, dtype=jnp.float32)

    tables = width_table(width, columns, length, place)
    planes = None
    far = {}
    for step, entries in enumerate(groups):
        if entries[0][0] >= top:
            blocks = [far[s][key] for key, s in entries]
        elif per_facet > 1:
            blocks = [near[entries[0][0]]]
        else:
            blocks = [near[key] for key, _ in entries]
        planes = width_forward(
            blocks, tables, planes, int(starts[step]), columns, facets * height
        )
        if step < per_facet:
            block, planes = barrier((crossed[step], planes))
            far[step] = spread(block, top)
        if step == len(groups) - 2:
            local = prior_term(regrouped, gram, planes)
            local, planes = barrier((local, planes))
            prior = lax.all_to_all(local, "chan", split_axis=0, concat_axis=0, tiled=True)
            prior = prior.reshape(height, width)

    rows = row_pass(planes, spectra[0], slots)

    arrived = {}
    near_sums = {}
    held = [rows]
    previous = None
    sequence = [at for at in range(len(groups)) if groups[at][0][0] >= top]
    sequence += [at for at in range(len(groups)) if groups[at][0][0] < top][::-1]

    def send(entries, parts):
        sums = {key: part for (key, _), part in zip(entries, parts)}
        bit = 1
        while bit < top:
            sums = {
                key: sums[key] + swap_pairs(sums[key | bit], facets, bit)
                for key in sorted(sums, reverse=True)
                if not key & bit
            }
            bit *= 2
        arrived[entries[0][1]] = swap_pairs(sums[top], facets, top)
        return sums[top]

    for turn_at, at in enumerate(sequence):
        entries = groups[at]
        far_rows = entries[0][0] >= top
        counts = [FINE] * len(entries) if far_rows or per_facet == 1 else [height]
        parts = width_back(rows, tables, int(starts[at]), counts, held)
        held = [parts[0]]
        if previous is not None:
            held.append(send(*previous))
            previous = None
        if turn_at >= 3 and turn_at - 3 < per_facet:
            held.append(arrived[groups[sequence[turn_at - 3]][0][1]])
        if far_rows:
            previous = (entries, parts)
        else:
            near_sums.update({key: part for (key, _), part in zip(entries, parts)})
    bit = 1
    while 2 * bit < top:
        near_sums = {
            key: near_sums[key] + swap_pairs(near_sums[key | bit], facets, bit)
            for key in sorted(near_sums, reverse=True)
            if not key & bit
        }
        bit *= 2
    wide = [near_sums[0], swap_pairs(near_sums[bit], facets, bit)]

    applied = None
    moments = []
    for s in range(per_facet):
        first = s * FINE
        applied, moment = moments_of(
            wide, prior, arrived[s], residual[0], own, applied, first
        )
        moments.append(moment)
    sums = reduce_moments(moments, ("chan", "facet"), sizes)
    results = update(sums, solution[0], residual[0], own, applied)
    return tuple(result[None] for result in results)


def solution(mesh):
    return jax.shard_map(
        body,
        mesh=mesh,
        in_specs=(
            P("chan", "facet", None),
            P("chan", "facet", None),
            P("chan", "facet", None),
            P("chan", None, "facet"),
            P(),
            P(),
        ),
        out_specs=(P("chan", "facet", None), P("chan", "facet", None), P("chan", "facet", None)),
        check_vma=False,
    )
```

```python
import functools
import math

import jax
import jax.numpy as jnp
import ml_dtypes
import numpy as np
from jax import lax
from jax.experimental import pallas as pl
from jax.experimental.pallas import tpu as pltpu
from jax.sharding import PartitionSpec as P

RADIX = 32
FINE = 128
ROOT = 64
LANES = 128
TILE = 256
HIGHEST = lax.Precision.HIGHEST
PRIOR_FLOOR = 0.25
HALF = math.sqrt(0.5)
MESH = pl.DeviceIdType.MESH
SMALL = pl.CostEstimate(flops=1, bytes_accessed=1, transcendentals=0)


def np_split(table):
    high = table.astype(ml_dtypes.bfloat16)
    low = (table - high.astype(np.float64)).astype(ml_dtypes.bfloat16)
    return high, low


@functools.cache
def row_tables():
    length = RADIX * FINE
    coarse = np.arange(RADIX)[:, None, None]
    fine = np.arange(FINE)[None, :, None]
    place = np.arange(FINE)[None, None, :]
    angle = -2.0 * np.pi * ((place * (RADIX * fine + coarse)) % length) / length
    real, imag = np.cos(angle), np.sin(angle)
    forward = np.concatenate(
        [np.concatenate([real, -imag], axis=2), np.concatenate([imag, real], axis=2)], axis=1
    )
    inverse = np.transpose(forward, (0, 2, 1)) / float(length * length)
    return np_split(forward) + np_split(inverse)


@functools.cache
def column_factors(width, length):
    column = np.arange(length)[None, :]

    def wave(rows):
        angle = -2.0 * np.pi * ((rows[:, None] * column) % length) / length
        return np.cos(angle).astype(np.float32), np.sin(angle).astype(np.float32)

    return wave(np.arange(width // ROOT) * ROOT) + wave(np.arange(ROOT))


def split(values):
    high = values.astype(jnp.bfloat16)
    low = (values - high.astype(jnp.float32)).astype(jnp.bfloat16)
    return high, low


def turn(real, imag, num, den, sign):
    num %= den
    if (num * 8) % den == 0:
        eighth = (sign * (num * 8 // den)) % 8
        if eighth == 0:
            return real, imag
        if eighth == 1:
            return (real - imag) * HALF, (real + imag) * HALF
        if eighth == 2:
            return -imag, real
        if eighth == 3:
            return (real + imag) * -HALF, (real - imag) * HALF
        if eighth == 4:
            return -real, -imag
        if eighth == 5:
            return (imag - real) * HALF, (real + imag) * -HALF
        if eighth == 6:
            return imag, -real
        return (real + imag) * HALF, (imag - real) * HALF
    c = math.cos(2.0 * math.pi * num / den)
    s = sign * math.sin(2.0 * math.pi * num / den)
    return real * c - imag * s, real * s + imag * c


def fft(points, sign):
    count = len(points)
    if count == 1:
        return points
    half = count // 2
    even, odd = [], []
    for i in range(half):
        (ar, ai), (br, bi) = points[i], points[i + half]
        even.append((ar + br, ai + bi))
        if 4 * i == count:
            odd.append((ai - bi, br - ar) if sign < 0 else (bi - ai, ar - br))
        else:
            odd.append(turn(ar - br, ai - bi, i, count, sign))
    result = [None] * count
    result[0::2] = fft(even, sign)
    result[1::2] = fft(odd, sign)
    return result


def dot3(table_high, table_low, values):
    high, low = split(values)
    dot = functools.partial(jnp.dot, preferred_element_type=jnp.float32)
    return dot(table_high, high) + dot(table_low, high) + dot(table_high, low)


def row_kernel(slot_ref, planes_ref, weight_ref, *refs):
    table_hbm, (out_ref, work_a, work_b, *tables, table_sem) = refs[:4], refs[4:]
    forward_high, forward_low, inverse_high, inverse_low = tables
    used = RADIX // 2
    slots = [slot_ref[a] * FINE for a in range(used)]
    tile = pl.program_id(0)
    last = pl.num_programs(0) - 1
    copies = [
        pltpu.make_async_copy(source, target, table_sem.at[n])
        for n, (source, target) in enumerate(zip(table_hbm, tables))
    ]

    def rows(base, at):
        return pl.ds(pl.multiple_of(base + at, 8), 8)

    def position(step):
        lanes = pl.ds(pl.multiple_of(step // (FINE // 8) * LANES, LANES), LANES)
        return lax.rem(step, FINE // 8) * 8, lanes

    def forward(step, outer, inner):
        at, col = position(step)
        points = [(planes_ref[0, rows(s, at), col], planes_ref[1, rows(s, at), col]) for s in slots]
        for k, (real, imag) in enumerate(fft(points, -1)):
            outer[2 * k, rows(0, at), col] = real
            outer[2 * k, rows(FINE, at), col] = imag
        points = [turn(*point, a, RADIX, -1) for a, point in enumerate(points)]
        for k, (real, imag) in enumerate(fft(points, -1)):
            outer[2 * k + 1, rows(0, at), col] = real
            outer[2 * k + 1, rows(FINE, at), col] = imag

    def middle(k, outer, inner):
        freqs = dot3(forward_high[k], forward_low[k], inner[k])
        weight = weight_ref[k]
        freqs = freqs * jnp.concatenate([weight, weight], axis=0)
        inner[k] = dot3(inverse_high[k], inverse_low[k], freqs)

    def inverse(step, outer, inner):
        at, col = position(step)

        def side(odd):
            points = [
                (outer[2 * k + odd, rows(0, at), col], outer[2 * k + odd, rows(FINE, at), col])
                for k in range(used)
            ]
            return fft(points, 1)

        even, odd = side(0), side(1)
        for a, s in enumerate(slots):
            real, imag = turn(*odd[a], a, RADIX, 1)
            out_ref[0, rows(s, at), col] = even[a][0] + real
            out_ref[1, rows(s, at), col] = even[a][1] + imag

    def loop(parts, outer, inner, unroll=1):
        def run(step, _):
            for part in parts:
                part(step, outer, inner)
            return 0

        lax.fori_loop(0, RADIX, run, 0, unroll=unroll)

    @pl.when(tile == 0)
    def _():
        for copy in copies:
            copy.start()
        loop([forward], work_a, work_b)
        for copy in copies:
            copy.wait()

    for parity in range(2):
        outer, inner = (work_a, work_b) if parity == 0 else (work_b, work_a)
        mine = lax.rem(tile, 2) == parity

        @pl.when(mine & (tile > 0) & (tile < last))
        def _(outer=outer, inner=inner):
            loop([middle, inverse, forward], outer, inner, unroll=16)

        @pl.when(mine & (tile == last))
        def _(outer=outer, inner=inner):
            loop([inverse], outer, inner)


def row_pass(planes, weight, slots):
    _, height, columns = planes.shape
    tables = [jnp.asarray(table) for table in row_tables()]
    count = columns // TILE
    block = (2, height, TILE)
    return pl.pallas_call(
        row_kernel,
        grid_spec=pltpu.PrefetchScalarGridSpec(
            num_scalar_prefetch=1,
            grid=(count + 2,),
            in_specs=[
                pl.BlockSpec(block, lambda i, s: (0, 0, jnp.minimum(i, count - 1))),
                pl.BlockSpec(
                    (RADIX, FINE, TILE), lambda i, s: (0, 0, jnp.clip(i - 1, 0, count - 1))
                ),
            ]
            + [pl.BlockSpec(memory_space=pl.ANY)] * 4,
            out_specs=pl.BlockSpec(block, lambda i, s: (0, 0, jnp.maximum(i - 2, 0))),
            scratch_shapes=[pltpu.VMEM((RADIX, 2 * FINE, TILE), jnp.float32)] * 2
            + [pltpu.VMEM((RADIX, 2 * FINE, 2 * FINE), jnp.bfloat16)] * 4
            + [pltpu.SemaphoreType.DMA((4,))],
        ),
        out_shape=jax.ShapeDtypeStruct(planes.shape, jnp.float32),
        compiler_params=pltpu.CompilerParams(vmem_limit_bytes=62 << 20),
        cost_estimate=SMALL,
        name="row_pass",
    )(slots, planes, weight, *tables)


def table_kernel(place_ref, coarse_real, coarse_imag, fine_real, fine_imag, high_ref, low_ref):
    columns = fine_real.shape[1]
    row = pl.ds(pl.program_id(0) % 8, 1)
    coarse_r, coarse_i = coarse_real[row, :], coarse_imag[row, :]
    for at in range(0, columns, LANES):
        real, imag = slice(at, at + LANES), slice(columns + at, columns + at + LANES)
        cr, ci = coarse_r[:, real], coarse_i[:, real]
        fr, fi = fine_real[:, real], fine_imag[:, real]
        high_ref[:, real], low_ref[:, real] = split(cr * fr - ci * fi)
        high_ref[:, imag], low_ref[:, imag] = split(cr * fi + ci * fr)


def width_table(width, columns, length, place):
    factors = [jnp.asarray(factor) for factor in column_factors(width, length)]
    coarse = pl.BlockSpec((8, columns), lambda i, p: (i // 8, p[0]))
    fine = pl.BlockSpec((ROOT, columns), lambda i, p: (0, p[0]))
    out = pl.BlockSpec((ROOT, 2 * columns), lambda i, p: (i, 0))
    return pl.pallas_call(
        table_kernel,
        grid_spec=pltpu.PrefetchScalarGridSpec(
            num_scalar_prefetch=1,
            grid=(width // ROOT,),
            in_specs=[coarse, coarse, fine, fine],
            out_specs=[out, out],
        ),
        out_shape=[jax.ShapeDtypeStruct((width, 2 * columns), jnp.bfloat16)] * 2,
        cost_estimate=SMALL,
        name="width_table",
    )(place.reshape(1), *factors)


def width_kernel(count, *refs):
    blocks = refs[:count]
    table_high, table_low = refs[count : count + 2]
    out_ref, high_ref, low_ref = refs[-3:]

    @pl.when(pl.program_id(0) == 0)
    def _():
        base = 0
        for ref in blocks:
            rows = ref.shape[0]
            high_ref[base : base + rows], low_ref[base : base + rows] = split(ref[...])
            base += rows

    dot = functools.partial(jnp.dot, preferred_element_type=jnp.float32)
    high, low = high_ref[...], low_ref[...]
    weight = table_high[...]
    out_ref[0] = dot(high, weight) + dot(low, weight) + dot(high, table_low[...])


def width_forward(blocks, tables, planes, first, columns, height):
    width = blocks[0].shape[1]
    total = sum(block.shape[0] for block in blocks)
    tiles = columns // TILE
    before = [] if planes is None else [planes]
    table = pl.BlockSpec((width, TILE), lambda n: (0, n))
    return pl.pallas_call(
        functools.partial(width_kernel, len(blocks)),
        grid=(2 * tiles,),
        in_specs=[pl.BlockSpec(block.shape, lambda n: (0, 0)) for block in blocks]
        + [table, table]
        + [pl.BlockSpec(memory_space=pl.ANY)] * len(before),
        out_specs=pl.BlockSpec(
            (1, total, TILE), lambda n: (n // tiles, first // total, n % tiles)
        ),
        out_shape=jax.ShapeDtypeStruct((2, height, columns), jnp.float32),
        scratch_shapes=[pltpu.VMEM((total, width), jnp.bfloat16)] * 2,
        input_output_aliases={len(blocks) + 2: 0} if before else {},
        compiler_params=pltpu.CompilerParams(vmem_limit_bytes=48 << 20),
        cost_estimate=SMALL,
        name="width_forward",
    )(*blocks, *tables, *before)


def back_kernel(count, planes_ref, table_high, table_low, *refs):
    outs = refs[-count - 2 : -2]
    high_ref, low_ref = refs[-2:]
    columns = planes_ref.shape[2]

    @pl.when(pl.program_id(0) == 0)
    def _():
        for part in range(2):
            col = slice(part * columns, (part + 1) * columns)
            high_ref[:, col], low_ref[:, col] = split(planes_ref[part])

    wide = (((1,), (1,)), ((), ()))
    dot = functools.partial(
        lax.dot_general, dimension_numbers=wide, preferred_element_type=jnp.float32
    )
    high, low = high_ref[...], low_ref[...]
    weight = table_high[...]
    image = dot(high, weight) + dot(low, weight) + dot(high, table_low[...])
    base = 0
    for ref in outs:
        rows = ref.shape[0]
        ref[...] = image[base : base + rows]
        base += rows


def width_back(planes, tables, first, sizes, after):
    _, _, columns = planes.shape
    width = tables[0].shape[0]
    total = sum(sizes)
    table = pl.BlockSpec((TILE, 2 * columns), lambda n: (n, 0))
    return pl.pallas_call(
        functools.partial(back_kernel, len(sizes)),
        grid=(width // TILE,),
        in_specs=[
            pl.BlockSpec((2, total, columns), lambda n: (0, first // total, 0)),
            table,
            table,
        ]
        + [pl.BlockSpec(memory_space=pl.ANY)] * len(after),
        out_specs=[pl.BlockSpec((rows, TILE), lambda n: (0, n)) for rows in sizes],
        out_shape=[jax.ShapeDtypeStruct((rows, width), jnp.float32) for rows in sizes],
        scratch_shapes=[pltpu.VMEM((total, 2 * columns), jnp.bfloat16)] * 2,
        compiler_params=pltpu.CompilerParams(vmem_limit_bytes=48 << 20),
        cost_estimate=SMALL,
        name="width_back",
    )(planes, *tables, *after)


def prior_kernel(gram_ref, cube_ref, _, out_ref):
    count, rows, width = cube_ref.shape
    gram = [[gram_ref[c, k] for k in range(count)] for c in range(count)]
    for at in range(0, rows, 8):
        for col in range(0, width, LANES):
            here = slice(at, at + 8), slice(col, col + LANES)
            values = [cube_ref[(k,) + here] for k in range(count)]
            for c in range(count):
                total = gram[c][0] * values[0]
                for k in range(1, count):
                    total = total + gram[c][k] * values[k]
                out_ref[(c,) + here] = total


def prior_term(cube, gram, after):
    count, rows, width = cube.shape
    block = pl.BlockSpec((count, 8, width), lambda i: (0, i, 0))
    return pl.pallas_call(
        prior_kernel,
        grid=(rows // 8,),
        in_specs=[
            pl.BlockSpec(memory_space=pltpu.SMEM),
            block,
            pl.BlockSpec(memory_space=pl.ANY),
        ],
        out_specs=block,
        out_shape=jax.ShapeDtypeStruct(cube.shape, jnp.float32),
        cost_estimate=SMALL,
        name="prior_term",
    )(gram, cube, after)


def moment_kernel(terms, *refs):
    parts = refs[:terms]
    residual_ref, direction_ref = refs[terms : terms + 2]
    applied_ref, moment_ref = refs[-2:]

    @pl.when(pl.program_id(0) == 0)
    def _():
        moment_ref[...] = jnp.zeros_like(moment_ref)

    applied = parts[0][...]
    for ref in parts[1:]:
        applied = applied + ref[...]
    applied_ref[...] = applied
    residual, direction = residual_ref[...], direction_ref[...]
    width = applied.shape[1]

    def fold(product):
        total = product[:8]
        for at in range(8, product.shape[0], 8):
            total = total + product[at : at + 8]
        folded = total[:, :LANES]
        for at in range(LANES, width, LANES):
            folded = folded + total[:, at : at + LANES]
        return folded

    moment_ref[0] += fold(residual * residual)
    moment_ref[1] += fold(direction * applied)
    moment_ref[2] += fold(residual * applied)
    moment_ref[3] += fold(applied * applied)


def moments_of(wide, prior, chunk, residual, direction, applied, first):
    rows, width = chunk.shape
    step = min(64, rows)
    at = first // step
    here = pl.BlockSpec((step, width), lambda i: (at + i, 0))
    chunk_spec = pl.BlockSpec((step, width), lambda i: (i, 0))
    terms = len(wide) + 2
    before = [] if applied is None else [applied]
    return pl.pallas_call(
        functools.partial(moment_kernel, terms),
        grid=(rows // step,),
        in_specs=[here] * len(wide)
        + [here, chunk_spec, here, here]
        + [pl.BlockSpec(memory_space=pl.ANY)] * len(before),
        out_specs=[here, pl.BlockSpec((4, 8, LANES), lambda i: (0, 0, 0))],
        out_shape=[
            jax.ShapeDtypeStruct(residual.shape, jnp.float32),
            jax.ShapeDtypeStruct((4, 8, LANES), jnp.float32),
        ],
        input_output_aliases={terms + 2: 0} if before else {},
        cost_estimate=SMALL,
        name="moments",
    )(*wide, prior, chunk, residual, direction, *before)


def group_sum(axes, sizes, total, out_ref, mine, landed, send_sem, recv_sem):
    slot = 0
    for axis in range(2):
        size = sizes[axis]
        me = lax.axis_index(axes[axis])
        mine[axis] = total
        copies = [
            pltpu.make_async_remote_copy(
                src_ref=mine.at[axis],
                dst_ref=landed.at[slot + hop - 1],
                send_sem=send_sem.at[slot + hop - 1],
                recv_sem=recv_sem.at[slot + hop - 1],
                device_id={axes[axis]: lax.rem(me + hop, size)},
                device_id_type=MESH,
            )
            for hop in range(1, size)
        ]
        for copy in copies:
            copy.start()
        for copy in copies:
            copy.wait()
        total = jnp.zeros_like(total)
        for source in range(size):
            hop = lax.rem(me - source + size, size)
            arrived = landed[slot + jnp.maximum(hop, 1) - 1]
            total = total + jnp.where(hop == 0, mine[axis], arrived)
        slot += size - 1
    sums = jnp.sum(jnp.sum(total, axis=2, keepdims=True), axis=1, keepdims=True)
    out_ref[...] = jnp.broadcast_to(sums, total.shape)


def reduce_kernel(axes, sizes, parts, *refs):
    inputs = refs[:parts]
    out_ref, mine, landed, send_sem, recv_sem = refs[parts:]
    barrier = pltpu.get_barrier_semaphore()
    for axis in range(2):
        me = lax.axis_index(axes[axis])
        for hop in range(1, sizes[axis]):
            peer = lax.rem(me + hop, sizes[axis])
            pl.semaphore_signal(barrier, inc=1, device_id={axes[axis]: peer}, device_id_type=MESH)
    total = inputs[0][...]
    for ref in inputs[1:]:
        total = total + ref[...]
    pl.semaphore_wait(barrier, sizes[0] + sizes[1] - 2)
    group_sum(axes, sizes, total, out_ref, mine, landed, send_sem, recv_sem)


def reduce_moments(moments, axes, sizes):
    shape = moments[0].shape
    slots = sizes[0] + sizes[1] - 2
    return pl.pallas_call(
        functools.partial(reduce_kernel, axes, sizes, len(moments)),
        out_shape=jax.ShapeDtypeStruct(shape, jnp.float32),
        in_specs=[pl.BlockSpec(memory_space=pltpu.VMEM)] * len(moments),
        out_specs=pl.BlockSpec(memory_space=pltpu.VMEM),
        scratch_shapes=[
            pltpu.VMEM((2,) + shape, jnp.float32),
            pltpu.VMEM((slots,) + shape, jnp.float32),
            pltpu.SemaphoreType.DMA((slots,)),
            pltpu.SemaphoreType.DMA((slots,)),
        ],
        compiler_params=pltpu.CompilerParams(collective_id=0, has_side_effects=True),
        cost_estimate=SMALL,
        name="reduce_moments",
    )(*moments)


def far_pieces(slabs, small_first):
    pieces = []
    for slab in range(slabs):
        halved = slab == slabs - 1 or (small_first and slab == 0)
        size = FINE // 2 if halved else FINE
        pieces += [(slab, first, size) for first in range(0, FINE, size)]
    return pieces


def gather_kernel(axes, sizes, basis_ref, slot_ref, own_hbm, spectrum_hbm, coarse_real_hbm,
                  coarse_imag_hbm, fine_real_hbm, fine_imag_hbm, planes_hbm, prior_hbm, high_hbm,
                  low_hbm, weight_hbm,
                  table_high, table_low, coarse, fine, mine, beside, cross, passed, high_ref,
                  low_ref, result, cube, strip, sorted_strip,
                  gram, strip_sem, sorted_sem, own_sem, factor_sem, table_sem, result_sem,
                  prior_sem, send_sem, recv_sem, group_send, group_recv):
    height, width = own_hbm.shape
    columns = fine.shape[2]
    unit = high_ref.shape[0]
    chunks = height // FINE
    halves = height // unit
    slots = sizes[0]
    block = height // slots
    place = lax.axis_index("facet")
    me = lax.axis_index("chan")
    sibling = place + 1 - 2 * lax.rem(place, 2)
    partner = lax.rem(place + 2, 4)

    def half_rows(h):
        return pl.ds(h * unit, unit)

    def block_rows(at):
        return pl.ds(pl.multiple_of(at * block, block), block)

    def remote(source, target, slot, device):
        return pltpu.make_async_remote_copy(
            src_ref=source,
            dst_ref=target,
            send_sem=send_sem.at[slot],
            recv_sem=recv_sem.at[slot],
            device_id={"facet": device},
            device_id_type=MESH,
        )

    pieces = far_pieces(chunks, False)
    count = len(pieces)
    crossing = [
        remote(
            own_hbm.at[pl.ds(c * FINE + first, size)],
            cross.at[c, pl.ds(first, size)],
            n,
            partner,
        )
        for n, (c, first, size) in enumerate(pieces)
    ]
    passing = [
        remote(
            cross.at[c, pl.ds(first, size)],
            passed.at[c, pl.ds(first, size)],
            count + n,
            sibling,
        )
        for n, (c, first, size) in enumerate(pieces)
    ]
    nearby = [
        remote(own_hbm.at[half_rows(h)], beside.at[half_rows(h)], 2 * count + h, sibling)
        for h in range(halves)
    ]
    strips = columns // LANES

    def strip_lanes(n):
        return pl.ds(n * LANES, LANES)

    strip_loads = [
        pltpu.make_async_copy(
            spectrum_hbm.at[:, strip_lanes(n)], strip.at[n % 2], strip_sem.at[n % 2]
        )
        for n in range(strips)
    ]
    strip_outs = [
        pltpu.make_async_copy(
            sorted_strip.at[n % 2], weight_hbm.at[:, :, strip_lanes(n)], sorted_sem.at[n % 2]
        )
        for n in range(strips)
    ]
    regroup = []
    for hop in range(1, slots):
        peer = lax.rem(me + hop, slots)
        regroup.append(
            pltpu.make_async_remote_copy(
                src_ref=own_hbm.at[block_rows(peer)],
                dst_ref=cube.at[me],
                send_sem=group_send.at[hop - 1],
                recv_sem=group_recv.at[hop - 1],
                device_id={"chan": peer},
                device_id_type=MESH,
            )
        )
    kept = pltpu.make_async_copy(own_hbm.at[block_rows(me)], cube.at[me], prior_sem.at[0])
    own_loads = [
        pltpu.make_async_copy(own_hbm.at[half_rows(h)], mine.at[half_rows(h)], own_sem.at[h])
        for h in range(halves)
    ]
    col = pl.ds(pl.multiple_of(place * columns, columns), columns)
    factors = [
        pltpu.make_async_copy(source.at[:, col], target, factor_sem.at[n])
        for n, (source, target) in enumerate(
            (
                (coarse_real_hbm, coarse.at[0]),
                (coarse_imag_hbm, coarse.at[1]),
                (fine_real_hbm, fine.at[0]),
                (fine_imag_hbm, fine.at[1]),
            )
        )
    ]

    barrier = pltpu.get_barrier_semaphore()
    for axis in range(2):
        at = lax.axis_index(axes[axis])
        for hop in range(1, sizes[axis]):
            peer = lax.rem(at + hop, sizes[axis])
            pl.semaphore_signal(barrier, inc=1, device_id={axes[axis]: peer}, device_id_type=MESH)
    for copy in factors + own_loads + [kept]:
        copy.start()
    pl.semaphore_wait(barrier, sizes[0] + sizes[1] - 2)
    for copy in crossing + nearby + regroup:
        copy.start()

    for copy in factors:
        copy.wait()

    def table_rows(j, _):
        rows = pl.ds(pl.multiple_of(j * ROOT, ROOT), ROOT)
        coarse_r, coarse_i = coarse[0, pl.ds(j, 1), :], coarse[1, pl.ds(j, 1), :]
        for at in range(0, columns, LANES):
            real, imag = slice(at, at + LANES), slice(columns + at, columns + at + LANES)
            cr, ci = coarse_r[:, real], coarse_i[:, real]
            fr, fi = fine[0, :, real], fine[1, :, real]
            table_high[rows, real], table_low[rows, real] = split(cr * fr - ci * fi)
            table_high[rows, imag], table_low[rows, imag] = split(cr * fi + ci * fr)
        return 0

    lax.fori_loop(0, width // ROOT, table_rows, 0)
    table_outs = [
        pltpu.make_async_copy(table_high, high_hbm, table_sem.at[0]),
        pltpu.make_async_copy(table_low, low_hbm, table_sem.at[1]),
    ]
    for copy in table_outs:
        copy.start()

    loadings = [
        [basis_ref[slot_ref[c], q] for q in range(basis_ref.shape[1])] for c in range(slots)
    ]
    for c in range(slots):
        for k in range(c + 1):
            total = loadings[c][0] * loadings[k][0]
            for q in range(1, basis_ref.shape[1]):
                total = total + loadings[c][q] * loadings[k][q]
            if c == k:
                total = total + PRIOR_FLOOR
            gram[c, k] = total
            gram[k, c] = total

    def sort_strip(n):
        strip_loads[n].wait()
        if n >= 2:
            strip_outs[n - 2].wait()

        def order(k, _):
            sorted_strip[n % 2, k] = strip[n % 2, pl.ds(k, FINE, stride=RADIX), :]
            return 0

        lax.fori_loop(0, RADIX, order, 0)
        strip_outs[n].start()
        if n + 2 < strips:
            strip_loads[n + 2].start()

    todo = list(range(strips))

    def sort_strips(number):
        for _ in range(min(number, len(todo))):
            sort_strip(todo.pop(0))

    for copy in strip_loads[:2]:
        copy.start()
    outs = []

    def transform(inputs, targets):
        u = len(outs)
        base = 0
        for ref, first, rows in inputs:
            here = slice(base, base + rows)
            high_ref[here], low_ref[here] = split(ref[first : first + rows])
            base += rows
        if u >= 2:
            for out in outs[u - 2]:
                out.wait()
        dot = functools.partial(jnp.dot, preferred_element_type=jnp.float32)
        for part in range(2):

            def tile(t, _, part=part):
                at = pl.ds(pl.multiple_of(t * TILE, TILE), TILE)
                source = pl.ds(pl.multiple_of(part * columns + t * TILE, TILE), TILE)
                weight = table_high[:, source]
                high = high_ref[:base]
                result[u % 2, part, :base, at] = (
                    dot(high, weight)
                    + dot(low_ref[:base], weight)
                    + dot(high, table_low[:, source])
                )
                return 0

            lax.fori_loop(0, columns // TILE, tile, 0)
        copies = []
        at = 0
        for n, (first, rows) in enumerate(targets):
            copies.append(
                pltpu.make_async_copy(
                    result.at[u % 2, :, pl.ds(at, rows)],
                    planes_hbm.at[:, pl.ds(first, rows)],
                    result_sem.at[u % 2, n],
                )
            )
            at += rows
        for copy in copies:
            copy.start()
        outs.append(copies)

    def pass_on(n):
        crossing[n].wait_recv()
        passing[n].start()

    def far(n):
        c, first, size = pieces[n]
        passing[n].wait_recv()
        base = 2 * height + c * unit + first
        transform(
            [(cross.at[c], first, size), (passed.at[c], first, size)],
            [(base, size), (base + FINE, size)],
        )

    for h in range(halves):
        own_loads[h].wait()
        transform([(mine, h * unit, unit)], [(h * unit, unit)])
    pass_on(0)
    for h in range(halves):
        nearby[h].wait_recv()
        transform([(beside, h * unit, unit)], [(height + h * unit, unit)])
    share = -(-strips // (count - 1))
    for n in range(1, count):
        sort_strips(share if n < count - 1 else strips)
        if n == count - 1:
            far(n - 1)
            pass_on(n)
        else:
            pass_on(n)
            far(n - 1)

    kept.wait()
    for copy in regroup:
        copy.wait_recv()
    gram_values = [[gram[c, k] for k in range(slots)] for c in range(slots)]

    def mix(step, _):
        rows = pl.ds(pl.multiple_of(step // (width // LANES) * 8, 8), 8)
        lanes = pl.ds(pl.multiple_of(step % (width // LANES) * LANES, LANES), LANES)
        values = [cube[k, rows, lanes] for k in range(slots)]
        for c in range(slots):
            total = gram_values[c][0] * values[0]
            for k in range(1, slots):
                total = total + gram_values[c][k] * values[k]
            cube[c, rows, lanes] = total
        return 0

    lax.fori_loop(0, block // 8 * (width // LANES), mix, 0, unroll=2)
    prior_out = pltpu.make_async_copy(cube, prior_hbm, prior_sem.at[1])
    prior_out.start()
    far(count - 1)

    for copy in crossing + nearby + passing + regroup:
        copy.wait_send()
    for copy in table_outs + outs[-2] + outs[-1] + strip_outs[-2:] + [prior_out]:
        copy.wait()


def gather(basis, slot_channel, own, spectrum, sizes):
    height, width = own.shape
    length, columns = spectrum.shape
    factors = [jnp.asarray(factor) for factor in column_factors(width, length)]
    unit = 2 * FINE
    chunks = height // FINE
    halves = height // unit
    flights = 2 * len(far_pieces(chunks, False)) + halves
    block = height // sizes[0]
    anywhere = pl.BlockSpec(memory_space=pl.ANY)
    scalars = pl.BlockSpec(memory_space=pltpu.SMEM)
    table = jax.ShapeDtypeStruct((width, 2 * columns), jnp.bfloat16)
    dma = pltpu.SemaphoreType.DMA
    return pl.pallas_call(
        functools.partial(gather_kernel, ("chan", "facet"), sizes),
        in_specs=[scalars, scalars] + [anywhere] * 6,
        out_specs=[anywhere] * 5,
        out_shape=[
            jax.ShapeDtypeStruct((2, sizes[1] * height, columns), jnp.float32),
            jax.ShapeDtypeStruct((sizes[0], block, width), jnp.float32),
            table,
            table,
            jax.ShapeDtypeStruct((RADIX, FINE, columns), jnp.float32),
        ],
        scratch_shapes=[
            pltpu.VMEM(table.shape, jnp.bfloat16),
            pltpu.VMEM(table.shape, jnp.bfloat16),
            pltpu.VMEM((2, width // ROOT, columns), jnp.float32),
            pltpu.VMEM((2, ROOT, columns), jnp.float32),
            pltpu.VMEM((height, width), jnp.float32),
            pltpu.VMEM((height, width), jnp.float32),
            pltpu.VMEM((chunks, FINE, width), jnp.float32),
            pltpu.VMEM((chunks, FINE, width), jnp.float32),
            pltpu.VMEM((unit, width), jnp.bfloat16),
            pltpu.VMEM((unit, width), jnp.bfloat16),
            pltpu.VMEM((2, 2, unit, columns), jnp.float32),
            pltpu.VMEM((sizes[0], block, width), jnp.float32),
            pltpu.VMEM((2, length, LANES), jnp.float32),
            pltpu.VMEM((2, RADIX, FINE, LANES), jnp.float32),
            pltpu.SMEM((sizes[0], sizes[0]), jnp.float32),
            dma((2,)),
            dma((2,)),
            dma((halves,)),
            dma((4,)),
            dma((2,)),
            dma((2, 2)),
            dma((2,)),
            dma((flights,)),
            dma((flights,)),
            dma((sizes[0] - 1,)),
            dma((sizes[0] - 1,)),
        ],
        compiler_params=pltpu.CompilerParams(
            collective_id=2, has_side_effects=True, vmem_limit_bytes=60 << 20
        ),
        cost_estimate=SMALL,
        name="gather",
    )(basis, slot_channel, own, spectrum, *factors)


def scatter_kernel(axes, sizes, rows_hbm, high_hbm, low_hbm, prior_hbm, residual_hbm,
                   direction_hbm, applied_hbm, sums_ref, table_high, table_low, held, high_ref,
                   low_ref, part, landed, beside, own, near, cross, prior, stream, moment,
                   mine, got, table_sem, held_sem, stream_sem, out_sem, kept_sem, send_sem,
                   recv_sem, group_send, group_recv, regroup_send, regroup_recv):
    width = table_high.shape[0]
    columns = held.shape[3]
    unit = held.shape[2]
    height = own.shape[0]
    chunks = height // FINE
    tiles = width // TILE
    place = lax.axis_index("facet")
    sibling = place + 1 - 2 * lax.rem(place, 2)
    partner = lax.rem(place + 2, 4)

    def peers(axis):
        me = lax.axis_index(axes[axis])
        return [lax.rem(me + hop, sizes[axis]) for hop in range(1, sizes[axis])]

    def table_copies(t):
        at = pl.ds(pl.multiple_of(t * TILE, TILE), TILE)
        return [
            pltpu.make_async_copy(source.at[at], target.at[at], table_sem.at[n, t])
            for n, (source, target) in enumerate(((high_hbm, table_high), (low_hbm, table_low)))
        ]

    pieces = far_pieces(chunks, True)
    count = len(pieces)
    halves = height // unit
    units = []
    for c, first, size in pieces:
        base = 2 * height + unit * c + first
        units.append([(base, size), (base + FINE, size)])
    units += [[(height + unit * h, unit)] for h in range(halves)]
    units += [[(unit * h, unit)] for h in range(halves)]
    loads = []
    for u, blocks in enumerate(units):
        copies, at = [], 0
        for n, (first, size) in enumerate(blocks):
            copies.append(
                pltpu.make_async_copy(
                    rows_hbm.at[:, pl.ds(first, size)],
                    held.at[u % 2, :, pl.ds(at, size)],
                    held_sem.at[u % 2, n],
                )
            )
            at += size
        loads.append(copies)

    def load(u):
        for copy in loads[u]:
            copy.start()

    barrier = pltpu.get_barrier_semaphore()
    load(0)
    for t in range(tiles):
        for copy in table_copies(t):
            copy.start()
    for axis in range(2):
        for peer in peers(axis):
            pl.semaphore_signal(barrier, inc=1, device_id={axes[axis]: peer}, device_id_type=MESH)

    def image(u, targets):
        size = sum(rows for _, rows in units[u])
        for copy in loads[u]:
            copy.wait()
        if u + 1 < len(units):
            load(u + 1)
        for part_at in range(2):
            col = slice(part_at * columns, (part_at + 1) * columns)
            high_ref[:size, col], low_ref[:size, col] = split(held[u % 2, part_at, :size])
        wide = (((1,), (1,)), ((), ()))
        dot = functools.partial(
            lax.dot_general, dimension_numbers=wide, preferred_element_type=jnp.float32
        )

        def tile(t, _):
            if u == 0:
                for copy in table_copies(t):
                    copy.wait()
            at = pl.ds(pl.multiple_of(t * TILE, TILE), TILE)
            weight = table_high[at, :]
            high = high_ref[:size]
            values = (
                dot(high, weight) + dot(low_ref[:size], weight) + dot(high, table_low[at, :])
            )
            base = 0
            for ref, first, rows in targets:
                ref[first : first + rows, at] = values[base : base + rows]
                base += rows
            return 0

        lax.fori_loop(0, tiles, tile, 0)

    def remote(source, target, slot, device):
        return pltpu.make_async_remote_copy(
            src_ref=source,
            dst_ref=target,
            send_sem=send_sem.at[slot],
            recv_sem=recv_sem.at[slot],
            device_id={"facet": device},
            device_id_type=MESH,
        )

    def piece_rows(n):
        c, first, size = pieces[n]
        return pl.ds(c * FINE + first, size)

    paired, crossing = [], []
    for n, (c, first, size) in enumerate(pieces):
        here = pl.ds(first, size)
        paired.append(
            remote(part.at[c, pl.ds(FINE + first, size)], landed.at[c, here], n, sibling)
        )
        crossing.append(remote(part.at[c, here], cross.at[piece_rows(n)], count + n, partner))
    nearby = [
        remote(beside.at[h], near.at[pl.ds(h * unit, unit)], 2 * count + h, sibling)
        for h in range(halves)
    ]

    def cross_over(n):
        c, first, size = pieces[n]
        paired[n].wait_recv()

        def add(i, _):
            at = pl.ds(pl.multiple_of(first + i * 8, 8), 8)
            part[c, at, :] += landed[c, at, :]
            return 0

        lax.fori_loop(0, size // 8, add, 0)
        crossing[n].start()

    me = lax.axis_index(axes[0])
    block = height // sizes[0]
    mine_rows = pl.ds(pl.multiple_of(me * block, block), block)
    kept = pltpu.make_async_copy(prior_hbm.at[me], prior.at[mine_rows], kept_sem)
    kept.start()
    regroup = []
    for hop, peer in enumerate(peers(0)):
        regroup.append(
            pltpu.make_async_remote_copy(
                src_ref=prior_hbm.at[peer],
                dst_ref=prior.at[mine_rows],
                send_sem=regroup_send.at[hop],
                recv_sem=regroup_recv.at[hop],
                device_id={axes[0]: peer},
                device_id_type=MESH,
            )
        )
    pl.semaphore_wait(barrier, sizes[0] + sizes[1] - 2)
    for copy in regroup:
        copy.start()

    for n, (c, first, size) in enumerate(pieces):
        image(n, [(part.at[c], first, size), (part.at[c], FINE + first, size)])
        paired[n].start()
        if n:
            cross_over(n - 1)
    for h in range(halves):
        image(count + h, [(beside.at[h], 0, unit)])
        if h == 0:
            cross_over(count - 1)
        nearby[h].start()
    streams = [
        [
            pltpu.make_async_copy(
                source.at[piece_rows(n)],
                stream.at[k, pl.ds(0, pieces[n][2])],
                stream_sem.at[k],
            )
            for k, source in enumerate((residual_hbm, direction_hbm))
        ]
        for n in range(count)
    ]
    for copy in streams[0]:
        copy.start()
    for h in range(halves):
        image(count + halves + h, [(own, h * unit, unit)])

    moment[...] = jnp.zeros_like(moment)
    for copy in nearby + regroup:
        copy.wait_recv()
    kept.wait()
    outs = []

    def fold(total):
        folded = total[:, :LANES]
        for at in range(LANES, width, LANES):
            folded = folded + total[:, at : at + LANES]
        return folded

    for n, (c, first, size) in enumerate(pieces):
        for copy in streams[n]:
            copy.wait()
        crossing[n].wait_recv()

        def gather_rows(i, _, base=c * FINE + first):
            at = pl.ds(pl.multiple_of(i * 8, 8), 8)
            here = pl.ds(pl.multiple_of(base + i * 8, 8), 8)
            applied = own[here, :] + near[here, :] + cross[here, :] + prior[here, :]
            own[here, :] = applied
            residual, direction = stream[0, at, :], stream[1, at, :]
            moment[0] += fold(residual * residual)
            moment[1] += fold(direction * applied)
            moment[2] += fold(residual * applied)
            moment[3] += fold(applied * applied)
            return 0

        lax.fori_loop(0, size // 8, gather_rows, 0)
        if n + 1 < count:
            for copy in streams[n + 1]:
                copy.start()
        out = pltpu.make_async_copy(
            own.at[piece_rows(n)], applied_hbm.at[piece_rows(n)], out_sem.at[n]
        )
        out.start()
        outs.append(out)

    group_sum(axes, sizes, moment[...], sums_ref, mine, got, group_send, group_recv)
    for copy in paired + crossing + nearby + regroup:
        copy.wait_send()
    for out in outs:
        out.wait()


def scatter(rows, tables, prior, residual, direction, sizes):
    height, width = direction.shape
    columns = rows.shape[2]
    unit = 2 * FINE
    chunks = height // FINE
    hops = sizes[0] + sizes[1] - 2
    count = len(far_pieces(chunks, True))
    flights = 2 * count + height // unit
    anywhere = pl.BlockSpec(memory_space=pl.ANY)
    shape = (4, 8, LANES)
    whole = pltpu.VMEM((height, width), jnp.float32)
    dma = pltpu.SemaphoreType.DMA
    return pl.pallas_call(
        functools.partial(scatter_kernel, ("chan", "facet"), sizes),
        in_specs=[anywhere] * 6,
        out_specs=[anywhere, pl.BlockSpec(memory_space=pltpu.VMEM)],
        out_shape=[
            jax.ShapeDtypeStruct((height, width), jnp.float32),
            jax.ShapeDtypeStruct(shape, jnp.float32),
        ],
        scratch_shapes=[
            pltpu.VMEM((width, 2 * columns), jnp.bfloat16),
            pltpu.VMEM((width, 2 * columns), jnp.bfloat16),
            pltpu.VMEM((2, 2, unit, columns), jnp.float32),
            pltpu.VMEM((unit, 2 * columns), jnp.bfloat16),
            pltpu.VMEM((unit, 2 * columns), jnp.bfloat16),
            pltpu.VMEM((chunks, unit, width), jnp.float32),
            pltpu.VMEM((chunks, FINE, width), jnp.float32),
            pltpu.VMEM((height // unit, unit, width), jnp.float32),
            whole,
            whole,
            whole,
            whole,
            pltpu.VMEM((2, FINE, width), jnp.float32),
            pltpu.VMEM(shape, jnp.float32),
            pltpu.VMEM((2,) + shape, jnp.float32),
            pltpu.VMEM((hops,) + shape, jnp.float32),
            dma((2, width // TILE)),
            dma((2, 2)),
            dma((2,)),
            dma((count,)),
            dma,
            dma((flights,)),
            dma((flights,)),
            dma((hops,)),
            dma((hops,)),
            dma((sizes[0] - 1,)),
            dma((sizes[0] - 1,)),
        ],
        compiler_params=pltpu.CompilerParams(
            collective_id=1, has_side_effects=True, vmem_limit_bytes=60 << 20
        ),
        cost_estimate=SMALL,
        name="scatter",
    )(rows, *tables, prior, residual, direction)


def update_kernel(
    sum_ref, solution_ref, residual_ref, direction_ref, applied_ref, x_ref, r_ref, d_ref
):
    def scalar(at):
        return sum_ref[at, 0:1, 0:1]

    norm_now, curvature, cross, square = [scalar(at) for at in range(4)]
    step_size = norm_now / curvature
    norm_next = norm_now - 2.0 * step_size * cross + step_size * step_size * square
    ratio = norm_next / norm_now
    direction = direction_ref[...]
    x_ref[...] = solution_ref[...] + step_size * direction
    residual = residual_ref[...] - step_size * applied_ref[...]
    r_ref[...] = residual
    d_ref[...] = residual + ratio * direction


def update(sums, solution, residual, direction, applied):
    height, width = applied.shape
    step = 64
    block = pl.BlockSpec((step, width), lambda i: (i, 0))
    return pl.pallas_call(
        update_kernel,
        grid=(height // step,),
        in_specs=[pl.BlockSpec(sums.shape, lambda i: (0, 0, 0))] + [block] * 4,
        out_specs=[block] * 3,
        out_shape=[jax.ShapeDtypeStruct((height, width), jnp.float32)] * 3,
        cost_estimate=SMALL,
        name="update",
    )(sums, solution, residual, direction, applied)


def swap_pairs(array, count, bit):
    pairs = [(place, place ^ bit) for place in range(count)]
    return lax.ppermute(array, "facet", pairs)


def body(solution, residual, direction, spectra, basis, slot_channel):
    channel_count = basis.shape[0]
    length = RADIX * FINE
    facets = lax.axis_size("facet")
    place = lax.axis_index("facet")
    height, width = direction.shape[1:]
    columns = spectra.shape[2]
    own = direction[0]
    top = facets // 2
    per_facet = height // FINE
    barrier = lax.optimization_barrier

    groups = []
    if per_facet > 1:
        groups += [[(key, s) for s in range(per_facet)] for key in range(top)]
    else:
        groups.append([(key, 0) for key in range(top)])
    groups += [[(key, s) for key in range(top, facets)] for s in range(per_facet)]
    starts = np.cumsum([0] + [len(entries) * FINE for entries in groups])
    slot_of = np.zeros((facets, per_facet), np.int32)
    for at, (key, s) in enumerate(entry for entries in groups for entry in entries):
        slot_of[key, s] = at
    slots = jnp.asarray(slot_of)[jnp.arange(facets, dtype=jnp.int32) ^ place].reshape(-1)

    sizes = (lax.axis_size("chan"), facets)
    if facets == 4 and per_facet % 2 == 0 and height % (8 * sizes[0]) == 0:
        planes, local, *tables, weight = gather(basis, slot_channel, own, spectra[0], sizes)
        rows = row_pass(planes, weight, slots)
        applied, sums = scatter(rows, tables, local, residual[0], own, sizes)
        results = update(sums, solution[0], residual[0], own, applied)
        return tuple(result[None] for result in results)

    chunks = [own[at * FINE : (at + 1) * FINE] for at in range(per_facet)]
    crossed = [swap_pairs(chunk, facets, top) for chunk in chunks]

    def spread(block, key):
        blocks = {key: block}
        bit = top // 2
        while bit:
            blocks.update({k ^ bit: swap_pairs(blocks[k], facets, bit) for k in list(blocks)})
            bit //= 2
        return blocks

    near = spread(own, 0)

    cube = own.reshape(channel_count, height // channel_count, width)
    regrouped = lax.all_to_all(cube, "chan", split_axis=0, concat_axis=0, tiled=True)
    one_hot = (
        slot_channel[:, None] == jnp.arange(channel_count, dtype=jnp.int32)[None, :]
    ).astype(jnp.float32)
    loadings = jnp.dot(one_hot, basis, precision=HIGHEST)
    gram = jnp.einsum("cq,dq->cd", loadings, loadings, precision=HIGHEST)
    gram = gram + PRIOR_FLOOR * jnp.eye(channel_count, dtype=jnp.float32)

    tables = width_table(width, columns, length, place)
    planes = None
    far = {}
    for step, entries in enumerate(groups):
        if entries[0][0] >= top:
            blocks = [far[s][key] for key, s in entries]
        elif per_facet > 1:
            blocks = [near[entries[0][0]]]
        else:
            blocks = [near[key] for key, _ in entries]
        planes = width_forward(
            blocks, tables, planes, int(starts[step]), columns, facets * height
        )
        if step < per_facet:
            block, planes = barrier((crossed[step], planes))
            far[step] = spread(block, top)
        if step == len(groups) - 2:
            local = prior_term(regrouped, gram, planes)
            local, planes = barrier((local, planes))
            prior = lax.all_to_all(local, "chan", split_axis=0, concat_axis=0, tiled=True)
            prior = prior.reshape(height, width)

    weight = spectra[0].reshape(FINE, RADIX, columns).transpose(1, 0, 2)
    rows = row_pass(planes, weight, slots)

    arrived = {}
    near_sums = {}
    held = [rows]
    previous = None
    sequence = [at for at in range(len(groups)) if groups[at][0][0] >= top]
    sequence += [at for at in range(len(groups)) if groups[at][0][0] < top][::-1]

    def send(entries, parts):
        sums = {key: part for (key, _), part in zip(entries, parts)}
        bit = 1
        while bit < top:
            sums = {
                key: sums[key] + swap_pairs(sums[key | bit], facets, bit)
                for key in sorted(sums, reverse=True)
                if not key & bit
            }
            bit *= 2
        arrived[entries[0][1]] = swap_pairs(sums[top], facets, top)
        return sums[top]

    for turn_at, at in enumerate(sequence):
        entries = groups[at]
        far_rows = entries[0][0] >= top
        counts = [FINE] * len(entries) if far_rows or per_facet == 1 else [height]
        parts = width_back(rows, tables, int(starts[at]), counts, held)
        held = [parts[0]]
        if previous is not None:
            held.append(send(*previous))
            previous = None
        if turn_at >= 3 and turn_at - 3 < per_facet:
            held.append(arrived[groups[sequence[turn_at - 3]][0][1]])
        if far_rows:
            previous = (entries, parts)
        else:
            near_sums.update({key: part for (key, _), part in zip(entries, parts)})
    bit = 1
    while 2 * bit < top:
        near_sums = {
            key: near_sums[key] + swap_pairs(near_sums[key | bit], facets, bit)
            for key in sorted(near_sums, reverse=True)
            if not key & bit
        }
        bit *= 2
    wide = [near_sums[0], swap_pairs(near_sums[bit], facets, bit)]

    applied = None
    moments = []
    for s in range(per_facet):
        first = s * FINE
        applied, moment = moments_of(
            wide, prior, arrived[s], residual[0], own, applied, first
        )
        moments.append(moment)
    sums = reduce_moments(moments, ("chan", "facet"), sizes)
    results = update(sums, solution[0], residual[0], own, applied)
    return tuple(result[None] for result in results)


def solution(mesh):
    return jax.shard_map(
        body,
        mesh=mesh,
        in_specs=(
            P("chan", "facet", None),
            P("chan", "facet", None),
            P("chan", "facet", None),
            P("chan", None, "facet"),
            P(),
            P(),
        ),
        out_specs=(P("chan", "facet", None), P("chan", "facet", None), P("chan", "facet", None)),
        check_vma=False,
    )
```

```python
import functools
import math

import jax
import jax.numpy as jnp
import ml_dtypes
import numpy as np
from jax import lax
from jax.experimental import pallas as pl
from jax.experimental.pallas import tpu as pltpu
from jax.sharding import PartitionSpec as P

RADIX = 32
FINE = 128
ROOT = 64
LANES = 128
TILE = 256
HIGHEST = lax.Precision.HIGHEST
PRIOR_FLOOR = 0.25
HALF = math.sqrt(0.5)
MESH = pl.DeviceIdType.MESH
SMALL = pl.CostEstimate(flops=1, bytes_accessed=1, transcendentals=0)


def np_split(table):
    high = table.astype(ml_dtypes.bfloat16)
    low = (table - high.astype(np.float64)).astype(ml_dtypes.bfloat16)
    return high, low


@functools.cache
def row_tables():
    length = RADIX * FINE
    coarse = np.arange(RADIX)[:, None, None]
    fine = np.arange(FINE)[None, :, None]
    place = np.arange(FINE)[None, None, :]
    angle = -2.0 * np.pi * ((place * (RADIX * fine + coarse)) % length) / length
    real, imag = np.cos(angle), np.sin(angle)
    forward = np.concatenate(
        [np.concatenate([real, -imag], axis=2), np.concatenate([imag, real], axis=2)], axis=1
    )
    inverse = np.transpose(forward, (0, 2, 1)) / float(length * length)
    return np_split(forward) + np_split(inverse)


@functools.cache
def column_factors(width, length):
    column = np.arange(length)[None, :]

    def wave(rows):
        angle = -2.0 * np.pi * ((rows[:, None] * column) % length) / length
        return np.cos(angle).astype(np.float32), np.sin(angle).astype(np.float32)

    return wave(np.arange(width // ROOT) * ROOT) + wave(np.arange(ROOT))


def split(values):
    high = values.astype(jnp.bfloat16)
    low = (values - high.astype(jnp.float32)).astype(jnp.bfloat16)
    return high, low


def turn(real, imag, num, den, sign):
    num %= den
    if (num * 8) % den == 0:
        eighth = (sign * (num * 8 // den)) % 8
        if eighth == 0:
            return real, imag
        if eighth == 1:
            return (real - imag) * HALF, (real + imag) * HALF
        if eighth == 2:
            return -imag, real
        if eighth == 3:
            return (real + imag) * -HALF, (real - imag) * HALF
        if eighth == 4:
            return -real, -imag
        if eighth == 5:
            return (imag - real) * HALF, (real + imag) * -HALF
        if eighth == 6:
            return imag, -real
        return (real + imag) * HALF, (imag - real) * HALF
    c = math.cos(2.0 * math.pi * num / den)
    s = sign * math.sin(2.0 * math.pi * num / den)
    return real * c - imag * s, real * s + imag * c


def fft(points, sign):
    count = len(points)
    if count == 1:
        return points
    half = count // 2
    even, odd = [], []
    for i in range(half):
        (ar, ai), (br, bi) = points[i], points[i + half]
        even.append((ar + br, ai + bi))
        if 4 * i == count:
            odd.append((ai - bi, br - ar) if sign < 0 else (bi - ai, ar - br))
        else:
            odd.append(turn(ar - br, ai - bi, i, count, sign))
    result = [None] * count
    result[0::2] = fft(even, sign)
    result[1::2] = fft(odd, sign)
    return result


def dot3(table_high, table_low, values):
    high, low = split(values)
    dot = functools.partial(jnp.dot, preferred_element_type=jnp.float32)
    return dot(table_high, high) + dot(table_low, high) + dot(table_high, low)


def row_kernel(slot_of, planes_ref, weight_ref, *refs):
    table_hbm, (out_ref, work_a, work_b, *tables, table_sem) = refs[:4], refs[4:]
    forward_high, forward_low, inverse_high, inverse_low = tables
    used = RADIX // 2
    place = lax.axis_index("facet")
    facets, per_facet = slot_of.shape

    def slot(a):
        choices = [int(slot_of[a // per_facet ^ p, a % per_facet]) for p in range(facets)]
        at = choices[0]
        for p in range(1, facets):
            at = jnp.where(place == p, choices[p], at)
        return at * FINE

    slots = [slot(a) for a in range(used)]
    tile = pl.program_id(0)
    last = pl.num_programs(0) - 1
    copies = [
        pltpu.make_async_copy(source, target, table_sem.at[n])
        for n, (source, target) in enumerate(zip(table_hbm, tables))
    ]

    def rows(base, at):
        return pl.ds(pl.multiple_of(base + at, 8), 8)

    def position(step):
        lanes = pl.ds(pl.multiple_of(step // (FINE // 8) * LANES, LANES), LANES)
        return lax.rem(step, FINE // 8) * 8, lanes

    def forward(step, outer, inner):
        at, col = position(step)
        points = [(planes_ref[0, rows(s, at), col], planes_ref[1, rows(s, at), col]) for s in slots]
        for k, (real, imag) in enumerate(fft(points, -1)):
            outer[2 * k, rows(0, at), col] = real
            outer[2 * k, rows(FINE, at), col] = imag
        points = [turn(*point, a, RADIX, -1) for a, point in enumerate(points)]
        for k, (real, imag) in enumerate(fft(points, -1)):
            outer[2 * k + 1, rows(0, at), col] = real
            outer[2 * k + 1, rows(FINE, at), col] = imag

    def middle(k, outer, inner):
        freqs = dot3(forward_high[k], forward_low[k], inner[k])
        weight = weight_ref[k]
        freqs = freqs * jnp.concatenate([weight, weight], axis=0)
        inner[k] = dot3(inverse_high[k], inverse_low[k], freqs)

    def inverse(step, outer, inner):
        at, col = position(step)

        def side(odd):
            points = [
                (outer[2 * k + odd, rows(0, at), col], outer[2 * k + odd, rows(FINE, at), col])
                for k in range(used)
            ]
            return fft(points, 1)

        even, odd = side(0), side(1)
        for a, s in enumerate(slots):
            real, imag = turn(*odd[a], a, RADIX, 1)
            out_ref[0, rows(s, at), col] = even[a][0] + real
            out_ref[1, rows(s, at), col] = even[a][1] + imag

    def loop(parts, outer, inner, unroll=1):
        def run(step, _):
            for part in parts:
                part(step, outer, inner)
            return 0

        lax.fori_loop(0, RADIX, run, 0, unroll=unroll)

    @pl.when(tile == 0)
    def _():
        for copy in copies:
            copy.start()
        loop([forward], work_a, work_b)
        for copy in copies:
            copy.wait()

    for parity in range(2):
        outer, inner = (work_a, work_b) if parity == 0 else (work_b, work_a)
        mine = lax.rem(tile, 2) == parity

        @pl.when(mine & (tile > 0) & (tile < last))
        def _(outer=outer, inner=inner):
            loop([middle, inverse, forward], outer, inner, unroll=16)

        @pl.when(mine & (tile == last))
        def _(outer=outer, inner=inner):
            loop([inverse], outer, inner)


def row_pass(planes, weight, slot_of):
    _, height, columns = planes.shape
    tables = [jnp.asarray(table) for table in row_tables()]
    count = columns // TILE
    block = (2, height, TILE)
    return pl.pallas_call(
        functools.partial(row_kernel, slot_of),
        grid_spec=pltpu.PrefetchScalarGridSpec(
            num_scalar_prefetch=0,
            grid=(count + 2,),
            in_specs=[
                pl.BlockSpec(block, lambda i: (0, 0, jnp.minimum(i, count - 1))),
                pl.BlockSpec(
                    (RADIX, FINE, TILE), lambda i: (0, 0, jnp.clip(i - 1, 0, count - 1))
                ),
            ]
            + [pl.BlockSpec(memory_space=pl.ANY)] * 4,
            out_specs=pl.BlockSpec(block, lambda i: (0, 0, jnp.maximum(i - 2, 0))),
            scratch_shapes=[pltpu.VMEM((RADIX, 2 * FINE, TILE), jnp.float32)] * 2
            + [pltpu.VMEM((RADIX, 2 * FINE, 2 * FINE), jnp.bfloat16)] * 4
            + [pltpu.SemaphoreType.DMA((4,))],
        ),
        out_shape=jax.ShapeDtypeStruct(planes.shape, jnp.float32),
        compiler_params=pltpu.CompilerParams(vmem_limit_bytes=62 << 20),
        cost_estimate=SMALL,
        name="row_pass",
    )(planes, weight, *tables)


def table_kernel(place_ref, coarse_real, coarse_imag, fine_real, fine_imag, high_ref, low_ref):
    columns = fine_real.shape[1]
    row = pl.ds(pl.program_id(0) % 8, 1)
    coarse_r, coarse_i = coarse_real[row, :], coarse_imag[row, :]
    for at in range(0, columns, LANES):
        real, imag = slice(at, at + LANES), slice(columns + at, columns + at + LANES)
        cr, ci = coarse_r[:, real], coarse_i[:, real]
        fr, fi = fine_real[:, real], fine_imag[:, real]
        high_ref[:, real], low_ref[:, real] = split(cr * fr - ci * fi)
        high_ref[:, imag], low_ref[:, imag] = split(cr * fi + ci * fr)


def width_table(width, columns, length, place):
    factors = [jnp.asarray(factor) for factor in column_factors(width, length)]
    coarse = pl.BlockSpec((8, columns), lambda i, p: (i // 8, p[0]))
    fine = pl.BlockSpec((ROOT, columns), lambda i, p: (0, p[0]))
    out = pl.BlockSpec((ROOT, 2 * columns), lambda i, p: (i, 0))
    return pl.pallas_call(
        table_kernel,
        grid_spec=pltpu.PrefetchScalarGridSpec(
            num_scalar_prefetch=1,
            grid=(width // ROOT,),
            in_specs=[coarse, coarse, fine, fine],
            out_specs=[out, out],
        ),
        out_shape=[jax.ShapeDtypeStruct((width, 2 * columns), jnp.bfloat16)] * 2,
        cost_estimate=SMALL,
        name="width_table",
    )(place.reshape(1), *factors)


def width_kernel(count, *refs):
    blocks = refs[:count]
    table_high, table_low = refs[count : count + 2]
    out_ref, high_ref, low_ref = refs[-3:]

    @pl.when(pl.program_id(0) == 0)
    def _():
        base = 0
        for ref in blocks:
            rows = ref.shape[0]
            high_ref[base : base + rows], low_ref[base : base + rows] = split(ref[...])
            base += rows

    dot = functools.partial(jnp.dot, preferred_element_type=jnp.float32)
    high, low = high_ref[...], low_ref[...]
    weight = table_high[...]
    out_ref[0] = dot(high, weight) + dot(low, weight) + dot(high, table_low[...])


def width_forward(blocks, tables, planes, first, columns, height):
    width = blocks[0].shape[1]
    total = sum(block.shape[0] for block in blocks)
    tiles = columns // TILE
    before = [] if planes is None else [planes]
    table = pl.BlockSpec((width, TILE), lambda n: (0, n))
    return pl.pallas_call(
        functools.partial(width_kernel, len(blocks)),
        grid=(2 * tiles,),
        in_specs=[pl.BlockSpec(block.shape, lambda n: (0, 0)) for block in blocks]
        + [table, table]
        + [pl.BlockSpec(memory_space=pl.ANY)] * len(before),
        out_specs=pl.BlockSpec(
            (1, total, TILE), lambda n: (n // tiles, first // total, n % tiles)
        ),
        out_shape=jax.ShapeDtypeStruct((2, height, columns), jnp.float32),
        scratch_shapes=[pltpu.VMEM((total, width), jnp.bfloat16)] * 2,
        input_output_aliases={len(blocks) + 2: 0} if before else {},
        compiler_params=pltpu.CompilerParams(vmem_limit_bytes=48 << 20),
        cost_estimate=SMALL,
        name="width_forward",
    )(*blocks, *tables, *before)


def back_kernel(count, planes_ref, table_high, table_low, *refs):
    outs = refs[-count - 2 : -2]
    high_ref, low_ref = refs[-2:]
    columns = planes_ref.shape[2]

    @pl.when(pl.program_id(0) == 0)
    def _():
        for part in range(2):
            col = slice(part * columns, (part + 1) * columns)
            high_ref[:, col], low_ref[:, col] = split(planes_ref[part])

    wide = (((1,), (1,)), ((), ()))
    dot = functools.partial(
        lax.dot_general, dimension_numbers=wide, preferred_element_type=jnp.float32
    )
    high, low = high_ref[...], low_ref[...]
    weight = table_high[...]
    image = dot(high, weight) + dot(low, weight) + dot(high, table_low[...])
    base = 0
    for ref in outs:
        rows = ref.shape[0]
        ref[...] = image[base : base + rows]
        base += rows


def width_back(planes, tables, first, sizes, after):
    _, _, columns = planes.shape
    width = tables[0].shape[0]
    total = sum(sizes)
    table = pl.BlockSpec((TILE, 2 * columns), lambda n: (n, 0))
    return pl.pallas_call(
        functools.partial(back_kernel, len(sizes)),
        grid=(width // TILE,),
        in_specs=[
            pl.BlockSpec((2, total, columns), lambda n: (0, first // total, 0)),
            table,
            table,
        ]
        + [pl.BlockSpec(memory_space=pl.ANY)] * len(after),
        out_specs=[pl.BlockSpec((rows, TILE), lambda n: (0, n)) for rows in sizes],
        out_shape=[jax.ShapeDtypeStruct((rows, width), jnp.float32) for rows in sizes],
        scratch_shapes=[pltpu.VMEM((total, 2 * columns), jnp.bfloat16)] * 2,
        compiler_params=pltpu.CompilerParams(vmem_limit_bytes=48 << 20),
        cost_estimate=SMALL,
        name="width_back",
    )(planes, *tables, *after)


def prior_kernel(gram_ref, cube_ref, _, out_ref):
    count, rows, width = cube_ref.shape
    gram = [[gram_ref[c, k] for k in range(count)] for c in range(count)]
    for at in range(0, rows, 8):
        for col in range(0, width, LANES):
            here = slice(at, at + 8), slice(col, col + LANES)
            values = [cube_ref[(k,) + here] for k in range(count)]
            for c in range(count):
                total = gram[c][0] * values[0]
                for k in range(1, count):
                    total = total + gram[c][k] * values[k]
                out_ref[(c,) + here] = total


def prior_term(cube, gram, after):
    count, rows, width = cube.shape
    block = pl.BlockSpec((count, 8, width), lambda i: (0, i, 0))
    return pl.pallas_call(
        prior_kernel,
        grid=(rows // 8,),
        in_specs=[
            pl.BlockSpec(memory_space=pltpu.SMEM),
            block,
            pl.BlockSpec(memory_space=pl.ANY),
        ],
        out_specs=block,
        out_shape=jax.ShapeDtypeStruct(cube.shape, jnp.float32),
        cost_estimate=SMALL,
        name="prior_term",
    )(gram, cube, after)


def moment_kernel(terms, *refs):
    parts = refs[:terms]
    residual_ref, direction_ref = refs[terms : terms + 2]
    applied_ref, moment_ref = refs[-2:]

    @pl.when(pl.program_id(0) == 0)
    def _():
        moment_ref[...] = jnp.zeros_like(moment_ref)

    applied = parts[0][...]
    for ref in parts[1:]:
        applied = applied + ref[...]
    applied_ref[...] = applied
    residual, direction = residual_ref[...], direction_ref[...]
    width = applied.shape[1]

    def fold(product):
        total = product[:8]
        for at in range(8, product.shape[0], 8):
            total = total + product[at : at + 8]
        folded = total[:, :LANES]
        for at in range(LANES, width, LANES):
            folded = folded + total[:, at : at + LANES]
        return folded

    moment_ref[0] += fold(residual * residual)
    moment_ref[1] += fold(direction * applied)
    moment_ref[2] += fold(residual * applied)
    moment_ref[3] += fold(applied * applied)


def moments_of(wide, prior, chunk, residual, direction, applied, first):
    rows, width = chunk.shape
    step = min(64, rows)
    at = first // step
    here = pl.BlockSpec((step, width), lambda i: (at + i, 0))
    chunk_spec = pl.BlockSpec((step, width), lambda i: (i, 0))
    terms = len(wide) + 2
    before = [] if applied is None else [applied]
    return pl.pallas_call(
        functools.partial(moment_kernel, terms),
        grid=(rows // step,),
        in_specs=[here] * len(wide)
        + [here, chunk_spec, here, here]
        + [pl.BlockSpec(memory_space=pl.ANY)] * len(before),
        out_specs=[here, pl.BlockSpec((4, 8, LANES), lambda i: (0, 0, 0))],
        out_shape=[
            jax.ShapeDtypeStruct(residual.shape, jnp.float32),
            jax.ShapeDtypeStruct((4, 8, LANES), jnp.float32),
        ],
        input_output_aliases={terms + 2: 0} if before else {},
        cost_estimate=SMALL,
        name="moments",
    )(*wide, prior, chunk, residual, direction, *before)


def group_sum(axes, sizes, total, out_ref, mine, landed, send_sem, recv_sem):
    slot = 0
    for axis in range(2):
        size = sizes[axis]
        me = lax.axis_index(axes[axis])
        mine[axis] = total
        copies = [
            pltpu.make_async_remote_copy(
                src_ref=mine.at[axis],
                dst_ref=landed.at[slot + hop - 1],
                send_sem=send_sem.at[slot + hop - 1],
                recv_sem=recv_sem.at[slot + hop - 1],
                device_id={axes[axis]: lax.rem(me + hop, size)},
                device_id_type=MESH,
            )
            for hop in range(1, size)
        ]
        for copy in copies:
            copy.start()
        for copy in copies:
            copy.wait()
        total = jnp.zeros_like(total)
        for source in range(size):
            hop = lax.rem(me - source + size, size)
            arrived = landed[slot + jnp.maximum(hop, 1) - 1]
            total = total + jnp.where(hop == 0, mine[axis], arrived)
        slot += size - 1
    sums = jnp.sum(jnp.sum(total, axis=2, keepdims=True), axis=1, keepdims=True)
    out_ref[...] = jnp.broadcast_to(sums, total.shape)


def reduce_kernel(axes, sizes, parts, *refs):
    inputs = refs[:parts]
    out_ref, mine, landed, send_sem, recv_sem = refs[parts:]
    barrier = pltpu.get_barrier_semaphore()
    for axis in range(2):
        me = lax.axis_index(axes[axis])
        for hop in range(1, sizes[axis]):
            peer = lax.rem(me + hop, sizes[axis])
            pl.semaphore_signal(barrier, inc=1, device_id={axes[axis]: peer}, device_id_type=MESH)
    total = inputs[0][...]
    for ref in inputs[1:]:
        total = total + ref[...]
    pl.semaphore_wait(barrier, sizes[0] + sizes[1] - 2)
    group_sum(axes, sizes, total, out_ref, mine, landed, send_sem, recv_sem)


def reduce_moments(moments, axes, sizes):
    shape = moments[0].shape
    slots = sizes[0] + sizes[1] - 2
    return pl.pallas_call(
        functools.partial(reduce_kernel, axes, sizes, len(moments)),
        out_shape=jax.ShapeDtypeStruct(shape, jnp.float32),
        in_specs=[pl.BlockSpec(memory_space=pltpu.VMEM)] * len(moments),
        out_specs=pl.BlockSpec(memory_space=pltpu.VMEM),
        scratch_shapes=[
            pltpu.VMEM((2,) + shape, jnp.float32),
            pltpu.VMEM((slots,) + shape, jnp.float32),
            pltpu.SemaphoreType.DMA((slots,)),
            pltpu.SemaphoreType.DMA((slots,)),
        ],
        compiler_params=pltpu.CompilerParams(collective_id=0, has_side_effects=True),
        cost_estimate=SMALL,
        name="reduce_moments",
    )(*moments)


def far_pieces(slabs):
    pieces = [(slab, 0, FINE) for slab in range(slabs - 1)]
    return pieces + [(slabs - 1, first, FINE // 2) for first in (0, FINE // 2)]


def tile_pieces(slabs, tiles):
    pieces = []
    for slab in range(slabs):
        if slab == 0:
            sizes = [tiles // 4, tiles // 4, tiles - tiles // 2]
        elif slab == slabs - 1:
            sizes = [tiles - tiles // 4, tiles // 4]
        else:
            sizes = [tiles]
        first = 0
        for size in sizes:
            pieces.append((slab, first, size))
            first += size
    return pieces


def gather_kernel(axes, sizes, basis_ref, slot_ref, own_hbm, spectrum_hbm, coarse_real_hbm,
                  coarse_imag_hbm, fine_real_hbm, fine_imag_hbm, planes_hbm, prior_hbm, high_hbm,
                  low_hbm, weight_hbm,
                  table_high, table_low, coarse, fine, mine, beside, cross, passed, high_ref,
                  low_ref, result, cube, strip, sorted_strip,
                  gram, strip_sem, sorted_sem, own_sem, factor_sem, table_sem, result_sem,
                  prior_sem, send_sem, recv_sem, group_send, group_recv):
    height, width = own_hbm.shape
    columns = fine.shape[2]
    unit = high_ref.shape[0]
    chunks = height // FINE
    halves = height // unit
    slots = sizes[0]
    block = height // slots
    place = lax.axis_index("facet")
    me = lax.axis_index("chan")
    sibling = place + 1 - 2 * lax.rem(place, 2)
    partner = lax.rem(place + 2, 4)

    def half_rows(h):
        return pl.ds(h * unit, unit)

    def block_rows(at):
        return pl.ds(pl.multiple_of(at * block, block), block)

    def remote(source, target, slot, device):
        return pltpu.make_async_remote_copy(
            src_ref=source,
            dst_ref=target,
            send_sem=send_sem.at[slot],
            recv_sem=recv_sem.at[slot],
            device_id={"facet": device},
            device_id_type=MESH,
        )

    pieces = far_pieces(chunks)
    count = len(pieces)
    crossing = [
        remote(
            own_hbm.at[pl.ds(c * FINE + first, size)],
            cross.at[c, pl.ds(first, size)],
            n,
            partner,
        )
        for n, (c, first, size) in enumerate(pieces)
    ]
    passing = [
        remote(
            cross.at[c, pl.ds(first, size)],
            passed.at[c, pl.ds(first, size)],
            count + n,
            sibling,
        )
        for n, (c, first, size) in enumerate(pieces)
    ]
    nearby = [
        remote(own_hbm.at[half_rows(h)], beside.at[half_rows(h)], 2 * count + h, sibling)
        for h in range(halves)
    ]
    strips = columns // LANES

    def strip_lanes(n):
        return pl.ds(n * LANES, LANES)

    strip_loads = [
        pltpu.make_async_copy(
            spectrum_hbm.at[:, strip_lanes(n)], strip.at[n % 2], strip_sem.at[n % 2]
        )
        for n in range(strips)
    ]
    strip_outs = [
        pltpu.make_async_copy(
            sorted_strip.at[n % 2], weight_hbm.at[:, :, strip_lanes(n)], sorted_sem.at[n % 2]
        )
        for n in range(strips)
    ]
    regroup = []
    for hop in range(1, slots):
        peer = lax.rem(me + hop, slots)
        regroup.append(
            pltpu.make_async_remote_copy(
                src_ref=own_hbm.at[block_rows(peer)],
                dst_ref=cube.at[me],
                send_sem=group_send.at[hop - 1],
                recv_sem=group_recv.at[hop - 1],
                device_id={"chan": peer},
                device_id_type=MESH,
            )
        )
    kept = pltpu.make_async_copy(own_hbm.at[block_rows(me)], cube.at[me], prior_sem.at[0])
    own_loads = [
        pltpu.make_async_copy(own_hbm.at[half_rows(h)], mine.at[half_rows(h)], own_sem.at[h])
        for h in range(halves)
    ]
    col = pl.ds(pl.multiple_of(place * columns, columns), columns)
    factors = [
        pltpu.make_async_copy(source.at[:, col], target, factor_sem.at[n])
        for n, (source, target) in enumerate(
            (
                (coarse_real_hbm, coarse.at[0]),
                (coarse_imag_hbm, coarse.at[1]),
                (fine_real_hbm, fine.at[0]),
                (fine_imag_hbm, fine.at[1]),
            )
        )
    ]

    barrier = pltpu.get_barrier_semaphore()
    for axis in range(2):
        at = lax.axis_index(axes[axis])
        for hop in range(1, sizes[axis]):
            peer = lax.rem(at + hop, sizes[axis])
            pl.semaphore_signal(barrier, inc=1, device_id={axes[axis]: peer}, device_id_type=MESH)
    for copy in factors + own_loads + [kept]:
        copy.start()
    pl.semaphore_wait(barrier, sizes[0] + sizes[1] - 2)
    for copy in crossing + nearby + regroup:
        copy.start()

    for copy in factors:
        copy.wait()

    def table_rows(j, _):
        rows = pl.ds(pl.multiple_of(j * ROOT, ROOT), ROOT)
        coarse_r, coarse_i = coarse[0, pl.ds(j, 1), :], coarse[1, pl.ds(j, 1), :]
        for at in range(0, columns, LANES):
            real, imag = slice(at, at + LANES), slice(columns + at, columns + at + LANES)
            cr, ci = coarse_r[:, real], coarse_i[:, real]
            fr, fi = fine[0, :, real], fine[1, :, real]
            table_high[rows, real], table_low[rows, real] = split(cr * fr - ci * fi)
            table_high[rows, imag], table_low[rows, imag] = split(cr * fi + ci * fr)
        return 0

    lax.fori_loop(0, width // ROOT, table_rows, 0)
    table_outs = [
        pltpu.make_async_copy(table_high, high_hbm, table_sem.at[0]),
        pltpu.make_async_copy(table_low, low_hbm, table_sem.at[1]),
    ]
    for copy in table_outs:
        copy.start()

    loadings = [
        [basis_ref[slot_ref[c], q] for q in range(basis_ref.shape[1])] for c in range(slots)
    ]
    for c in range(slots):
        for k in range(c + 1):
            total = loadings[c][0] * loadings[k][0]
            for q in range(1, basis_ref.shape[1]):
                total = total + loadings[c][q] * loadings[k][q]
            if c == k:
                total = total + PRIOR_FLOOR
            gram[c, k] = total
            gram[k, c] = total

    def sort_strip(n):
        strip_loads[n].wait()
        if n >= 2:
            strip_outs[n - 2].wait()

        def order(k, _):
            sorted_strip[n % 2, k] = strip[n % 2, pl.ds(k, FINE, stride=RADIX), :]
            return 0

        lax.fori_loop(0, RADIX, order, 0)
        strip_outs[n].start()
        if n + 2 < strips:
            strip_loads[n + 2].start()

    todo = list(range(strips))

    def sort_strips(number):
        for _ in range(min(number, len(todo))):
            sort_strip(todo.pop(0))

    for copy in strip_loads[:2]:
        copy.start()
    outs = []

    def transform(inputs, targets):
        u = len(outs)
        base = 0
        for ref, first, rows in inputs:
            here = slice(base, base + rows)
            high_ref[here], low_ref[here] = split(ref[first : first + rows])
            base += rows
        if u >= 2:
            for out in outs[u - 2]:
                out.wait()
        dot = functools.partial(jnp.dot, preferred_element_type=jnp.float32)
        for part in range(2):

            def tile(t, _, part=part):
                at = pl.ds(pl.multiple_of(t * TILE, TILE), TILE)
                source = pl.ds(pl.multiple_of(part * columns + t * TILE, TILE), TILE)
                weight = table_high[:, source]
                high = high_ref[:base]
                result[u % 2, part, :base, at] = (
                    dot(high, weight)
                    + dot(low_ref[:base], weight)
                    + dot(high, table_low[:, source])
                )
                return 0

            lax.fori_loop(0, columns // TILE, tile, 0)
        copies = []
        at = 0
        for n, (first, rows) in enumerate(targets):
            copies.append(
                pltpu.make_async_copy(
                    result.at[u % 2, :, pl.ds(at, rows)],
                    planes_hbm.at[:, pl.ds(first, rows)],
                    result_sem.at[u % 2, n],
                )
            )
            at += rows
        for copy in copies:
            copy.start()
        outs.append(copies)

    def pass_on(n):
        crossing[n].wait_recv()
        passing[n].start()

    def far(n):
        c, first, size = pieces[n]
        passing[n].wait_recv()
        base = 2 * height + c * unit + first
        transform(
            [(cross.at[c], first, size), (passed.at[c], first, size)],
            [(base, size), (base + FINE, size)],
        )

    for h in range(halves):
        own_loads[h].wait()
        transform([(mine, h * unit, unit)], [(h * unit, unit)])
    pass_on(0)
    for h in range(halves):
        nearby[h].wait_recv()
        transform([(beside, h * unit, unit)], [(height + h * unit, unit)])
    share = -(-strips // max(count - 3, 1))
    for n in range(1, count):
        if n < count - 2:
            sort_strips(share)
            pass_on(n)
            far(n - 1)
        else:
            sort_strips(strips)
            far(n - 1)
            pass_on(n)

    kept.wait()
    for copy in regroup:
        copy.wait_recv()
    gram_values = [[gram[c, k] for k in range(slots)] for c in range(slots)]

    def mix(step, _):
        rows = pl.ds(pl.multiple_of(step // (width // LANES) * 8, 8), 8)
        lanes = pl.ds(pl.multiple_of(step % (width // LANES) * LANES, LANES), LANES)
        values = [cube[k, rows, lanes] for k in range(slots)]
        for c in range(slots):
            total = gram_values[c][0] * values[0]
            for k in range(1, slots):
                total = total + gram_values[c][k] * values[k]
            cube[c, rows, lanes] = total
        return 0

    lax.fori_loop(0, block // 8 * (width // LANES), mix, 0, unroll=2)
    prior_out = pltpu.make_async_copy(cube, prior_hbm, prior_sem.at[1])
    prior_out.start()
    far(count - 1)

    for copy in crossing + nearby + passing + regroup:
        copy.wait_send()
    for copy in table_outs + outs[-2] + outs[-1] + strip_outs[-2:] + [prior_out]:
        copy.wait()


def gather(basis, slot_channel, own, spectrum, sizes):
    height, width = own.shape
    length, columns = spectrum.shape
    factors = [jnp.asarray(factor) for factor in column_factors(width, length)]
    unit = 2 * FINE
    chunks = height // FINE
    halves = height // unit
    flights = 2 * len(far_pieces(chunks)) + halves
    block = height // sizes[0]
    anywhere = pl.BlockSpec(memory_space=pl.ANY)
    scalars = pl.BlockSpec(memory_space=pltpu.SMEM)
    table = jax.ShapeDtypeStruct((width, 2 * columns), jnp.bfloat16)
    dma = pltpu.SemaphoreType.DMA
    return pl.pallas_call(
        functools.partial(gather_kernel, ("chan", "facet"), sizes),
        in_specs=[scalars, scalars] + [anywhere] * 6,
        out_specs=[anywhere] * 5,
        out_shape=[
            jax.ShapeDtypeStruct((2, sizes[1] * height, columns), jnp.float32),
            jax.ShapeDtypeStruct((sizes[0], block, width), jnp.float32),
            table,
            table,
            jax.ShapeDtypeStruct((RADIX, FINE, columns), jnp.float32),
        ],
        scratch_shapes=[
            pltpu.VMEM(table.shape, jnp.bfloat16),
            pltpu.VMEM(table.shape, jnp.bfloat16),
            pltpu.VMEM((2, width // ROOT, columns), jnp.float32),
            pltpu.VMEM((2, ROOT, columns), jnp.float32),
            pltpu.VMEM((height, width), jnp.float32),
            pltpu.VMEM((height, width), jnp.float32),
            pltpu.VMEM((chunks, FINE, width), jnp.float32),
            pltpu.VMEM((chunks, FINE, width), jnp.float32),
            pltpu.VMEM((unit, width), jnp.bfloat16),
            pltpu.VMEM((unit, width), jnp.bfloat16),
            pltpu.VMEM((2, 2, unit, columns), jnp.float32),
            pltpu.VMEM((sizes[0], block, width), jnp.float32),
            pltpu.VMEM((2, length, LANES), jnp.float32),
            pltpu.VMEM((2, RADIX, FINE, LANES), jnp.float32),
            pltpu.SMEM((sizes[0], sizes[0]), jnp.float32),
            dma((2,)),
            dma((2,)),
            dma((halves,)),
            dma((4,)),
            dma((2,)),
            dma((2, 2)),
            dma((2,)),
            dma((flights,)),
            dma((flights,)),
            dma((sizes[0] - 1,)),
            dma((sizes[0] - 1,)),
        ],
        compiler_params=pltpu.CompilerParams(
            collective_id=2, has_side_effects=True, vmem_limit_bytes=60 << 20
        ),
        cost_estimate=SMALL,
        name="gather",
    )(basis, slot_channel, own, spectrum, *factors)


def scatter_kernel(axes, sizes, rows_hbm, high_hbm, low_hbm, prior_hbm, residual_hbm,
                   direction_hbm, applied_hbm, sums_ref, table_high, table_low, held, high_ref,
                   low_ref, part, landed, beside, own, near, cross, prior, stream, moment,
                   mine, got, table_sem, held_sem, stream_sem, out_sem, kept_sem, send_sem,
                   recv_sem, group_send, group_recv, regroup_send, regroup_recv):
    width = table_high.shape[0]
    columns = held.shape[3]
    unit = held.shape[2]
    height = own.shape[0]
    chunks = height // FINE
    tiles = width // TILE
    place = lax.axis_index("facet")
    sibling = place + 1 - 2 * lax.rem(place, 2)
    partner = lax.rem(place + 2, 4)

    def peers(axis):
        me = lax.axis_index(axes[axis])
        return [lax.rem(me + hop, sizes[axis]) for hop in range(1, sizes[axis])]

    def table_copies(t):
        at = pl.ds(pl.multiple_of(t * TILE, TILE), TILE)
        return [
            pltpu.make_async_copy(source.at[at], target.at[at], table_sem.at[n, t])
            for n, (source, target) in enumerate(((high_hbm, table_high), (low_hbm, table_low)))
        ]

    pieces = tile_pieces(chunks, tiles)
    count = len(pieces)
    halves = height // unit
    units = []
    units += [[(2 * height + unit * c, unit)] for c in range(chunks)]
    units += [[(height + unit * h, unit)] for h in range(halves)]
    units += [[(unit * h, unit)] for h in range(halves)]
    loads = []
    for u, blocks in enumerate(units):
        copies, at = [], 0
        for n, (first, size) in enumerate(blocks):
            copies.append(
                pltpu.make_async_copy(
                    rows_hbm.at[:, pl.ds(first, size)],
                    held.at[u % 2, :, pl.ds(at, size)],
                    held_sem.at[u % 2, n],
                )
            )
            at += size
        loads.append(copies)

    def load(u):
        for copy in loads[u]:
            copy.start()

    barrier = pltpu.get_barrier_semaphore()
    load(0)
    for t in range(tiles):
        for copy in table_copies(t):
            copy.start()
    for axis in range(2):
        for peer in peers(axis):
            pl.semaphore_signal(barrier, inc=1, device_id={axes[axis]: peer}, device_id_type=MESH)

    def prepare(u):
        for copy in loads[u]:
            copy.wait()
        if u + 1 < len(units):
            load(u + 1)
        for part_at in range(2):
            col = slice(part_at * columns, (part_at + 1) * columns)
            high_ref[:, col], low_ref[:, col] = split(held[u % 2, part_at])

    def image(target, first, number, loading=False):
        wide = (((1,), (1,)), ((), ()))
        dot = functools.partial(
            lax.dot_general, dimension_numbers=wide, preferred_element_type=jnp.float32
        )

        def tile(t, _):
            if loading:
                for copy in table_copies(t):
                    copy.wait()
            at = pl.ds(pl.multiple_of(t * TILE, TILE), TILE)
            weight = table_high[at, :]
            high = high_ref[...]
            target[:, at] = (
                dot(high, weight) + dot(low_ref[...], weight) + dot(high, table_low[at, :])
            )
            return 0

        lax.fori_loop(first, first + number, tile, 0)

    def remote(source, target, slot, device):
        return pltpu.make_async_remote_copy(
            src_ref=source,
            dst_ref=target,
            send_sem=send_sem.at[slot],
            recv_sem=recv_sem.at[slot],
            device_id={"facet": device},
            device_id_type=MESH,
        )

    def slab_rows(c):
        return pl.ds(c * FINE, FINE)

    upper, lower = pl.ds(0, FINE), pl.ds(FINE, FINE)
    paired, crossing = [], []
    for n, (c, first, number) in enumerate(pieces):
        col = pl.ds(first * TILE, number * TILE)
        paired.append(remote(part.at[c, lower, col], landed.at[c, :, col], n, sibling))
        crossing.append(
            remote(part.at[c, upper, col], cross.at[slab_rows(c), col], count + n, partner)
        )
    nearby = [
        remote(beside.at[h], near.at[pl.ds(h * unit, unit)], 2 * count + h, sibling)
        for h in range(halves)
    ]

    def cross_over(n):
        c, first, number = pieces[n]
        col = pl.ds(first * TILE, number * TILE)
        paired[n].wait_recv()

        def add(i, _):
            at = pl.ds(pl.multiple_of(i * 8, 8), 8)
            part[c, at, col] += landed[c, at, col]
            return 0

        lax.fori_loop(0, FINE // 8, add, 0)
        crossing[n].start()

    me = lax.axis_index(axes[0])
    block = height // sizes[0]
    mine_rows = pl.ds(pl.multiple_of(me * block, block), block)
    kept = pltpu.make_async_copy(prior_hbm.at[me], prior.at[mine_rows], kept_sem)
    kept.start()
    regroup = []
    for hop, peer in enumerate(peers(0)):
        regroup.append(
            pltpu.make_async_remote_copy(
                src_ref=prior_hbm.at[peer],
                dst_ref=prior.at[mine_rows],
                send_sem=regroup_send.at[hop],
                recv_sem=regroup_recv.at[hop],
                device_id={axes[0]: peer},
                device_id_type=MESH,
            )
        )
    pl.semaphore_wait(barrier, sizes[0] + sizes[1] - 2)
    for copy in regroup:
        copy.start()

    for n, (c, first, number) in enumerate(pieces):
        if first == 0:
            prepare(c)
        image(part.at[c], first, number, loading=c == 0)
        paired[n].start()
        if n:
            cross_over(n - 1)
    for h in range(halves):
        prepare(chunks + h)
        image(beside.at[h], 0, tiles)
        if h == 0:
            cross_over(count - 1)
        nearby[h].start()
    streams = [
        [
            pltpu.make_async_copy(source.at[slab_rows(c)], stream.at[k], stream_sem.at[k])
            for k, source in enumerate((residual_hbm, direction_hbm))
        ]
        for c in range(chunks)
    ]
    for copy in streams[0]:
        copy.start()
    for h in range(halves):
        prepare(chunks + halves + h)
        image(own.at[pl.ds(h * unit, unit)], 0, tiles)

    moment[...] = jnp.zeros_like(moment)
    for copy in nearby + regroup:
        copy.wait_recv()
    kept.wait()
    outs = []

    def fold(total):
        folded = total[:, :LANES]
        for at in range(LANES, total.shape[1], LANES):
            folded = folded + total[:, at : at + LANES]
        return folded

    for n, (c, first, number) in enumerate(pieces):
        if first == 0:
            for copy in streams[c]:
                copy.wait()
        crossing[n].wait_recv()

        def gather_rows(i, _, c=c, col=pl.ds(first * TILE, number * TILE)):
            at = pl.ds(pl.multiple_of(i * 8, 8), 8)
            here = pl.ds(pl.multiple_of(c * FINE + i * 8, 8), 8)
            applied = own[here, col] + near[here, col] + cross[here, col] + prior[here, col]
            own[here, col] = applied
            residual, direction = stream[0, at, col], stream[1, at, col]
            moment[0] += fold(residual * residual)
            moment[1] += fold(direction * applied)
            moment[2] += fold(residual * applied)
            moment[3] += fold(applied * applied)
            return 0

        lax.fori_loop(0, FINE // 8, gather_rows, 0)
        if first + number < tiles:
            continue
        if c + 1 < chunks:
            for copy in streams[c + 1]:
                copy.start()
        out = pltpu.make_async_copy(
            own.at[slab_rows(c)], applied_hbm.at[slab_rows(c)], out_sem.at[c]
        )
        out.start()
        outs.append(out)

    group_sum(axes, sizes, moment[...], sums_ref, mine, got, group_send, group_recv)
    for copy in paired + crossing + nearby + regroup:
        copy.wait_send()
    for out in outs:
        out.wait()


def scatter(rows, tables, prior, residual, direction, sizes):
    height, width = direction.shape
    columns = rows.shape[2]
    unit = 2 * FINE
    chunks = height // FINE
    hops = sizes[0] + sizes[1] - 2
    count = len(tile_pieces(chunks, width // TILE))
    flights = 2 * count + height // unit
    anywhere = pl.BlockSpec(memory_space=pl.ANY)
    shape = (4, 8, LANES)
    whole = pltpu.VMEM((height, width), jnp.float32)
    dma = pltpu.SemaphoreType.DMA
    return pl.pallas_call(
        functools.partial(scatter_kernel, ("chan", "facet"), sizes),
        in_specs=[anywhere] * 6,
        out_specs=[anywhere, pl.BlockSpec(memory_space=pltpu.VMEM)],
        out_shape=[
            jax.ShapeDtypeStruct((height, width), jnp.float32),
            jax.ShapeDtypeStruct(shape, jnp.float32),
        ],
        scratch_shapes=[
            pltpu.VMEM((width, 2 * columns), jnp.bfloat16),
            pltpu.VMEM((width, 2 * columns), jnp.bfloat16),
            pltpu.VMEM((2, 2, unit, columns), jnp.float32),
            pltpu.VMEM((unit, 2 * columns), jnp.bfloat16),
            pltpu.VMEM((unit, 2 * columns), jnp.bfloat16),
            pltpu.VMEM((chunks, unit, width), jnp.float32),
            pltpu.VMEM((chunks, FINE, width), jnp.float32),
            pltpu.VMEM((height // unit, unit, width), jnp.float32),
            whole,
            whole,
            whole,
            whole,
            pltpu.VMEM((2, FINE, width), jnp.float32),
            pltpu.VMEM(shape, jnp.float32),
            pltpu.VMEM((2,) + shape, jnp.float32),
            pltpu.VMEM((hops,) + shape, jnp.float32),
            dma((2, width // TILE)),
            dma((2, 1)),
            dma((2,)),
            dma((chunks,)),
            dma,
            dma((flights,)),
            dma((flights,)),
            dma((hops,)),
            dma((hops,)),
            dma((sizes[0] - 1,)),
            dma((sizes[0] - 1,)),
        ],
        compiler_params=pltpu.CompilerParams(
            collective_id=1, has_side_effects=True, vmem_limit_bytes=60 << 20
        ),
        cost_estimate=SMALL,
        name="scatter",
    )(rows, *tables, prior, residual, direction)


def update_kernel(
    sum_ref, solution_ref, residual_ref, direction_ref, applied_ref, x_ref, r_ref, d_ref
):
    def scalar(at):
        return sum_ref[at, 0:1, 0:1]

    norm_now, curvature, cross, square = [scalar(at) for at in range(4)]
    step_size = norm_now / curvature
    norm_next = norm_now - 2.0 * step_size * cross + step_size * step_size * square
    ratio = norm_next / norm_now
    direction = direction_ref[...]
    x_ref[...] = solution_ref[...] + step_size * direction
    residual = residual_ref[...] - step_size * applied_ref[...]
    r_ref[...] = residual
    d_ref[...] = residual + ratio * direction


def update(sums, solution, residual, direction, applied):
    height, width = applied.shape
    step = 64
    block = pl.BlockSpec((step, width), lambda i: (i, 0))
    return pl.pallas_call(
        update_kernel,
        grid=(height // step,),
        in_specs=[pl.BlockSpec(sums.shape, lambda i: (0, 0, 0))] + [block] * 4,
        out_specs=[block] * 3,
        out_shape=[jax.ShapeDtypeStruct((height, width), jnp.float32)] * 3,
        cost_estimate=SMALL,
        name="update",
    )(sums, solution, residual, direction, applied)


def swap_pairs(array, count, bit):
    pairs = [(place, place ^ bit) for place in range(count)]
    return lax.ppermute(array, "facet", pairs)


def body(solution, residual, direction, spectra, basis, slot_channel):
    channel_count = basis.shape[0]
    length = RADIX * FINE
    facets = lax.axis_size("facet")
    place = lax.axis_index("facet")
    height, width = direction.shape[1:]
    columns = spectra.shape[2]
    own = direction[0]
    top = facets // 2
    per_facet = height // FINE
    barrier = lax.optimization_barrier

    groups = []
    if per_facet > 1:
        groups += [[(key, s) for s in range(per_facet)] for key in range(top)]
    else:
        groups.append([(key, 0) for key in range(top)])
    groups += [[(key, s) for key in range(top, facets)] for s in range(per_facet)]
    starts = np.cumsum([0] + [len(entries) * FINE for entries in groups])
    slot_of = np.zeros((facets, per_facet), np.int32)
    for at, (key, s) in enumerate(entry for entries in groups for entry in entries):
        slot_of[key, s] = at

    sizes = (lax.axis_size("chan"), facets)
    if facets == 4 and per_facet % 2 == 0 and height % (8 * sizes[0]) == 0:
        planes, local, *tables, weight = gather(basis, slot_channel, own, spectra[0], sizes)
        rows = row_pass(planes, weight, slot_of)
        applied, sums = scatter(rows, tables, local, residual[0], own, sizes)
        results = update(sums, solution[0], residual[0], own, applied)
        return tuple(result[None] for result in results)

    chunks = [own[at * FINE : (at + 1) * FINE] for at in range(per_facet)]
    crossed = [swap_pairs(chunk, facets, top) for chunk in chunks]

    def spread(block, key):
        blocks = {key: block}
        bit = top // 2
        while bit:
            blocks.update({k ^ bit: swap_pairs(blocks[k], facets, bit) for k in list(blocks)})
            bit //= 2
        return blocks

    near = spread(own, 0)

    cube = own.reshape(channel_count, height // channel_count, width)
    regrouped = lax.all_to_all(cube, "chan", split_axis=0, concat_axis=0, tiled=True)
    one_hot = (
        slot_channel[:, None] == jnp.arange(channel_count, dtype=jnp.int32)[None, :]
    ).astype(jnp.float32)
    loadings = jnp.dot(one_hot, basis, precision=HIGHEST)
    gram = jnp.einsum("cq,dq->cd", loadings, loadings, precision=HIGHEST)
    gram = gram + PRIOR_FLOOR * jnp.eye(channel_count, dtype=jnp.float32)

    tables = width_table(width, columns, length, place)
    planes = None
    far = {}
    for step, entries in enumerate(groups):
        if entries[0][0] >= top:
            blocks = [far[s][key] for key, s in entries]
        elif per_facet > 1:
            blocks = [near[entries[0][0]]]
        else:
            blocks = [near[key] for key, _ in entries]
        planes = width_forward(
            blocks, tables, planes, int(starts[step]), columns, facets * height
        )
        if step < per_facet:
            block, planes = barrier((crossed[step], planes))
            far[step] = spread(block, top)
        if step == len(groups) - 2:
            local = prior_term(regrouped, gram, planes)
            local, planes = barrier((local, planes))
            prior = lax.all_to_all(local, "chan", split_axis=0, concat_axis=0, tiled=True)
            prior = prior.reshape(height, width)

    weight = spectra[0].reshape(FINE, RADIX, columns).transpose(1, 0, 2)
    rows = row_pass(planes, weight, slot_of)

    arrived = {}
    near_sums = {}
    held = [rows]
    previous = None
    sequence = [at for at in range(len(groups)) if groups[at][0][0] >= top]
    sequence += [at for at in range(len(groups)) if groups[at][0][0] < top][::-1]

    def send(entries, parts):
        sums = {key: part for (key, _), part in zip(entries, parts)}
        bit = 1
        while bit < top:
            sums = {
                key: sums[key] + swap_pairs(sums[key | bit], facets, bit)
                for key in sorted(sums, reverse=True)
                if not key & bit
            }
            bit *= 2
        arrived[entries[0][1]] = swap_pairs(sums[top], facets, top)
        return sums[top]

    for turn_at, at in enumerate(sequence):
        entries = groups[at]
        far_rows = entries[0][0] >= top
        counts = [FINE] * len(entries) if far_rows or per_facet == 1 else [height]
        parts = width_back(rows, tables, int(starts[at]), counts, held)
        held = [parts[0]]
        if previous is not None:
            held.append(send(*previous))
            previous = None
        if turn_at >= 3 and turn_at - 3 < per_facet:
            held.append(arrived[groups[sequence[turn_at - 3]][0][1]])
        if far_rows:
            previous = (entries, parts)
        else:
            near_sums.update({key: part for (key, _), part in zip(entries, parts)})
    bit = 1
    while 2 * bit < top:
        near_sums = {
            key: near_sums[key] + swap_pairs(near_sums[key | bit], facets, bit)
            for key in sorted(near_sums, reverse=True)
            if not key & bit
        }
        bit *= 2
    wide = [near_sums[0], swap_pairs(near_sums[bit], facets, bit)]

    applied = None
    moments = []
    for s in range(per_facet):
        first = s * FINE
        applied, moment = moments_of(
            wide, prior, arrived[s], residual[0], own, applied, first
        )
        moments.append(moment)
    sums = reduce_moments(moments, ("chan", "facet"), sizes)
    results = update(sums, solution[0], residual[0], own, applied)
    return tuple(result[None] for result in results)


def solution(mesh):
    return jax.shard_map(
        body,
        mesh=mesh,
        in_specs=(
            P("chan", "facet", None),
            P("chan", "facet", None),
            P("chan", "facet", None),
            P("chan", None, "facet"),
            P(),
            P(),
        ),
        out_specs=(P("chan", "facet", None), P("chan", "facet", None), P("chan", "facet", None)),
        check_vma=False,
    )
```

```python
import functools
import math

import jax
import jax.numpy as jnp
import ml_dtypes
import numpy as np
from jax import lax
from jax.experimental import pallas as pl
from jax.experimental.pallas import tpu as pltpu
from jax.sharding import PartitionSpec as P

RADIX = 32
FINE = 128
ROOT = 64
LANES = 128
TILE = 256
HIGHEST = lax.Precision.HIGHEST
PRIOR_FLOOR = 0.25
HALF = math.sqrt(0.5)
MESH = pl.DeviceIdType.MESH
SMALL = pl.CostEstimate(flops=1, bytes_accessed=1, transcendentals=0)


def np_split(table):
    high = table.astype(ml_dtypes.bfloat16)
    low = (table - high.astype(np.float64)).astype(ml_dtypes.bfloat16)
    return high, low


@functools.cache
def row_tables():
    length = RADIX * FINE
    coarse = np.arange(RADIX)[:, None, None]
    fine = np.arange(FINE)[None, :, None]
    place = np.arange(FINE)[None, None, :]
    angle = -2.0 * np.pi * ((place * (RADIX * fine + coarse)) % length) / length
    real, imag = np.cos(angle), np.sin(angle)
    forward = np.concatenate(
        [np.concatenate([real, -imag], axis=2), np.concatenate([imag, real], axis=2)], axis=1
    )
    inverse = np.transpose(forward, (0, 2, 1)) / float(length * length)
    return np_split(forward) + np_split(inverse)


@functools.cache
def column_factors(width, length):
    column = np.arange(length)[None, :]

    def wave(rows):
        angle = -2.0 * np.pi * ((rows[:, None] * column) % length) / length
        return np.cos(angle).astype(np.float32), np.sin(angle).astype(np.float32)

    return wave(np.arange(width // ROOT) * ROOT) + wave(np.arange(ROOT))


def split(values):
    high = values.astype(jnp.bfloat16)
    low = (values - high.astype(jnp.float32)).astype(jnp.bfloat16)
    return high, low


def turn(real, imag, num, den, sign):
    num %= den
    if (num * 8) % den == 0:
        eighth = (sign * (num * 8 // den)) % 8
        if eighth == 0:
            return real, imag
        if eighth == 1:
            return (real - imag) * HALF, (real + imag) * HALF
        if eighth == 2:
            return -imag, real
        if eighth == 3:
            return (real + imag) * -HALF, (real - imag) * HALF
        if eighth == 4:
            return -real, -imag
        if eighth == 5:
            return (imag - real) * HALF, (real + imag) * -HALF
        if eighth == 6:
            return imag, -real
        return (real + imag) * HALF, (imag - real) * HALF
    c = math.cos(2.0 * math.pi * num / den)
    s = sign * math.sin(2.0 * math.pi * num / den)
    return real * c - imag * s, real * s + imag * c


def fft(points, sign):
    count = len(points)
    if count == 1:
        return points
    half = count // 2
    even, odd = [], []
    for i in range(half):
        (ar, ai), (br, bi) = points[i], points[i + half]
        even.append((ar + br, ai + bi))
        if 4 * i == count:
            odd.append((ai - bi, br - ar) if sign < 0 else (bi - ai, ar - br))
        else:
            odd.append(turn(ar - br, ai - bi, i, count, sign))
    result = [None] * count
    result[0::2] = fft(even, sign)
    result[1::2] = fft(odd, sign)
    return result


def dot3(table_high, table_low, values):
    high, low = split(values)
    dot = functools.partial(jnp.dot, preferred_element_type=jnp.float32)
    return dot(table_high, high) + dot(table_low, high) + dot(table_high, low)


def row_kernel(slot_of, planes_ref, weight_ref, *refs):
    table_hbm, (out_ref, work_a, work_b, *tables, table_sem) = refs[:4], refs[4:]
    forward_high, forward_low, inverse_high, inverse_low = tables
    used = RADIX // 2
    place = lax.axis_index("facet")
    facets, per_facet = slot_of.shape

    def slot(a):
        choices = [int(slot_of[a // per_facet ^ p, a % per_facet]) for p in range(facets)]
        at = choices[0]
        for p in range(1, facets):
            at = jnp.where(place == p, choices[p], at)
        return at * FINE

    slots = [slot(a) for a in range(used)]
    tile = pl.program_id(0)
    last = pl.num_programs(0) - 1
    copies = [
        pltpu.make_async_copy(source, target, table_sem.at[n])
        for n, (source, target) in enumerate(zip(table_hbm, tables))
    ]

    def rows(base, at):
        return pl.ds(pl.multiple_of(base + at, 8), 8)

    def position(step):
        lanes = pl.ds(pl.multiple_of(step // (FINE // 8) * LANES, LANES), LANES)
        return lax.rem(step, FINE // 8) * 8, lanes

    def forward(step, outer, inner):
        at, col = position(step)
        points = [(planes_ref[0, rows(s, at), col], planes_ref[1, rows(s, at), col]) for s in slots]
        for k, (real, imag) in enumerate(fft(points, -1)):
            outer[2 * k, rows(0, at), col] = real
            outer[2 * k, rows(FINE, at), col] = imag
        points = [turn(*point, a, RADIX, -1) for a, point in enumerate(points)]
        for k, (real, imag) in enumerate(fft(points, -1)):
            outer[2 * k + 1, rows(0, at), col] = real
            outer[2 * k + 1, rows(FINE, at), col] = imag

    def middle(k, outer, inner):
        freqs = dot3(forward_high[k], forward_low[k], inner[k])
        weight = weight_ref[k]
        freqs = freqs * jnp.concatenate([weight, weight], axis=0)
        inner[k] = dot3(inverse_high[k], inverse_low[k], freqs)

    def inverse(step, outer, inner):
        at, col = position(step)

        def side(odd):
            points = [
                (outer[2 * k + odd, rows(0, at), col], outer[2 * k + odd, rows(FINE, at), col])
                for k in range(used)
            ]
            return fft(points, 1)

        even, odd = side(0), side(1)
        for a, s in enumerate(slots):
            real, imag = turn(*odd[a], a, RADIX, 1)
            out_ref[0, rows(s, at), col] = even[a][0] + real
            out_ref[1, rows(s, at), col] = even[a][1] + imag

    def loop(parts, outer, inner, unroll=1):
        def run(step, _):
            for part in parts:
                part(step, outer, inner)
            return 0

        lax.fori_loop(0, RADIX, run, 0, unroll=unroll)

    @pl.when(tile == 0)
    def _():
        for copy in copies:
            copy.start()
        loop([forward], work_a, work_b)
        for copy in copies:
            copy.wait()

    for parity in range(2):
        outer, inner = (work_a, work_b) if parity == 0 else (work_b, work_a)
        mine = lax.rem(tile, 2) == parity

        @pl.when(mine & (tile > 0) & (tile < last))
        def _(outer=outer, inner=inner):
            loop([middle, inverse, forward], outer, inner, unroll=16)

        @pl.when(mine & (tile == last))
        def _(outer=outer, inner=inner):
            loop([inverse], outer, inner)


def row_pass(planes, weight, slot_of):
    _, height, columns = planes.shape
    tables = [jnp.asarray(table) for table in row_tables()]
    count = columns // TILE
    block = (2, height, TILE)
    return pl.pallas_call(
        functools.partial(row_kernel, slot_of),
        grid_spec=pltpu.PrefetchScalarGridSpec(
            num_scalar_prefetch=0,
            grid=(count + 2,),
            in_specs=[
                pl.BlockSpec(block, lambda i: (0, 0, jnp.minimum(i, count - 1))),
                pl.BlockSpec(
                    (RADIX, FINE, TILE), lambda i: (0, 0, jnp.clip(i - 1, 0, count - 1))
                ),
            ]
            + [pl.BlockSpec(memory_space=pl.ANY)] * 4,
            out_specs=pl.BlockSpec(block, lambda i: (0, 0, jnp.maximum(i - 2, 0))),
            scratch_shapes=[pltpu.VMEM((RADIX, 2 * FINE, TILE), jnp.float32)] * 2
            + [pltpu.VMEM((RADIX, 2 * FINE, 2 * FINE), jnp.bfloat16)] * 4
            + [pltpu.SemaphoreType.DMA((4,))],
        ),
        out_shape=jax.ShapeDtypeStruct(planes.shape, jnp.float32),
        compiler_params=pltpu.CompilerParams(vmem_limit_bytes=62 << 20),
        cost_estimate=SMALL,
        name="row_pass",
    )(planes, weight, *tables)


def table_kernel(place_ref, coarse_real, coarse_imag, fine_real, fine_imag, high_ref, low_ref):
    columns = fine_real.shape[1]
    row = pl.ds(pl.program_id(0) % 8, 1)
    coarse_r, coarse_i = coarse_real[row, :], coarse_imag[row, :]
    for at in range(0, columns, LANES):
        real, imag = slice(at, at + LANES), slice(columns + at, columns + at + LANES)
        cr, ci = coarse_r[:, real], coarse_i[:, real]
        fr, fi = fine_real[:, real], fine_imag[:, real]
        high_ref[:, real], low_ref[:, real] = split(cr * fr - ci * fi)
        high_ref[:, imag], low_ref[:, imag] = split(cr * fi + ci * fr)


def width_table(width, columns, length, place):
    factors = [jnp.asarray(factor) for factor in column_factors(width, length)]
    coarse = pl.BlockSpec((8, columns), lambda i, p: (i // 8, p[0]))
    fine = pl.BlockSpec((ROOT, columns), lambda i, p: (0, p[0]))
    out = pl.BlockSpec((ROOT, 2 * columns), lambda i, p: (i, 0))
    return pl.pallas_call(
        table_kernel,
        grid_spec=pltpu.PrefetchScalarGridSpec(
            num_scalar_prefetch=1,
            grid=(width // ROOT,),
            in_specs=[coarse, coarse, fine, fine],
            out_specs=[out, out],
        ),
        out_shape=[jax.ShapeDtypeStruct((width, 2 * columns), jnp.bfloat16)] * 2,
        cost_estimate=SMALL,
        name="width_table",
    )(place.reshape(1), *factors)


def width_kernel(count, *refs):
    blocks = refs[:count]
    table_high, table_low = refs[count : count + 2]
    out_ref, high_ref, low_ref = refs[-3:]

    @pl.when(pl.program_id(0) == 0)
    def _():
        base = 0
        for ref in blocks:
            rows = ref.shape[0]
            high_ref[base : base + rows], low_ref[base : base + rows] = split(ref[...])
            base += rows

    dot = functools.partial(jnp.dot, preferred_element_type=jnp.float32)
    high, low = high_ref[...], low_ref[...]
    weight = table_high[...]
    out_ref[0] = dot(high, weight) + dot(low, weight) + dot(high, table_low[...])


def width_forward(blocks, tables, planes, first, columns, height):
    width = blocks[0].shape[1]
    total = sum(block.shape[0] for block in blocks)
    tiles = columns // TILE
    before = [] if planes is None else [planes]
    table = pl.BlockSpec((width, TILE), lambda n: (0, n))
    return pl.pallas_call(
        functools.partial(width_kernel, len(blocks)),
        grid=(2 * tiles,),
        in_specs=[pl.BlockSpec(block.shape, lambda n: (0, 0)) for block in blocks]
        + [table, table]
        + [pl.BlockSpec(memory_space=pl.ANY)] * len(before),
        out_specs=pl.BlockSpec(
            (1, total, TILE), lambda n: (n // tiles, first // total, n % tiles)
        ),
        out_shape=jax.ShapeDtypeStruct((2, height, columns), jnp.float32),
        scratch_shapes=[pltpu.VMEM((total, width), jnp.bfloat16)] * 2,
        input_output_aliases={len(blocks) + 2: 0} if before else {},
        compiler_params=pltpu.CompilerParams(vmem_limit_bytes=48 << 20),
        cost_estimate=SMALL,
        name="width_forward",
    )(*blocks, *tables, *before)


def back_kernel(count, planes_ref, table_high, table_low, *refs):
    outs = refs[-count - 2 : -2]
    high_ref, low_ref = refs[-2:]
    columns = planes_ref.shape[2]

    @pl.when(pl.program_id(0) == 0)
    def _():
        for part in range(2):
            col = slice(part * columns, (part + 1) * columns)
            high_ref[:, col], low_ref[:, col] = split(planes_ref[part])

    wide = (((1,), (1,)), ((), ()))
    dot = functools.partial(
        lax.dot_general, dimension_numbers=wide, preferred_element_type=jnp.float32
    )
    high, low = high_ref[...], low_ref[...]
    weight = table_high[...]
    image = dot(high, weight) + dot(low, weight) + dot(high, table_low[...])
    base = 0
    for ref in outs:
        rows = ref.shape[0]
        ref[...] = image[base : base + rows]
        base += rows


def width_back(planes, tables, first, sizes, after):
    _, _, columns = planes.shape
    width = tables[0].shape[0]
    total = sum(sizes)
    table = pl.BlockSpec((TILE, 2 * columns), lambda n: (n, 0))
    return pl.pallas_call(
        functools.partial(back_kernel, len(sizes)),
        grid=(width // TILE,),
        in_specs=[
            pl.BlockSpec((2, total, columns), lambda n: (0, first // total, 0)),
            table,
            table,
        ]
        + [pl.BlockSpec(memory_space=pl.ANY)] * len(after),
        out_specs=[pl.BlockSpec((rows, TILE), lambda n: (0, n)) for rows in sizes],
        out_shape=[jax.ShapeDtypeStruct((rows, width), jnp.float32) for rows in sizes],
        scratch_shapes=[pltpu.VMEM((total, 2 * columns), jnp.bfloat16)] * 2,
        compiler_params=pltpu.CompilerParams(vmem_limit_bytes=48 << 20),
        cost_estimate=SMALL,
        name="width_back",
    )(planes, *tables, *after)


def prior_kernel(gram_ref, cube_ref, _, out_ref):
    count, rows, width = cube_ref.shape
    gram = [[gram_ref[c, k] for k in range(count)] for c in range(count)]
    for at in range(0, rows, 8):
        for col in range(0, width, LANES):
            here = slice(at, at + 8), slice(col, col + LANES)
            values = [cube_ref[(k,) + here] for k in range(count)]
            for c in range(count):
                total = gram[c][0] * values[0]
                for k in range(1, count):
                    total = total + gram[c][k] * values[k]
                out_ref[(c,) + here] = total


def prior_term(cube, gram, after):
    count, rows, width = cube.shape
    block = pl.BlockSpec((count, 8, width), lambda i: (0, i, 0))
    return pl.pallas_call(
        prior_kernel,
        grid=(rows // 8,),
        in_specs=[
            pl.BlockSpec(memory_space=pltpu.SMEM),
            block,
            pl.BlockSpec(memory_space=pl.ANY),
        ],
        out_specs=block,
        out_shape=jax.ShapeDtypeStruct(cube.shape, jnp.float32),
        cost_estimate=SMALL,
        name="prior_term",
    )(gram, cube, after)


def moment_kernel(terms, *refs):
    parts = refs[:terms]
    residual_ref, direction_ref = refs[terms : terms + 2]
    applied_ref, moment_ref = refs[-2:]

    @pl.when(pl.program_id(0) == 0)
    def _():
        moment_ref[...] = jnp.zeros_like(moment_ref)

    applied = parts[0][...]
    for ref in parts[1:]:
        applied = applied + ref[...]
    applied_ref[...] = applied
    residual, direction = residual_ref[...], direction_ref[...]
    width = applied.shape[1]

    def fold(product):
        total = product[:8]
        for at in range(8, product.shape[0], 8):
            total = total + product[at : at + 8]
        folded = total[:, :LANES]
        for at in range(LANES, width, LANES):
            folded = folded + total[:, at : at + LANES]
        return folded

    moment_ref[0] += fold(residual * residual)
    moment_ref[1] += fold(direction * applied)
    moment_ref[2] += fold(residual * applied)
    moment_ref[3] += fold(applied * applied)


def moments_of(wide, prior, chunk, residual, direction, applied, first):
    rows, width = chunk.shape
    step = min(64, rows)
    at = first // step
    here = pl.BlockSpec((step, width), lambda i: (at + i, 0))
    chunk_spec = pl.BlockSpec((step, width), lambda i: (i, 0))
    terms = len(wide) + 2
    before = [] if applied is None else [applied]
    return pl.pallas_call(
        functools.partial(moment_kernel, terms),
        grid=(rows // step,),
        in_specs=[here] * len(wide)
        + [here, chunk_spec, here, here]
        + [pl.BlockSpec(memory_space=pl.ANY)] * len(before),
        out_specs=[here, pl.BlockSpec((4, 8, LANES), lambda i: (0, 0, 0))],
        out_shape=[
            jax.ShapeDtypeStruct(residual.shape, jnp.float32),
            jax.ShapeDtypeStruct((4, 8, LANES), jnp.float32),
        ],
        input_output_aliases={terms + 2: 0} if before else {},
        cost_estimate=SMALL,
        name="moments",
    )(*wide, prior, chunk, residual, direction, *before)


def group_sum(axes, sizes, total, out_ref, mine, landed, send_sem, recv_sem):
    slot = 0
    for axis in range(2):
        size = sizes[axis]
        me = lax.axis_index(axes[axis])
        mine[axis] = total
        copies = [
            pltpu.make_async_remote_copy(
                src_ref=mine.at[axis],
                dst_ref=landed.at[slot + hop - 1],
                send_sem=send_sem.at[slot + hop - 1],
                recv_sem=recv_sem.at[slot + hop - 1],
                device_id={axes[axis]: lax.rem(me + hop, size)},
                device_id_type=MESH,
            )
            for hop in range(1, size)
        ]
        for copy in copies:
            copy.start()
        for copy in copies:
            copy.wait()
        total = jnp.zeros_like(total)
        for source in range(size):
            hop = lax.rem(me - source + size, size)
            arrived = landed[slot + jnp.maximum(hop, 1) - 1]
            total = total + jnp.where(hop == 0, mine[axis], arrived)
        slot += size - 1
    sums = jnp.sum(jnp.sum(total, axis=2, keepdims=True), axis=1, keepdims=True)
    out_ref[...] = jnp.broadcast_to(sums, total.shape)


def reduce_kernel(axes, sizes, parts, *refs):
    inputs = refs[:parts]
    out_ref, mine, landed, send_sem, recv_sem = refs[parts:]
    barrier = pltpu.get_barrier_semaphore()
    for axis in range(2):
        me = lax.axis_index(axes[axis])
        for hop in range(1, sizes[axis]):
            peer = lax.rem(me + hop, sizes[axis])
            pl.semaphore_signal(barrier, inc=1, device_id={axes[axis]: peer}, device_id_type=MESH)
    total = inputs[0][...]
    for ref in inputs[1:]:
        total = total + ref[...]
    pl.semaphore_wait(barrier, sizes[0] + sizes[1] - 2)
    group_sum(axes, sizes, total, out_ref, mine, landed, send_sem, recv_sem)


def reduce_moments(moments, axes, sizes):
    shape = moments[0].shape
    slots = sizes[0] + sizes[1] - 2
    return pl.pallas_call(
        functools.partial(reduce_kernel, axes, sizes, len(moments)),
        out_shape=jax.ShapeDtypeStruct(shape, jnp.float32),
        in_specs=[pl.BlockSpec(memory_space=pltpu.VMEM)] * len(moments),
        out_specs=pl.BlockSpec(memory_space=pltpu.VMEM),
        scratch_shapes=[
            pltpu.VMEM((2,) + shape, jnp.float32),
            pltpu.VMEM((slots,) + shape, jnp.float32),
            pltpu.SemaphoreType.DMA((slots,)),
            pltpu.SemaphoreType.DMA((slots,)),
        ],
        compiler_params=pltpu.CompilerParams(collective_id=0, has_side_effects=True),
        cost_estimate=SMALL,
        name="reduce_moments",
    )(*moments)


def far_pieces(slabs):
    pieces = [(slab, 0, FINE) for slab in range(slabs - 1)]
    return pieces + [(slabs - 1, first, FINE // 2) for first in (0, FINE // 2)]


def tile_pieces(slabs, tiles):
    pieces = []
    for slab in range(slabs):
        if slab == 0:
            sizes = [tiles // 4, tiles // 4, tiles - tiles // 2]
        elif slab == slabs - 1:
            sizes = [tiles - tiles // 4, tiles // 4]
        else:
            sizes = [tiles]
        first = 0
        for size in sizes:
            pieces.append((slab, first, size))
            first += size
    return pieces


def gather_kernel(axes, sizes, basis_ref, slot_ref, own_hbm, spectrum_hbm, coarse_real_hbm,
                  coarse_imag_hbm, fine_real_hbm, fine_imag_hbm, planes_hbm, prior_hbm, high_hbm,
                  low_hbm, weight_hbm,
                  table_high, table_low, coarse, fine, mine, beside, cross, passed, high_ref,
                  low_ref, result, cube, strip, sorted_strip,
                  gram, strip_sem, sorted_sem, own_sem, factor_sem, table_sem, result_sem,
                  prior_sem, send_sem, recv_sem, group_send, group_recv):
    height, width = own_hbm.shape
    columns = fine.shape[2]
    unit = high_ref.shape[0]
    chunks = height // FINE
    halves = height // unit
    slots = sizes[0]
    block = height // slots
    place = lax.axis_index("facet")
    me = lax.axis_index("chan")
    sibling = place + 1 - 2 * lax.rem(place, 2)
    partner = lax.rem(place + 2, 4)

    def half_rows(h):
        return pl.ds(h * unit, unit)

    def block_rows(at):
        return pl.ds(pl.multiple_of(at * block, block), block)

    def remote(source, target, slot, device):
        return pltpu.make_async_remote_copy(
            src_ref=source,
            dst_ref=target,
            send_sem=send_sem.at[slot],
            recv_sem=recv_sem.at[slot],
            device_id={"facet": device},
            device_id_type=MESH,
        )

    pieces = far_pieces(chunks)
    count = len(pieces)
    crossing = [
        remote(
            own_hbm.at[pl.ds(c * FINE + first, size)],
            cross.at[c, pl.ds(first, size)],
            n,
            partner,
        )
        for n, (c, first, size) in enumerate(pieces)
    ]
    passing = [
        remote(
            cross.at[c, pl.ds(first, size)],
            passed.at[c, pl.ds(first, size)],
            count + n,
            sibling,
        )
        for n, (c, first, size) in enumerate(pieces)
    ]
    nearby = [
        remote(own_hbm.at[half_rows(h)], beside.at[half_rows(h)], 2 * count + h, sibling)
        for h in range(halves)
    ]
    strips = columns // LANES

    def strip_lanes(n):
        return pl.ds(n * LANES, LANES)

    strip_loads = [
        pltpu.make_async_copy(
            spectrum_hbm.at[:, strip_lanes(n)], strip.at[n % 2], strip_sem.at[n % 2]
        )
        for n in range(strips)
    ]
    strip_outs = [
        pltpu.make_async_copy(
            sorted_strip.at[n % 2], weight_hbm.at[:, :, strip_lanes(n)], sorted_sem.at[n % 2]
        )
        for n in range(strips)
    ]
    regroup = []
    for hop in range(1, slots):
        peer = lax.rem(me + hop, slots)
        regroup.append(
            pltpu.make_async_remote_copy(
                src_ref=own_hbm.at[block_rows(peer)],
                dst_ref=cube.at[me],
                send_sem=group_send.at[hop - 1],
                recv_sem=group_recv.at[hop - 1],
                device_id={"chan": peer},
                device_id_type=MESH,
            )
        )
    kept = pltpu.make_async_copy(own_hbm.at[block_rows(me)], cube.at[me], prior_sem.at[0])
    own_loads = [
        pltpu.make_async_copy(own_hbm.at[half_rows(h)], mine.at[half_rows(h)], own_sem.at[h])
        for h in range(halves)
    ]
    col = pl.ds(pl.multiple_of(place * columns, columns), columns)
    factors = [
        pltpu.make_async_copy(source.at[:, col], target, factor_sem.at[n])
        for n, (source, target) in enumerate(
            (
                (coarse_real_hbm, coarse.at[0]),
                (coarse_imag_hbm, coarse.at[1]),
                (fine_real_hbm, fine.at[0]),
                (fine_imag_hbm, fine.at[1]),
            )
        )
    ]

    barrier = pltpu.get_barrier_semaphore()
    for axis in range(2):
        at = lax.axis_index(axes[axis])
        for hop in range(1, sizes[axis]):
            peer = lax.rem(at + hop, sizes[axis])
            pl.semaphore_signal(barrier, inc=1, device_id={axes[axis]: peer}, device_id_type=MESH)
    for copy in factors + own_loads + [kept]:
        copy.start()
    pl.semaphore_wait(barrier, sizes[0] + sizes[1] - 2)
    for copy in crossing + nearby + regroup:
        copy.start()

    for copy in factors:
        copy.wait()

    def table_rows(j, _):
        rows = pl.ds(pl.multiple_of(j * ROOT, ROOT), ROOT)
        coarse_r, coarse_i = coarse[0, pl.ds(j, 1), :], coarse[1, pl.ds(j, 1), :]
        for at in range(0, columns, LANES):
            real, imag = slice(at, at + LANES), slice(columns + at, columns + at + LANES)
            cr, ci = coarse_r[:, real], coarse_i[:, real]
            fr, fi = fine[0, :, real], fine[1, :, real]
            table_high[rows, real], table_low[rows, real] = split(cr * fr - ci * fi)
            table_high[rows, imag], table_low[rows, imag] = split(cr * fi + ci * fr)
        return 0

    lax.fori_loop(0, width // ROOT, table_rows, 0)
    table_outs = [
        pltpu.make_async_copy(table_high, high_hbm, table_sem.at[0]),
        pltpu.make_async_copy(table_low, low_hbm, table_sem.at[1]),
    ]
    for copy in table_outs:
        copy.start()

    loadings = [
        [basis_ref[slot_ref[c], q] for q in range(basis_ref.shape[1])] for c in range(slots)
    ]
    for c in range(slots):
        for k in range(c + 1):
            total = loadings[c][0] * loadings[k][0]
            for q in range(1, basis_ref.shape[1]):
                total = total + loadings[c][q] * loadings[k][q]
            if c == k:
                total = total + PRIOR_FLOOR
            gram[c, k] = total
            gram[k, c] = total

    def sort_strip(n):
        strip_loads[n].wait()
        if n >= 2:
            strip_outs[n - 2].wait()

        def order(k, _):
            sorted_strip[n % 2, k] = strip[n % 2, pl.ds(k, FINE, stride=RADIX), :]
            return 0

        lax.fori_loop(0, RADIX, order, 0)
        strip_outs[n].start()
        if n + 2 < strips:
            strip_loads[n + 2].start()

    todo = list(range(strips))

    def sort_strips(number):
        for _ in range(min(number, len(todo))):
            sort_strip(todo.pop(0))

    for copy in strip_loads[:2]:
        copy.start()
    outs = []

    def transform(inputs, targets):
        u = len(outs)
        base = 0
        for ref, first, rows in inputs:
            here = slice(base, base + rows)
            high_ref[here], low_ref[here] = split(ref[first : first + rows])
            base += rows
        if u >= 2:
            for out in outs[u - 2]:
                out.wait()
        dot = functools.partial(jnp.dot, preferred_element_type=jnp.float32)
        for part in range(2):

            def tile(t, _, part=part):
                at = pl.ds(pl.multiple_of(t * TILE, TILE), TILE)
                source = pl.ds(pl.multiple_of(part * columns + t * TILE, TILE), TILE)
                weight = table_high[:, source]
                high = high_ref[:base]
                result[u % 2, part, :base, at] = (
                    dot(high, weight)
                    + dot(low_ref[:base], weight)
                    + dot(high, table_low[:, source])
                )
                return 0

            lax.fori_loop(0, columns // TILE, tile, 0)
        copies = []
        at = 0
        for n, (first, rows) in enumerate(targets):
            copies.append(
                pltpu.make_async_copy(
                    result.at[u % 2, :, pl.ds(at, rows)],
                    planes_hbm.at[:, pl.ds(first, rows)],
                    result_sem.at[u % 2, n],
                )
            )
            at += rows
        for copy in copies:
            copy.start()
        outs.append(copies)

    def pass_on(n):
        crossing[n].wait_recv()
        passing[n].start()

    def far(n):
        c, first, size = pieces[n]
        passing[n].wait_recv()
        base = 2 * height + c * unit + first
        transform(
            [(cross.at[c], first, size), (passed.at[c], first, size)],
            [(base, size), (base + FINE, size)],
        )

    for h in range(halves):
        own_loads[h].wait()
        transform([(mine, h * unit, unit)], [(h * unit, unit)])
    pass_on(0)
    for h in range(halves):
        nearby[h].wait_recv()
        transform([(beside, h * unit, unit)], [(height + h * unit, unit)])
    share = -(-strips // max(count - 3, 1))
    for n in range(1, count):
        if n < count - 2:
            sort_strips(share)
            pass_on(n)
            far(n - 1)
        else:
            sort_strips(strips)
            far(n - 1)
            pass_on(n)

    kept.wait()
    for copy in regroup:
        copy.wait_recv()
    gram_values = [[gram[c, k] for k in range(slots)] for c in range(slots)]

    def mix(step, _):
        rows = pl.ds(pl.multiple_of(step // (width // LANES) * 8, 8), 8)
        lanes = pl.ds(pl.multiple_of(step % (width // LANES) * LANES, LANES), LANES)
        values = [cube[k, rows, lanes] for k in range(slots)]
        for c in range(slots):
            total = gram_values[c][0] * values[0]
            for k in range(1, slots):
                total = total + gram_values[c][k] * values[k]
            cube[c, rows, lanes] = total
        return 0

    lax.fori_loop(0, block // 8 * (width // LANES), mix, 0, unroll=2)
    prior_out = pltpu.make_async_copy(cube, prior_hbm, prior_sem.at[1])
    prior_out.start()
    far(count - 1)

    for copy in crossing + nearby + passing + regroup:
        copy.wait_send()
    for copy in table_outs + outs[-2] + outs[-1] + strip_outs[-2:] + [prior_out]:
        copy.wait()


def gather(basis, slot_channel, own, spectrum, sizes):
    height, width = own.shape
    length, columns = spectrum.shape
    factors = [jnp.asarray(factor) for factor in column_factors(width, length)]
    unit = 2 * FINE
    chunks = height // FINE
    halves = height // unit
    flights = 2 * len(far_pieces(chunks)) + halves
    block = height // sizes[0]
    anywhere = pl.BlockSpec(memory_space=pl.ANY)
    scalars = pl.BlockSpec(memory_space=pltpu.SMEM)
    table = jax.ShapeDtypeStruct((width, 2 * columns), jnp.bfloat16)
    dma = pltpu.SemaphoreType.DMA
    return pl.pallas_call(
        functools.partial(gather_kernel, ("chan", "facet"), sizes),
        in_specs=[scalars, scalars] + [anywhere] * 6,
        out_specs=[anywhere] * 5,
        out_shape=[
            jax.ShapeDtypeStruct((2, sizes[1] * height, columns), jnp.float32),
            jax.ShapeDtypeStruct((sizes[0], block, width), jnp.float32),
            table,
            table,
            jax.ShapeDtypeStruct((RADIX, FINE, columns), jnp.float32),
        ],
        scratch_shapes=[
            pltpu.VMEM(table.shape, jnp.bfloat16),
            pltpu.VMEM(table.shape, jnp.bfloat16),
            pltpu.VMEM((2, width // ROOT, columns), jnp.float32),
            pltpu.VMEM((2, ROOT, columns), jnp.float32),
            pltpu.VMEM((height, width), jnp.float32),
            pltpu.VMEM((height, width), jnp.float32),
            pltpu.VMEM((chunks, FINE, width), jnp.float32),
            pltpu.VMEM((chunks, FINE, width), jnp.float32),
            pltpu.VMEM((unit, width), jnp.bfloat16),
            pltpu.VMEM((unit, width), jnp.bfloat16),
            pltpu.VMEM((2, 2, unit, columns), jnp.float32),
            pltpu.VMEM((sizes[0], block, width), jnp.float32),
            pltpu.VMEM((2, length, LANES), jnp.float32),
            pltpu.VMEM((2, RADIX, FINE, LANES), jnp.float32),
            pltpu.SMEM((sizes[0], sizes[0]), jnp.float32),
            dma((2,)),
            dma((2,)),
            dma((halves,)),
            dma((4,)),
            dma((2,)),
            dma((2, 2)),
            dma((2,)),
            dma((flights,)),
            dma((flights,)),
            dma((sizes[0] - 1,)),
            dma((sizes[0] - 1,)),
        ],
        compiler_params=pltpu.CompilerParams(
            collective_id=2, has_side_effects=True, vmem_limit_bytes=60 << 20
        ),
        cost_estimate=SMALL,
        name="gather",
    )(basis, slot_channel, own, spectrum, *factors)


def scatter_kernel(axes, sizes, rows_hbm, high_hbm, low_hbm, prior_hbm, residual_hbm,
                   direction_hbm, applied_hbm, sums_ref, table_high, table_low, held, high_ref,
                   low_ref, part, landed, beside, own, near, cross, prior, stream, moment,
                   mine, got, table_sem, held_sem, stream_sem, out_sem, kept_sem, send_sem,
                   recv_sem, group_send, group_recv, regroup_send, regroup_recv):
    width = table_high.shape[0]
    columns = held.shape[3]
    unit = held.shape[2]
    height = own.shape[0]
    chunks = height // FINE
    tiles = width // TILE
    place = lax.axis_index("facet")
    sibling = place + 1 - 2 * lax.rem(place, 2)
    partner = lax.rem(place + 2, 4)

    def peers(axis):
        me = lax.axis_index(axes[axis])
        return [lax.rem(me + hop, sizes[axis]) for hop in range(1, sizes[axis])]

    def table_copies(t):
        at = pl.ds(pl.multiple_of(t * TILE, TILE), TILE)
        return [
            pltpu.make_async_copy(source.at[at], target.at[at], table_sem.at[n, t])
            for n, (source, target) in enumerate(((high_hbm, table_high), (low_hbm, table_low)))
        ]

    pieces = tile_pieces(chunks, tiles)
    count = len(pieces)
    halves = height // unit
    units = []
    units += [[(2 * height + unit * c, unit)] for c in range(chunks)]
    units += [[(height + unit * h, unit)] for h in range(halves)]
    units += [[(unit * h, unit)] for h in range(halves)]
    loads = []
    for u, blocks in enumerate(units):
        copies, at = [], 0
        for n, (first, size) in enumerate(blocks):
            copies.append(
                pltpu.make_async_copy(
                    rows_hbm.at[:, pl.ds(first, size)],
                    held.at[u % 2, :, pl.ds(at, size)],
                    held_sem.at[u % 2, n],
                )
            )
            at += size
        loads.append(copies)

    def load(u):
        for copy in loads[u]:
            copy.start()

    barrier = pltpu.get_barrier_semaphore()
    load(0)
    for t in range(tiles):
        for copy in table_copies(t):
            copy.start()
    for axis in range(2):
        for peer in peers(axis):
            pl.semaphore_signal(barrier, inc=1, device_id={axes[axis]: peer}, device_id_type=MESH)

    def prepare(u):
        for copy in loads[u]:
            copy.wait()
        if u + 1 < len(units):
            load(u + 1)
        for part_at in range(2):
            col = slice(part_at * columns, (part_at + 1) * columns)
            high_ref[:, col], low_ref[:, col] = split(held[u % 2, part_at])

    def image(target, first, number, loading=False):
        wide = (((1,), (1,)), ((), ()))
        dot = functools.partial(
            lax.dot_general, dimension_numbers=wide, preferred_element_type=jnp.float32
        )

        def tile(t, _):
            if loading:
                for copy in table_copies(t):
                    copy.wait()
            at = pl.ds(pl.multiple_of(t * TILE, TILE), TILE)
            weight = table_high[at, :]
            high = high_ref[...]
            target[:, at] = (
                dot(high, weight) + dot(low_ref[...], weight) + dot(high, table_low[at, :])
            )
            return 0

        lax.fori_loop(first, first + number, tile, 0)

    def remote(source, target, slot, device):
        return pltpu.make_async_remote_copy(
            src_ref=source,
            dst_ref=target,
            send_sem=send_sem.at[slot],
            recv_sem=recv_sem.at[slot],
            device_id={"facet": device},
            device_id_type=MESH,
        )

    def slab_rows(c):
        return pl.ds(c * FINE, FINE)

    upper, lower = pl.ds(0, FINE), pl.ds(FINE, FINE)
    paired, crossing = [], []
    for n, (c, first, number) in enumerate(pieces):
        col = pl.ds(first * TILE, number * TILE)
        paired.append(remote(part.at[c, lower, col], landed.at[c, :, col], n, sibling))
        crossing.append(
            remote(part.at[c, upper, col], cross.at[slab_rows(c), col], count + n, partner)
        )
    nearby = [
        remote(beside.at[h], near.at[pl.ds(h * unit, unit)], 2 * count + h, sibling)
        for h in range(halves)
    ]

    def cross_over(n):
        c, first, number = pieces[n]
        col = pl.ds(first * TILE, number * TILE)
        paired[n].wait_recv()

        def add(i, _):
            at = pl.ds(pl.multiple_of(i * 8, 8), 8)
            part[c, at, col] += landed[c, at, col]
            return 0

        lax.fori_loop(0, FINE // 8, add, 0)
        crossing[n].start()

    me = lax.axis_index(axes[0])
    block = height // sizes[0]
    mine_rows = pl.ds(pl.multiple_of(me * block, block), block)
    kept = pltpu.make_async_copy(prior_hbm.at[me], prior.at[mine_rows], kept_sem)
    kept.start()
    regroup = []
    for hop, peer in enumerate(peers(0)):
        regroup.append(
            pltpu.make_async_remote_copy(
                src_ref=prior_hbm.at[peer],
                dst_ref=prior.at[mine_rows],
                send_sem=regroup_send.at[hop],
                recv_sem=regroup_recv.at[hop],
                device_id={axes[0]: peer},
                device_id_type=MESH,
            )
        )
    pl.semaphore_wait(barrier, sizes[0] + sizes[1] - 2)
    for copy in regroup:
        copy.start()

    for n, (c, first, number) in enumerate(pieces):
        if first == 0:
            prepare(c)
        image(part.at[c], first, number, loading=c == 0)
        paired[n].start()
        if n:
            cross_over(n - 1)
    for h in range(halves):
        prepare(chunks + h)
        image(beside.at[h], 0, tiles)
        if h == 0:
            cross_over(count - 1)
        nearby[h].start()
    streams = [
        [
            pltpu.make_async_copy(source.at[slab_rows(c)], stream.at[k], stream_sem.at[k])
            for k, source in enumerate((residual_hbm, direction_hbm))
        ]
        for c in range(chunks)
    ]
    for copy in streams[0]:
        copy.start()
    for h in range(halves):
        prepare(chunks + halves + h)
        image(own.at[pl.ds(h * unit, unit)], 0, tiles)

    moment[...] = jnp.zeros_like(moment)
    for copy in nearby + regroup:
        copy.wait_recv()
    kept.wait()
    outs = []

    def fold(total):
        folded = total[:, :LANES]
        for at in range(LANES, total.shape[1], LANES):
            folded = folded + total[:, at : at + LANES]
        return folded

    for n, (c, first, number) in enumerate(pieces):
        if first == 0:
            for copy in streams[c]:
                copy.wait()
        crossing[n].wait_recv()

        def gather_rows(i, _, c=c, col=pl.ds(first * TILE, number * TILE)):
            at = pl.ds(pl.multiple_of(i * 8, 8), 8)
            here = pl.ds(pl.multiple_of(c * FINE + i * 8, 8), 8)
            applied = own[here, col] + near[here, col] + cross[here, col] + prior[here, col]
            own[here, col] = applied
            residual, direction = stream[0, at, col], stream[1, at, col]
            moment[0] += fold(residual * residual)
            moment[1] += fold(direction * applied)
            moment[2] += fold(residual * applied)
            moment[3] += fold(applied * applied)
            return 0

        lax.fori_loop(0, FINE // 8, gather_rows, 0)
        if first + number < tiles:
            continue
        if c + 1 < chunks:
            for copy in streams[c + 1]:
                copy.start()
        out = pltpu.make_async_copy(
            own.at[slab_rows(c)], applied_hbm.at[slab_rows(c)], out_sem.at[c]
        )
        out.start()
        outs.append(out)

    group_sum(axes, sizes, moment[...], sums_ref, mine, got, group_send, group_recv)
    for copy in paired + crossing + nearby + regroup:
        copy.wait_send()
    for out in outs:
        out.wait()


def scatter(rows, tables, prior, residual, direction, sizes):
    height, width = direction.shape
    columns = rows.shape[2]
    unit = 2 * FINE
    chunks = height // FINE
    hops = sizes[0] + sizes[1] - 2
    count = len(tile_pieces(chunks, width // TILE))
    flights = 2 * count + height // unit
    anywhere = pl.BlockSpec(memory_space=pl.ANY)
    shape = (4, 8, LANES)
    whole = pltpu.VMEM((height, width), jnp.float32)
    dma = pltpu.SemaphoreType.DMA
    return pl.pallas_call(
        functools.partial(scatter_kernel, ("chan", "facet"), sizes),
        in_specs=[anywhere] * 6,
        out_specs=[anywhere, pl.BlockSpec(memory_space=pltpu.VMEM)],
        out_shape=[
            jax.ShapeDtypeStruct((height, width), jnp.float32),
            jax.ShapeDtypeStruct(shape, jnp.float32),
        ],
        scratch_shapes=[
            pltpu.VMEM((width, 2 * columns), jnp.bfloat16),
            pltpu.VMEM((width, 2 * columns), jnp.bfloat16),
            pltpu.VMEM((2, 2, unit, columns), jnp.float32),
            pltpu.VMEM((unit, 2 * columns), jnp.bfloat16),
            pltpu.VMEM((unit, 2 * columns), jnp.bfloat16),
            pltpu.VMEM((chunks, unit, width), jnp.float32),
            pltpu.VMEM((chunks, FINE, width), jnp.float32),
            pltpu.VMEM((height // unit, unit, width), jnp.float32),
            whole,
            whole,
            whole,
            whole,
            pltpu.VMEM((2, FINE, width), jnp.float32),
            pltpu.VMEM(shape, jnp.float32),
            pltpu.VMEM((2,) + shape, jnp.float32),
            pltpu.VMEM((hops,) + shape, jnp.float32),
            dma((2, width // TILE)),
            dma((2, 1)),
            dma((2,)),
            dma((chunks,)),
            dma,
            dma((flights,)),
            dma((flights,)),
            dma((hops,)),
            dma((hops,)),
            dma((sizes[0] - 1,)),
            dma((sizes[0] - 1,)),
        ],
        compiler_params=pltpu.CompilerParams(
            collective_id=1, has_side_effects=True, vmem_limit_bytes=60 << 20
        ),
        cost_estimate=SMALL,
        name="scatter",
    )(rows, *tables, prior, residual, direction)


def update_kernel(
    sum_ref, solution_ref, residual_ref, direction_ref, applied_ref, x_ref, r_ref, d_ref
):
    def scalar(at):
        return sum_ref[at, 0:1, 0:1]

    norm_now, curvature, cross, square = [scalar(at) for at in range(4)]
    step_size = norm_now / curvature
    norm_next = norm_now - 2.0 * step_size * cross + step_size * step_size * square
    ratio = norm_next / norm_now
    direction = direction_ref[...]
    x_ref[...] = solution_ref[...] + step_size * direction
    residual = residual_ref[...] - step_size * applied_ref[...]
    r_ref[...] = residual
    d_ref[...] = residual + ratio * direction


def update(sums, solution, residual, direction, applied):
    height, width = applied.shape
    step = min(256, height)
    block = pl.BlockSpec((step, width), lambda i: (i, 0))
    return pl.pallas_call(
        update_kernel,
        grid=(height // step,),
        in_specs=[pl.BlockSpec(sums.shape, lambda i: (0, 0, 0))] + [block] * 4,
        out_specs=[block] * 3,
        out_shape=[jax.ShapeDtypeStruct((height, width), jnp.float32)] * 3,
        compiler_params=pltpu.CompilerParams(vmem_limit_bytes=48 << 20),
        cost_estimate=SMALL,
        name="update",
    )(sums, solution, residual, direction, applied)


def swap_pairs(array, count, bit):
    pairs = [(place, place ^ bit) for place in range(count)]
    return lax.ppermute(array, "facet", pairs)


def body(solution, residual, direction, spectra, basis, slot_channel):
    channel_count = basis.shape[0]
    length = RADIX * FINE
    facets = lax.axis_size("facet")
    place = lax.axis_index("facet")
    height, width = direction.shape[1:]
    columns = spectra.shape[2]
    own = direction[0]
    top = facets // 2
    per_facet = height // FINE
    barrier = lax.optimization_barrier

    groups = []
    if per_facet > 1:
        groups += [[(key, s) for s in range(per_facet)] for key in range(top)]
    else:
        groups.append([(key, 0) for key in range(top)])
    groups += [[(key, s) for key in range(top, facets)] for s in range(per_facet)]
    starts = np.cumsum([0] + [len(entries) * FINE for entries in groups])
    slot_of = np.zeros((facets, per_facet), np.int32)
    for at, (key, s) in enumerate(entry for entries in groups for entry in entries):
        slot_of[key, s] = at

    sizes = (lax.axis_size("chan"), facets)
    if facets == 4 and per_facet % 2 == 0 and height % (8 * sizes[0]) == 0:
        planes, local, *tables, weight = gather(basis, slot_channel, own, spectra[0], sizes)
        rows = row_pass(planes, weight, slot_of)
        applied, sums = scatter(rows, tables, local, residual[0], own, sizes)
        results = update(sums, solution[0], residual[0], own, applied)
        return tuple(result[None] for result in results)

    chunks = [own[at * FINE : (at + 1) * FINE] for at in range(per_facet)]
    crossed = [swap_pairs(chunk, facets, top) for chunk in chunks]

    def spread(block, key):
        blocks = {key: block}
        bit = top // 2
        while bit:
            blocks.update({k ^ bit: swap_pairs(blocks[k], facets, bit) for k in list(blocks)})
            bit //= 2
        return blocks

    near = spread(own, 0)

    cube = own.reshape(channel_count, height // channel_count, width)
    regrouped = lax.all_to_all(cube, "chan", split_axis=0, concat_axis=0, tiled=True)
    one_hot = (
        slot_channel[:, None] == jnp.arange(channel_count, dtype=jnp.int32)[None, :]
    ).astype(jnp.float32)
    loadings = jnp.dot(one_hot, basis, precision=HIGHEST)
    gram = jnp.einsum("cq,dq->cd", loadings, loadings, precision=HIGHEST)
    gram = gram + PRIOR_FLOOR * jnp.eye(channel_count, dtype=jnp.float32)

    tables = width_table(width, columns, length, place)
    planes = None
    far = {}
    for step, entries in enumerate(groups):
        if entries[0][0] >= top:
            blocks = [far[s][key] for key, s in entries]
        elif per_facet > 1:
            blocks = [near[entries[0][0]]]
        else:
            blocks = [near[key] for key, _ in entries]
        planes = width_forward(
            blocks, tables, planes, int(starts[step]), columns, facets * height
        )
        if step < per_facet:
            block, planes = barrier((crossed[step], planes))
            far[step] = spread(block, top)
        if step == len(groups) - 2:
            local = prior_term(regrouped, gram, planes)
            local, planes = barrier((local, planes))
            prior = lax.all_to_all(local, "chan", split_axis=0, concat_axis=0, tiled=True)
            prior = prior.reshape(height, width)

    weight = spectra[0].reshape(FINE, RADIX, columns).transpose(1, 0, 2)
    rows = row_pass(planes, weight, slot_of)

    arrived = {}
    near_sums = {}
    held = [rows]
    previous = None
    sequence = [at for at in range(len(groups)) if groups[at][0][0] >= top]
    sequence += [at for at in range(len(groups)) if groups[at][0][0] < top][::-1]

    def send(entries, parts):
        sums = {key: part for (key, _), part in zip(entries, parts)}
        bit = 1
        while bit < top:
            sums = {
                key: sums[key] + swap_pairs(sums[key | bit], facets, bit)
                for key in sorted(sums, reverse=True)
                if not key & bit
            }
            bit *= 2
        arrived[entries[0][1]] = swap_pairs(sums[top], facets, top)
        return sums[top]

    for turn_at, at in enumerate(sequence):
        entries = groups[at]
        far_rows = entries[0][0] >= top
        counts = [FINE] * len(entries) if far_rows or per_facet == 1 else [height]
        parts = width_back(rows, tables, int(starts[at]), counts, held)
        held = [parts[0]]
        if previous is not None:
            held.append(send(*previous))
            previous = None
        if turn_at >= 3 and turn_at - 3 < per_facet:
            held.append(arrived[groups[sequence[turn_at - 3]][0][1]])
        if far_rows:
            previous = (entries, parts)
        else:
            near_sums.update({key: part for (key, _), part in zip(entries, parts)})
    bit = 1
    while 2 * bit < top:
        near_sums = {
            key: near_sums[key] + swap_pairs(near_sums[key | bit], facets, bit)
            for key in sorted(near_sums, reverse=True)
            if not key & bit
        }
        bit *= 2
    wide = [near_sums[0], swap_pairs(near_sums[bit], facets, bit)]

    applied = None
    moments = []
    for s in range(per_facet):
        first = s * FINE
        applied, moment = moments_of(
            wide, prior, arrived[s], residual[0], own, applied, first
        )
        moments.append(moment)
    sums = reduce_moments(moments, ("chan", "facet"), sizes)
    results = update(sums, solution[0], residual[0], own, applied)
    return tuple(result[None] for result in results)


def solution(mesh):
    return jax.shard_map(
        body,
        mesh=mesh,
        in_specs=(
            P("chan", "facet", None),
            P("chan", "facet", None),
            P("chan", "facet", None),
            P("chan", None, "facet"),
            P(),
            P(),
        ),
        out_specs=(P("chan", "facet", None), P("chan", "facet", None), P("chan", "facet", None)),
        check_vma=False,
    )
```
